32 devices in a mesh: dp: 16 (over z, y, x), tensor: 2 (over core).
Axes of the slice: x: 2, y: 2, z: 4, core: 2. Of those that a mesh axis runs over, the one named last changes fastest.
Arguments:
- tokens: bfloat16 [16384, 768], P('dp'), may hold values from -6 to 6
- w_qkv: bfloat16 [3, 768, 768], P(None, None, 'tensor'), may hold values from -0.21875 to 0.21875
- bias_qv: float32 [2, 768], P(None, 'tensor'), may hold values from -3 to 3
- w_out: bfloat16 [768, 768], P('tensor'), may hold values from -0.875 to 0.875
- bias_out: float32 [768], replicated, may hold values from -2 to 2
- gain_attn: float32 [768], replicated, may hold values from 0.5 to 1.5
- shift_attn: float32 [768], replicated, may hold values from -2 to 2
- w_up: bfloat16 [768, 3072], P(None, 'tensor'), may hold values from -0.21875 to 0.21875
- bias_up: float32 [3072], P('tensor'), may hold values from -3 to 3
- w_down: bfloat16 [3072, 768], P('tensor'), may hold values from -0.21875 to 0.21875
- bias_down: float32 [768], replicated, may hold values from -2 to 2
- gain_ffn: float32 [768], replicated, may hold values from 0.5 to 1.5
- shift_ffn: float32 [768], replicated, may hold values from -2 to 2
- out_grad: bfloat16 [16384, 768], P('dp'), may hold values from -6 to 6
- bucket_len: int32 [16], P('dp'), may hold values from 128 to 512, as said below
- seq_lengths: int32 [16, 8], P('dp'), may hold values from 32 to 512, as said below
- keep_mask: int32 [16, 8], P('dp'), may hold values 0 or 1
Outputs:
- mixed: bfloat16 [16384, 768], P('dp')
- input_grad: float32 [16384, 768], P('dp')
- grad_w_qkv: float32 [3, 768, 768], P(None, None, 'tensor')
- grad_bias_qv: float32 [2, 768], P(None, 'tensor')
- grad_w_out: float32 [768, 768], P('tensor')
- grad_bias_out: float32 [768], replicated
- grad_gain_attn: float32 [768], replicated
- grad_shift_attn: float32 [768], replicated
- grad_w_up: float32 [768, 3072], P(None, 'tensor')
- grad_bias_up: float32 [3072], P('tensor')
- grad_w_down: float32 [3072, 768], P('tensor')
- grad_bias_down: float32 [768], replicated
- grad_gain_ffn: float32 [768], replicated
- grad_shift_ffn: float32 [768], replicated
The draws below stay inside these ranges and needn't reach their ends.
Inputs may be any that keep to these rules, and one draw needn't show every extreme that they name: `bucket_len`: group 0 has 512, group 1 has 128, every other group one of the two. seq_lengths[g, j] lies between bucket_len[g] // 4 and bucket_len[g]; slot 0 of every group equals bucket_len[g]; slots j >= 1024 // bucket_len[g] are not used. `keep_mask`: slots j >= 1024 // bucket_len[g] are not used.
All inputs are finite; a program needn't handle non-finite values. No bound on the sum of `keep_mask` on one device may be relied on, other than what follows from the above.
Results may differ from the reference program's by a relative error of at most 0.014.
The reference program's roundings to bfloat16 on the way count: a program that leaves them out, or rounds other values in their place, can miss the bound.
Values may be sent and summed in bfloat16 or wider, within the bound.
No kernel may reach another device: no remote copies, remote signals or barrier semaphores. Data moves between devices by JAX's collectives and lax.ppermute only.
A program may use at most 128 MiB of HBM per device.

```python
import math
import jax
import jax.numpy as jnp
from jax import lax

D = 768
H = 12
HD = 64
FF = 3072
TOK_DEV = 1024
BUCKET_LONG = 512
BUCKET_SHORT = 128
SLOTS = 8
TOKENS = 16384
N_DP = 16


def pick_buckets(key):
    coins = jax.random.randint(jax.random.fold_in(key, 11), (N_DP,), 0, 2)
    places = jnp.arange(N_DP, dtype=jnp.int32)
    chosen = jnp.where(coins > 0, BUCKET_LONG, BUCKET_SHORT)
    chosen = jnp.where(places == 0, BUCKET_LONG, jnp.where(places == 1, BUCKET_SHORT, chosen))
    return chosen.astype(jnp.int32)


def draw_bucket_len(key, part):
    return pick_buckets(key)


def draw_seq_lengths(key, part):
    spans = pick_buckets(key)[:, None]
    floor_len = spans // 4
    raw_bits = jax.random.randint(jax.random.fold_in(key, 12), (N_DP, SLOTS), 0, 1 << 20)
    lengths = floor_len + raw_bits % (spans - floor_len + 1)
    slot_ids = jnp.arange(SLOTS, dtype=jnp.int32)[None, :]
    return jnp.where(slot_ids == 0, spans, lengths).astype(jnp.int32)


def touch_ends(drawn, own_key, low, largest):
    longest = drawn.shape.index(max(drawn.shape))
    spots = []
    for shift in (0, 1):
        where = [jax.random.randint(jax.random.fold_in(own_key, axis), (), 0, length) for axis, length in enumerate(drawn.shape)]
        where[longest] = (where[longest] + shift) % drawn.shape[longest]
        spots.append(tuple(where))
    return drawn.at[spots[0]].set(low).at[spots[1]].set(largest)


def steps_of(own_key, extent, shards, least, largest):
    loudness = 1.0
    for position, shards_of in shards:
        steps = jax.random.uniform(jax.random.fold_in(jax.random.fold_in(own_key, 6), position), (shards_of,), jnp.float32, least / len(shards), largest / len(shards))
        loudness = loudness * jnp.repeat(jnp.exp(steps), extent[position] // shards_of).reshape((-1,) + (1,) * (len(extent) - 1 - position))
    return loudness


def bell_draw(key, dims, width, bound, split=(), held_as=jnp.bfloat16):
    entries = jax.random.normal(key, dims, jnp.float32) * width
    if len(split) > 0:
        entries = steps_of(key, dims, split, -0.22, 0.18) * entries
    return jnp.clip(entries, min=-bound, max=bound).astype(held_as)


def setup_inputs(seed: int = 0) -> dict:
    splits = jax.random.split(jax.random.key(seed), 18)
    tokens = bell_draw(splits[0], (TOKENS, D), 1.0, 6.0, ((0, 16),))
    w_qkv = bell_draw(splits[1], (3, D, D), D ** -0.5, 0.21875, ((2, 2),))
    bias_qv = bell_draw(splits[2], (2, D), 0.5, 3.0, ((1, 2),), jnp.float32)
    w_out = bell_draw(splits[3], (D, D), (D // 16) ** -0.5, 0.875, ((0, 2),))
    bias_out = bell_draw(splits[4], (D,), 0.3, 2.0, (), jnp.float32)
    gain_attn = jnp.clip(1.0 + 0.1 * jax.random.normal(splits[5], (D,), jnp.float32), 0.5, 1.5)
    shift_attn = bell_draw(splits[6], (D,), 0.3, 2.0, (), jnp.float32)
    w_up = bell_draw(splits[7], (D, FF), D ** -0.5, 0.21875, ((1, 2),))
    bias_up = bell_draw(splits[8], (FF,), 0.5, 3.0, ((0, 2),), jnp.float32)
    w_down = bell_draw(splits[9], (FF, D), (FF // 4) ** -0.5, 0.21875, ((0, 2),))
    bias_down = bell_draw(splits[10], (D,), 0.3, 2.0, (), jnp.float32)
    gain_ffn = jnp.clip(1.0 + 0.1 * jax.random.normal(splits[11], (D,), jnp.float32), 0.5, 1.5)
    shift_ffn = bell_draw(splits[12], (D,), 0.3, 2.0, (), jnp.float32)
    out_grad = bell_draw(splits[13], (TOKENS, D), 1.0, 6.0, ((0, 16),))
    bucket_len = draw_bucket_len(jax.random.fold_in(splits[17], 71), 0)
    seq_lengths = draw_seq_lengths(jax.random.fold_in(splits[17], 71), 0)
    keep_mask = touch_ends((jax.random.randint(splits[16], (N_DP, SLOTS), 0, 4) < 3).astype(jnp.int32), jax.random.fold_in(splits[16], 1), 0, 1)
    return {"tokens": tokens, "w_qkv": w_qkv, "bias_qv": bias_qv, "w_out": w_out, "bias_out": bias_out, "gain_attn": gain_attn, "shift_attn": shift_attn, "w_up": w_up, "bias_up": bias_up, "w_down": w_down, "bias_down": bias_down, "gain_ffn": gain_ffn, "shift_ffn": shift_ffn, "out_grad": out_grad, "bucket_len": bucket_len, "seq_lengths": seq_lengths, "keep_mask": keep_mask}


@jax.custom_vjp
def low(v):
    return lax.optimization_barrier(v.astype(jnp.bfloat16)).astype(jnp.float32)

@jax.custom_vjp
def low_back(v):
    return v

def low_keep(v):
    return (low(v), None)

def low_pass(kept, grad):
    return (grad,)

def back_keep(v):
    return (v, None)

def back_low(kept, grad):
    return (low(grad),)
low.defvjp(low_keep, low_pass)
low_back.defvjp(back_keep, back_low)

def round_both(array_in):
    return low(low_back(array_in))

def matmul_high(left_mat, right_mat):
    return jnp.dot(left_mat, right_mat, precision=lax.Precision.HIGHEST, preferred_element_type=jnp.float32)

def layer_norm(residual, scale_vec, shift_vec):
    centre = residual - lax.optimization_barrier(jnp.mean(residual, axis=-1, keepdims=True))
    spread = lax.optimization_barrier(jnp.mean(centre * centre, axis=-1, keepdims=True))
    return centre * lax.rsqrt(spread + 1e-05) * scale_vec + shift_vec

def attend_block(pieces):
    queries, key_rows, values, seq_ids, pos_ids, seq_lens = pieces
    heads_q = queries.reshape(BUCKET_LONG, H, HD)
    heads_k = key_rows.reshape(BUCKET_LONG, H, HD)
    heads_v = values.reshape(BUCKET_LONG, H, HD)
    scores = jnp.einsum('qhe,khe->hqk', heads_q, heads_k, precision=lax.Precision.HIGHEST) * 0.125
    scores = low_back(scores)
    allowed = (seq_ids[:, None] == seq_ids[None, :]) & (pos_ids[None, :] < seq_lens[None, :])
    scores = jnp.where(allowed[None], scores, -1e+30)
    weights = low(jax.nn.softmax(scores, axis=-1))
    mixed_rows = jnp.einsum('hqk,khe->qhe', weights, heads_v, precision=lax.Precision.HIGHEST)
    return mixed_rows.reshape(BUCKET_LONG, H * HD)

def layer(tokens, params, seq_ids, pos_ids, seq_lens, keep_rows):
    w_qkv, bias_qv, w_out, bias_out, gain_attn, shift_attn, w_up, bias_up, w_down, bias_down, gain_ffn, shift_ffn = params
    row_count = tokens.shape[0]
    block_count = row_count // BUCKET_LONG
    queries = round_both(matmul_high(tokens, w_qkv[0]) + bias_qv[0])
    key_rows = round_both(matmul_high(tokens, w_qkv[1]))
    values = round_both(matmul_high(tokens, w_qkv[2]) + bias_qv[1])

    def blocked(array_in):
        return array_in.reshape((block_count, BUCKET_LONG) + array_in.shape[1:])
    attended = lax.map(jax.checkpoint(attend_block), (blocked(queries), blocked(key_rows), blocked(values), blocked(seq_ids), blocked(pos_ids), blocked(seq_lens)))
    attended = round_both(attended.reshape(row_count, D))
    attn_sum = low_back(matmul_high(attended, w_out) + bias_out)
    normed = layer_norm(tokens + attn_sum, gain_attn, shift_attn)
    pre_act = low_back(matmul_high(low(normed), w_up) + bias_up)
    activated = low(jax.nn.gelu(pre_act, approximate=False))
    ffn_sum = low_back(matmul_high(activated, w_down) + bias_down)
    final = layer_norm(normed + ffn_sum, gain_ffn, shift_ffn)
    return jnp.where(keep_rows[:, None] > 0, final, tokens)

def reference(tokens, w_qkv, bias_qv, w_out, bias_out, gain_attn, shift_attn, w_up, bias_up, w_down, bias_down, gain_ffn, shift_ffn, out_grad, bucket_len, seq_lengths, keep_mask):
    group_size = math.gcd(N_DP, max(1, 4096 // TOK_DEV))
    stretch_count = N_DP // group_size
    stretch_rows = group_size * TOK_DEV
    places = jnp.arange(TOK_DEV, dtype=jnp.int32)
    bucket_rows = bucket_len.astype(jnp.int32)[:, None]
    seq_ids = places[None, :] // bucket_rows
    pos_ids = places[None, :] - seq_ids * bucket_rows
    slot_hit = (seq_ids[:, :, None] == jnp.arange(SLOTS, dtype=jnp.int32)[None, None, :]).astype(jnp.int32)
    seq_lens = lax.optimization_barrier(jnp.sum(slot_hit * seq_lengths.astype(jnp.int32)[:, None, :], axis=-1))
    keep_rows = lax.optimization_barrier(jnp.sum(slot_hit * keep_mask.astype(jnp.int32)[:, None, :], axis=-1))
    params = (w_qkv.astype(jnp.float32), bias_qv.astype(jnp.float32), w_out.astype(jnp.float32), bias_out.astype(jnp.float32), gain_attn.astype(jnp.float32), shift_attn.astype(jnp.float32), w_up.astype(jnp.float32), bias_up.astype(jnp.float32), w_down.astype(jnp.float32), bias_down.astype(jnp.float32), gain_ffn.astype(jnp.float32), shift_ffn.astype(jnp.float32))
    inputs_all = tokens.astype(jnp.float32).reshape(stretch_count, stretch_rows, D)
    grads_all = out_grad.astype(jnp.float32).reshape(stretch_count, stretch_rows, D)
    seq_all = seq_ids.reshape(stretch_count, stretch_rows)
    pos_all = pos_ids.reshape(stretch_count, stretch_rows)
    lens_all = seq_lens.reshape(stretch_count, stretch_rows)
    keep_all = keep_rows.reshape(stretch_count, stretch_rows)

    def accumulate(totals, stretch_item):
        stretch_x, stretch_g, stretch_seq, stretch_pos, stretch_len, stretch_keep = stretch_item

        def forward(inputs_in, weights_in):
            return layer(inputs_in, weights_in, stretch_seq, stretch_pos, stretch_len, stretch_keep)
        outputs, pullback = jax.vjp(forward, stretch_x, params)
        grad_x, grad_params = pullback(stretch_g)
        totals = jax.tree.map(lambda total_part, new_part: total_part + new_part, totals, grad_params)
        return (totals, (outputs.astype(jnp.bfloat16), grad_x))
    zeros_start = jax.tree.map(jnp.zeros_like, params)
    totals, (mixed_all, dx_all) = lax.scan(accumulate, zeros_start, (inputs_all, grads_all, seq_all, pos_all, lens_all, keep_all))
    return (mixed_all.reshape(TOKENS, D), dx_all.reshape(TOKENS, D), totals[0], totals[1], totals[2], totals[3], totals[4], totals[5], totals[6], totals[7], totals[8], totals[9], totals[10], totals[11])
```

```python
import functools

import jax
import jax.numpy as jnp
from jax import lax
from jax.experimental import pallas as pl
from jax.experimental.pallas import tpu as pltpu
from jax.sharding import PartitionSpec as P

HD = 64
BUCKET_LONG = 512
LANES = 128
EPS = 1e-05
F32 = jnp.float32
BF16 = jnp.bfloat16
NEG = -1e30
MIB = 1 << 20

STEP_BITS = (
    ((0, 1, 2, 3), (1, 0, 2, 3)),
    ((2, 0, 1, 3), (0, 1, 2, 3)),
    ((1, 0, 2, 3), (2, 1, 0, 3)),
)


def dot_nn(left, right):
    return lax.dot_general(left, right, (((1,), (0,)), ((), ())), preferred_element_type=F32)


def dot_nt(left, right):
    return lax.dot_general(left, right, (((1,), (1,)), ((), ())), preferred_element_type=F32)


def dot_tn(left, right):
    return lax.dot_general(left, right, (((0,), (0,)), ((), ())), preferred_element_type=F32)


def whole(shape):
    rank = len(shape)
    return pl.BlockSpec(shape, lambda *_: (0,) * rank)


def shaped(shape, dtype):
    return jax.ShapeDtypeStruct(shape, dtype)


def call(body, out_shape, grid, scalars, in_specs, out_specs, scratch, vmem, flops, moved, trans=0):
    return pl.pallas_call(
        body,
        out_shape=out_shape,
        grid_spec=pltpu.PrefetchScalarGridSpec(
            num_scalar_prefetch=scalars,
            grid=grid,
            in_specs=in_specs,
            out_specs=out_specs,
            scratch_shapes=scratch,
        ),
        compiler_params=pltpu.CompilerParams(
            dimension_semantics=("arbitrary",) * len(grid), vmem_limit_bytes=vmem * MIB
        ),
        cost_estimate=pl.CostEstimate(flops=flops, bytes_accessed=moved, transcendentals=trans),
    )


def bucket_shift(bucket_ref):
    return jnp.where(bucket_ref[0] >= BUCKET_LONG, 9, 7)


def mask_columns(ids_ref, bucket_ref, lens_ref, rows):
    shift = bucket_shift(bucket_ref)
    first = ids_ref[0] * lax.shift_right_logical(BUCKET_LONG, shift)
    place = lax.broadcasted_iota(jnp.int32, (rows, LANES), 0)
    lane = lax.broadcasted_iota(jnp.int32, (rows, LANES), 1) & (HD - 1)
    seq = lax.shift_right_logical(place, jnp.full((rows, LANES), shift, jnp.int32))
    pos = place - lax.shift_left(seq, jnp.full((rows, LANES), shift, jnp.int32))
    length = jnp.full((rows, LANES), lens_ref[0, first], jnp.int32)
    for slot in range(1, 4):
        length = jnp.where(seq == slot, lens_ref[0, first + slot], length)
    hit = seq == lane
    query_cols = jnp.where(hit, 1.0, 0.0)
    key_cols = jnp.where(hit & (pos < length), 0.0, NEG)
    key_cols = jnp.where(lane < 4, key_cols, jnp.where(lane < 7, 1.0, 0.0))
    return query_cols.astype(BF16), key_cols.astype(BF16)


def low_half(rows):
    return lax.broadcasted_iota(jnp.int32, (rows, LANES), 1) < HD


def attn_fwd_body(last, ids, bucket, lens, x_ref, w_ref, b_ref, *rest):
    if last:
        (other_o, wo_own, wo_other, bias_out, gain, shift_vec) = rest[:6]
        qa_ref, k_ref, v_ref, o_ref, n_ref, rstd_ref, hb_ref = rest[6:13]
        q_s, am_s, bm_s = rest[13:]
    else:
        qa_ref, k_ref, v_ref, o_ref = rest[:4]
        q_s, am_s, bm_s = rest[4:]
    rows = x_ref.shape[0]
    pairs = w_ref.shape[2] // LANES
    am, bm = mask_columns(ids, bucket, lens, rows)
    am_s[...] = am
    bm_s[...] = bm
    x = x_ref[...]
    q = ((dot_nn(x, w_ref[0]) + b_ref[0:1, :]).astype(BF16).astype(F32) * 0.125).astype(BF16)
    k = dot_nn(x, w_ref[1]).astype(BF16)
    v = (dot_nn(x, w_ref[2]) + b_ref[1:2, :]).astype(BF16)
    for p in range(pairs):
        cols = slice(p * LANES, (p + 1) * LANES)
        q_s[p] = q[:, cols]
        k_ref[p] = k[:, cols]
        v_ref[p] = v[:, cols]
    tile = rows // 2

    def step(i, carry):
        p = i // 2
        r0 = pl.multiple_of((i % 2) * tile, tile)
        qp = q_s[p, pl.ds(r0, tile), :]
        amb = am_s[pl.ds(r0, tile), :]
        kp = k_ref[p]
        vp = v_ref[p]
        bmb = bm_s[...]
        low_t, low_r = low_half(tile), low_half(rows)
        sums, tops = [], []
        for par in range(2):
            own_t = low_t if par == 0 else jnp.logical_not(low_t)
            own_r = low_r if par == 0 else jnp.logical_not(low_r)
            scores = dot_nt(jnp.where(own_t, qp, amb), jnp.where(own_r, kp, bmb))
            top = jnp.max(scores, axis=1, keepdims=True)
            expo = jnp.exp(scores - top).astype(BF16)
            sums.append(dot_nn(expo, jnp.where(own_r, vp, jnp.ones_like(vp))))
            tops.append(top)
        lane = lax.broadcasted_iota(jnp.int32, (tile, LANES), 1) & (HD - 1)
        for par in range(2):
            own_t = low_t if par == 0 else jnp.logical_not(low_t)
            neg_log = -(tops[par] + jnp.log(jnp.where(own_t, 1.0, sums[par])))
            hi = neg_log.astype(BF16)
            mid = (neg_log - hi.astype(F32)).astype(BF16)
            lo = (neg_log - hi.astype(F32) - mid.astype(F32)).astype(BF16)
            cols = jnp.where(lane == 4, hi, jnp.where(lane == 5, mid, jnp.where(lane == 6, lo, amb)))
            qa_ref[2 * p + par, pl.ds(r0, tile), :] = jnp.where(own_t, qp, cols)
        total = pltpu.roll(jnp.where(low_t, sums[1], sums[0]), HD, 1)
        o_ref[p, pl.ds(r0, tile), :] = (jnp.where(low_t, sums[0], sums[1]) / total).astype(BF16)
        return carry

    lax.fori_loop(0, 2 * pairs, step, 0)
    if last:
        block = rows // 4

        def norm(i, carry):
            r = pl.ds(pl.multiple_of(i * block, block), block)
            acc = x_ref[r, :].astype(F32) + bias_out[...]
            for p in range(pairs):
                cols = slice(p * LANES, (p + 1) * LANES)
                acc += dot_nn(o_ref[p, r, :], wo_own[cols, :])
                acc += dot_nn(other_o[p, r, :], wo_other[cols, :])
            centre = acc - jnp.mean(acc, axis=1, keepdims=True)
            rstd = lax.rsqrt(jnp.mean(centre * centre, axis=1, keepdims=True) + EPS)
            normed = centre * rstd
            n_ref[r, :] = normed
            rstd_ref[r, :] = jnp.broadcast_to(rstd, (block, LANES))
            hb_ref[r, :] = (normed * gain[...] + shift_vec[...]).astype(BF16)
            return carry

        lax.fori_loop(0, 4, norm, 0)


def attn_fwd(last, scal, tokens, w, b, rows, extra=()):
    width = tokens.shape[1]
    local = w.shape[2]
    pairs = local // LANES
    trio = (pairs, rows, LANES)
    outs = [shaped((2 * pairs, rows, LANES), BF16)] + [shaped(trio, BF16)] * 3
    if last:
        outs += [shaped((rows, width), F32), shaped((rows, LANES), F32), shaped((rows, width), BF16)]
    flops = 2 * rows * local * (3 * width + 4 * rows + (2 * width if last else 0))
    moved = 2 * (rows * width + 3 * width * local + 5 * rows * local) + (rows * width * 6 if last else 0)
    return call(
        functools.partial(attn_fwd_body, last),
        outs,
        (1,),
        3,
        [
            pl.BlockSpec((rows, width), lambda i, ids, *_: (ids[0], 0)),
            whole(w.shape),
            whole(b.shape),
        ]
        + [whole(e.shape) for e in extra],
        [whole(o.shape) for o in outs],
        [pltpu.VMEM(trio, BF16), pltpu.VMEM((rows, LANES), BF16), pltpu.VMEM((rows, LANES), BF16)],
        30,
        flops,
        moved,
        2 * pairs * rows * rows,
    )(*scal, tokens, w, b, *extra)


def keep_of(ids, bucket, keep, block):
    shift = bucket_shift(bucket)
    first = ids[0] * lax.shift_right_logical(BUCKET_LONG, shift)
    return keep[0, first + lax.shift_right_logical(block * LANES, shift)] > 0


def fold_rows(array_in):
    rows, cols = array_in.shape
    return jnp.sum(array_in.reshape(rows // 8, 8, cols), axis=0)


def ffn_fwd_body(
    ids, bucket, keep, hb_ref, n_ref, up_own, up_other, bu_own, bu_other, down_own, down_other,
    gain_a, shift_a, bias_down, gain_f, shift_f, x_ref, g_ref,
    gb_own, gb_other, gp_own, gp_other, mixed_ref, dr2_ref, df_ref, vec_ref, acc, fold_s,
):
    i = pl.program_id(0)
    rows, width = hb_ref.shape

    @pl.when(i == 0)
    def _():
        acc[...] = n_ref[...] * gain_a[...] + shift_a[...] + bias_down[...]

    half = rows // 2
    for r in range(2):
        rs = slice(r * half, (r + 1) * half)
        hb = hb_ref[rs, :]
        total = None
        for up, bu, down, gb, gp in (
            (up_own, bu_own, down_own, gb_own, gp_own),
            (up_other, bu_other, down_other, gb_other, gp_other),
        ):
            u = dot_nn(hb, up[...]) + bu[...]
            cdf = 0.5 * (1.0 + lax.erf(u * 0.7071067811865476))
            pdf = jnp.exp(-0.5 * u * u) * 0.3989422804014327
            gp[rs, :] = cdf + u * pdf
            act = (u * cdf).astype(BF16)
            gb[rs, :] = act
            part = dot_nn(act, down[...])
            total = part if total is None else total + part
        acc[rs, :] += total

    @pl.when(i == pl.num_programs(0) - 1)
    def _():
        fold_s[...] = jnp.zeros_like(fold_s)

        def norm(blk, carry):
            r = pl.ds(pl.multiple_of(blk * LANES, LANES), LANES)
            kept = keep_of(ids, bucket, keep, blk)
            res = acc[r, :]
            centre = res - jnp.mean(res, axis=1, keepdims=True)
            rstd = lax.rsqrt(jnp.mean(centre * centre, axis=1, keepdims=True) + EPS)
            normed = centre * rstd
            final = normed * gain_f[...] + shift_f[...]
            mixed_ref[r, :] = jnp.where(kept, final, x_ref[r, :].astype(F32)).astype(BF16)
            grad = jnp.where(kept, g_ref[r, :].astype(F32), 0.0)
            fold_s[0] += fold_rows(grad * normed)
            fold_s[1] += fold_rows(grad)
            scaled = grad * gain_f[...]
            mean_a = jnp.mean(scaled, axis=1, keepdims=True)
            mean_b = jnp.mean(scaled * normed, axis=1, keepdims=True)
            dr2 = (scaled - mean_a - normed * mean_b) * rstd
            dr2_ref[r, :] = dr2
            df = dr2.astype(BF16)
            df_ref[r, :] = df
            fold_s[2] += fold_rows(df.astype(F32))
            return carry

        lax.fori_loop(0, rows // LANES, norm, 0)
        vec_ref[...] = jnp.sum(fold_s[...], axis=1)


def ffn_fwd(scal, hb, n1, up_own, up_other, bu_own, bu_other, down_own, down_other, vecs, tokens, out_grad):
    rows, width = hb.shape
    hidden = up_own.shape[1]
    chunk = 256
    ids_rows = pl.BlockSpec((rows, width), lambda i, ids, *_: (ids[0], 0))
    up_spec = pl.BlockSpec((width, chunk), lambda i, *_: (0, i))
    bu_spec = pl.BlockSpec((1, chunk), lambda i, *_: (0, i))
    down_spec = pl.BlockSpec((chunk, width), lambda i, *_: (i, 0))
    act_spec = pl.BlockSpec((rows, chunk), lambda i, *_: (0, i))
    outs = [
        shaped((rows, hidden), BF16), shaped((rows, hidden), BF16),
        shaped((rows, hidden), F32), shaped((rows, hidden), F32),
        shaped((rows, width), BF16), shaped((rows, width), F32), shaped((rows, width), BF16),
        shaped((3, width), F32),
    ]
    return call(
        ffn_fwd_body,
        outs,
        (hidden // chunk,),
        3,
        [whole(hb.shape), whole(n1.shape), up_spec, up_spec, bu_spec, bu_spec, down_spec, down_spec]
        + [whole(vec.shape) for vec in vecs]
        + [ids_rows, ids_rows],
        [act_spec] * 4 + [whole(o.shape) for o in outs[4:]],
        [pltpu.VMEM((rows, width), F32), pltpu.VMEM((3, 8, width), F32)],
        30,
        8 * rows * width * hidden,
        12 * rows * hidden + 8 * width * hidden + 20 * rows * width,
        4 * rows * hidden,
    )(*scal, hb, n1, up_own, up_other, bu_own, bu_other, down_own, down_other, *vecs, tokens, out_grad)


def down_grad_body(pos, gb_own, gb_other, df_ref, out_own, out_other):
    i = pl.program_id(0)
    count, size, _ = out_own.shape
    per = gb_own.shape[1] // size
    df = df_ref[...]
    for table, gb, out in ((1, gb_other, out_other), (0, gb_own, out_own)):
        value = dot_tn(gb[...], df).astype(BF16)
        for c in range(per):
            out[pos[table, i * per + c]] = value[c * size : (c + 1) * size, :]


def down_grad(pos, gb_own, gb_other, df, count):
    rows, width = df.shape
    hidden = gb_own.shape[1]
    size = hidden // count
    chunk = size * (4 if count % 4 == 0 else 1)
    gb_spec = pl.BlockSpec((rows, chunk), lambda i, *_: (0, i))
    outs = [shaped((count, size, width), BF16)] * 2
    return call(
        down_grad_body,
        outs,
        (hidden // chunk,),
        1,
        [gb_spec, gb_spec, whole(df.shape)],
        [whole(o.shape) for o in outs],
        [],
        24,
        4 * rows * width * hidden,
        4 * rows * hidden + 4 * width * hidden + 2 * rows * width,
    )(pos, gb_own, gb_other, df)


def ffn_bwd_body(
    pos, df_ref, dr2_ref, hb_ref, gp_own, gp_other, down_own, down_other, up_own, up_other,
    n_ref, rstd_ref, gain_a, o_own, o_other,
    out_own, out_other, bu_own, bu_other, dr1_ref, da_ref, vec_ref, acc, fold_s,
):
    i = pl.program_id(0)
    rows, width = df_ref.shape
    count = out_own.shape[0]
    up_rows = width // count
    chunk = up_own.shape[1]
    per_line = width // chunk
    line = pl.multiple_of((i // per_line) * up_rows, up_rows)
    col = pl.multiple_of((i % per_line) * chunk, chunk)

    @pl.when(i == 0)
    def _():
        acc[...] = dr2_ref[...]

    df = df_ref[...]
    hb = hb_ref[...]
    total = None
    for table, gp, down, up, bu, out in (
        (1, gp_other, down_other, up_other, bu_other, out_other),
        (0, gp_own, down_own, up_own, bu_own, out_own),
    ):
        du = (dot_nt(df, down[...]) * gp[...]).astype(BF16)
        bu[...] = jnp.sum(fold_rows(du.astype(F32)), axis=0, keepdims=True)
        value = dot_tn(hb, du).astype(BF16)
        for a in range(count):
            out[pos[table, a], pl.ds(line, up_rows), pl.ds(col, chunk)] = value[a * up_rows : (a + 1) * up_rows, :]
        part = dot_nt(du, up[...])
        total = part if total is None else total + part
    acc[...] += total

    @pl.when(i == pl.num_programs(0) - 1)
    def _():
        fold_s[...] = jnp.zeros_like(fold_s)

        def norm(blk, carry):
            r = pl.ds(pl.multiple_of(blk * LANES, LANES), LANES)
            grad = acc[r, :]
            normed = n_ref[r, :]
            fold_s[0] += fold_rows(grad * normed)
            fold_s[1] += fold_rows(grad)
            scaled = grad * gain_a[...]
            mean_a = jnp.mean(scaled, axis=1, keepdims=True)
            mean_b = jnp.mean(scaled * normed, axis=1, keepdims=True)
            dr1 = (scaled - mean_a - normed * mean_b) * rstd_ref[r, 0:1]
            dr1_ref[r, :] = dr1
            da = dr1.astype(BF16)
            da_ref[r, :] = da
            fold_s[2] += fold_rows(da.astype(F32))
            return carry

        lax.fori_loop(0, rows // LANES, norm, 0)
        vec_ref[...] = jnp.sum(fold_s[...], axis=1)
        da = da_ref[...]
        pairs = o_own.shape[0]
        size = pairs * LANES // count
        first = out_own.shape[1] - size
        for table, o_ref, out in ((1, o_other, out_other), (0, o_own, out_own)):
            value = jnp.concatenate([dot_tn(o_ref[p], da) for p in range(pairs)], axis=0)
            for a in range(count):
                out[pos[table, a], first : first + size, :] = value[a * size : (a + 1) * size, :].astype(BF16)


def ffn_bwd(pos, df, dr2, hb, gp_own, gp_other, down_own, down_other, up_own, up_other, n1, rstd, gain_a, o_own, o_other, count):
    rows, width = df.shape
    hidden = up_own.shape[1]
    local = o_own.shape[0] * LANES
    chunk = 256
    block = (width * hidden + local * width) // (count * width)
    up_spec = pl.BlockSpec((width, chunk), lambda i, *_: (0, i))
    down_spec = pl.BlockSpec((chunk, width), lambda i, *_: (i, 0))
    act_spec = pl.BlockSpec((rows, chunk), lambda i, *_: (0, i))
    bu_spec = pl.BlockSpec((1, chunk), lambda i, *_: (0, i))
    outs = [
        shaped((count, block, width), BF16), shaped((count, block, width), BF16),
        shaped((1, hidden), F32), shaped((1, hidden), F32),
        shaped((rows, width), F32), shaped((rows, width), BF16), shaped((3, width), F32),
    ]
    return call(
        ffn_bwd_body,
        outs,
        (hidden // chunk,),
        1,
        [whole(df.shape), whole(dr2.shape), whole(hb.shape), act_spec, act_spec, down_spec, down_spec, up_spec, up_spec]
        + [whole(n1.shape), whole(rstd.shape), whole(gain_a.shape), whole(o_own.shape), whole(o_other.shape)],
        [whole(o.shape) for o in outs[:2]] + [bu_spec] * 2 + [whole(o.shape) for o in outs[4:]],
        [pltpu.VMEM((rows, width), F32), pltpu.VMEM((3, 8, width), F32)],
        40,
        12 * rows * width * hidden + 4 * rows * local * width,
        8 * rows * hidden + 12 * width * hidden + 20 * rows * width,
    )(pos, df, dr2, hb, gp_own, gp_other, down_own, down_other, up_own, up_other, n1, rstd, gain_a, o_own, o_other)


def attn_bwd_body(table, ids, bucket, lens, keep, pos, qa_ref, k_ref, v_ref, da_ref, wo_ref, w_ref, x_ref, *rest):
    if table == 1:
        dr1_ref, g_ref, dw_ref, db_ref, ig_ref, do_s, dq_s, dk_s, dv_s, bm_s = rest
    else:
        ig_in, dw_ref, db_ref, ig_ref, do_s, dq_s, dk_s, dv_s, bm_s = rest
    rows, width = da_ref.shape
    pairs = k_ref.shape[0]
    local = pairs * LANES
    _, bm = mask_columns(ids, bucket, lens, rows)
    bm_s[...] = bm
    do = dot_nt(da_ref[...], wo_ref[...]).astype(BF16)
    for p in range(pairs):
        do_s[p] = do[:, p * LANES : (p + 1) * LANES]
    tile = rows // 2

    def step(p, carry):
        kp = k_ref[p]
        vp = v_ref[p]
        bmb = bm_s[...]
        low_t, low_r = low_half(tile), low_half(rows)
        zero_t, zero_r = jnp.zeros((tile, LANES), BF16), jnp.zeros((rows, LANES), BF16)
        dk_sum = dv_sum = None
        for rb in range(2):
            r = pl.ds(rb * tile, tile)
            dop = do_s[p, r, :]
            dq = None
            for par in range(2):
                own_t = low_t if par == 0 else jnp.logical_not(low_t)
                own_r = low_r if par == 0 else jnp.logical_not(low_r)
                qa = qa_ref[2 * p + par, r, :]
                doa = jnp.where(own_t, dop, zero_t)
                prob = jnp.exp(dot_nt(jnp.where(own_r, kp, bmb), qa))
                dprob = dot_nt(vp, doa)
                inner = jnp.sum(prob * dprob, axis=0, keepdims=True)
                dscore = (prob * (dprob - inner)).astype(BF16)
                dv = dot_nn(prob.astype(BF16), doa)
                dk = dot_nn(dscore, jnp.where(own_t, qa, zero_t))
                dqp = dot_tn(dscore, jnp.where(own_r, kp, zero_r))
                dv_sum = dv if dv_sum is None else dv_sum + dv
                dk_sum = dk if dk_sum is None else dk_sum + dk
                dq = dqp if dq is None else dq + dqp
            dq_s[p, r, :] = (dq * 0.125).astype(BF16)
        dk_s[p] = dk_sum.astype(BF16)
        dv_s[p] = dv_sum.astype(BF16)
        return carry

    lax.fori_loop(0, pairs, step, 0)
    x = x_ref[...]
    count, block, _ = dw_ref.shape
    size = width // count
    grads = []
    for j, ref in enumerate((dq_s, dk_s, dv_s)):
        grad = jnp.concatenate([ref[p] for p in range(pairs)], axis=1)
        grads.append(grad)
        if j != 1:
            db_ref[j // 2 : j // 2 + 1, :] = jnp.sum(fold_rows(grad.astype(F32)), axis=0, keepdims=True)
        value = dot_tn(x, grad).astype(BF16)
        for a in range(count):
            dw_ref[pos[table, a], j * size : (j + 1) * size, :] = value[a * size : (a + 1) * size, :]
    back = dot_nt(grads[0], w_ref[0]) + dot_nt(grads[1], w_ref[1]) + dot_nt(grads[2], w_ref[2])
    if table == 1:
        for blk in range(rows // LANES):
            r = slice(blk * LANES, (blk + 1) * LANES)
            kept = keep_of(ids, bucket, keep, blk)
            ig_ref[r, :] = back[r, :] + (dr1_ref[r, :] + jnp.where(kept, 0.0, g_ref[r, :].astype(F32)))
    else:
        ig_ref[...] = back + ig_in[...]


def attn_bwd(table, scal, pos, qa, k, v, da, wo, w, tokens, extra, count):
    rows, width = da.shape
    pairs = k.shape[0]
    local = pairs * LANES
    ids_rows = pl.BlockSpec((rows, width), lambda i, ids, *_: (ids[0], 0))
    outs = [
        shaped((count, 3 * width // count, local), BF16),
        shaped((2, local), F32),
        shaped((rows, width), F32),
    ]
    trio = pltpu.VMEM((pairs, rows, LANES), BF16)
    extra_specs = [whole(extra[0].shape)] + ([ids_rows] if table == 1 else [])
    return call(
        functools.partial(attn_bwd_body, table),
        outs,
        (1,),
        5,
        [whole(qa.shape), whole(k.shape), whole(v.shape), whole(da.shape), whole(wo.shape), whole(w.shape), ids_rows]
        + extra_specs,
        [whole(o.shape) for o in outs],
        [trio] * 4 + [pltpu.VMEM((rows, LANES), BF16)],
        40,
        2 * rows * local * (7 * width + 10 * rows),
        2 * (rows * local * 4 + width * local * 7 + rows * width * 2) + 8 * rows * width,
        2 * pairs * rows * rows,
    )(*scal, pos, qa, k, v, da, wo, w, tokens, *extra)


def place_body(splits, pos, low_ref, high_ref, *out_refs):
    low = pos[pl.program_id(0)] < pos.shape[0] // 2
    for ref, chosen in ((low_ref, low), (high_ref, jnp.logical_not(low))):

        @pl.when(chosen)
        def _(ref=ref):
            for out, pieces in zip(out_refs, splits, strict=True):
                for index, start, size, c0, c1 in pieces:
                    out[index + (slice(None), slice(c0, c1))] = ref[0, start : start + size, :].astype(F32)


def place(pos, low, high, outs, out_specs, splits):
    half, block, width = low.shape
    count = 2 * half
    return call(
        functools.partial(place_body, splits),
        outs,
        (count,),
        1,
        [
            pl.BlockSpec((1, block, width), lambda a, pos: (jnp.minimum(pos[a], half - 1), 0, 0)),
            pl.BlockSpec((1, block, width), lambda a, pos: (jnp.maximum(pos[a] - half, 0), 0, 0)),
        ],
        out_specs,
        [],
        16,
        0,
        6 * count * block * width,
    )(pos, low, high)


def swap_cores(array_in, cores):
    return lax.ppermute(array_in, "tensor", [(c, cores - 1 - c) for c in range(cores)])


def sum_over_groups(mesh, batch, own, other):
    groups, cores = mesh.shape["dp"], mesh.shape["tensor"]
    steps = own.shape[0].bit_length() - 1

    def exchange(array_in, step):
        pairs = []
        for i in range(groups):
            for c in range(cores):
                j = i ^ (1 << STEP_BITS[batch][c % 2][step])
                pairs.append((i * cores + c, j * cores + c))
        return lax.ppermute(array_in, ("dp", "tensor"), pairs)

    def added(left, right):
        return (left.astype(F32) + right.astype(F32)).astype(BF16)

    current = added(own, swap_cores(other, cores))
    for step in range(steps):
        half = current.shape[0] // 2
        current = added(current[:half], exchange(current[half:], step))
    outer = groups >> steps
    if outer > 1:
        inner = 1 << steps
        members = [[o * inner + i for o in range(outer)] for i in range(inner)]
        current = lax.psum(current, "dp", axis_index_groups=members)
    for step in range(steps - 1, 0, -1):
        current = jnp.concatenate([current, exchange(current, step)], axis=0)
    return current, exchange(current, 0)


def block_places(mesh, count):
    steps = count.bit_length() - 1
    core = lax.axis_index("tensor")
    rel = (lax.axis_index("dp") & (count - 1)) ^ jnp.arange(count, dtype=jnp.int32)
    tables = []
    for bits in STEP_BITS:
        both = []
        for order in bits:
            place_of = jnp.zeros_like(rel)
            for step in range(steps):
                place_of |= ((rel >> order[step]) & 1) << (steps - 1 - step)
            both.append(place_of)
        even = (core % 2) == 0
        tables.append(jnp.stack([jnp.where(even, both[0], both[1]), jnp.where(even, both[1], both[0])]))
    return jnp.stack(tables)


def per_device(
    mesh,
    tokens,
    w_qkv,
    bias_qv,
    w_out,
    bias_out,
    gain_attn,
    shift_attn,
    w_up,
    bias_up,
    w_down,
    bias_down,
    gain_ffn,
    shift_ffn,
    out_grad,
    bucket_len,
    seq_lengths,
    keep_mask,
):
    cores = mesh.shape["tensor"]
    count = min(16, mesh.shape["dp"])
    width = tokens.shape[1]
    rows = tokens.shape[0] // cores
    hidden = w_up.shape[1]
    local = w_qkv.shape[2]
    core = lax.axis_index("tensor").astype(jnp.int32)
    ids = core[None]
    places = block_places(mesh, count)
    own_row = lambda vec: vec.reshape(1, -1)

    w_qkv_o = swap_cores(w_qkv, cores)
    bias_qv_o = swap_cores(bias_qv, cores)
    w_out_o = swap_cores(w_out, cores)
    bias_up_o = swap_cores(bias_up, cores)
    w_up_o = swap_cores(w_up, cores)
    w_down_o = swap_cores(w_down, cores)

    attn_scal = (ids, bucket_len, seq_lengths)
    qa, k, v, o = attn_fwd(False, attn_scal, tokens, w_qkv, bias_qv, rows)
    qa_o, k_o, v_o, o_o, n1, rstd, hb = attn_fwd(
        True,
        attn_scal,
        tokens,
        w_qkv_o,
        bias_qv_o,
        rows,
        (o, w_out_o, w_out, own_row(bias_out), own_row(gain_attn), own_row(shift_attn)),
    )
    keep_scal = (ids, bucket_len, keep_mask)
    vecs = tuple(own_row(vec) for vec in (gain_attn, shift_attn, bias_down, gain_ffn, shift_ffn))
    gb, gb_o, gp, gp_o, mixed, dr2, df, vec_f = ffn_fwd(
        keep_scal, hb, n1, w_up, w_up_o, own_row(bias_up), own_row(bias_up_o), w_down, w_down_o, vecs, tokens, out_grad
    )
    down_own, down_other = down_grad(places[0], gb, gb_o, df, count)
    down_low, down_high = sum_over_groups(mesh, 0, down_own, down_other)
    up_own, up_other, bu, bu_o, dr1, da, vec_a = ffn_bwd(
        places[1], df, dr2, hb, gp, gp_o, w_down, w_down_o, w_up, w_up_o, n1, rstd, own_row(gain_attn), o, o_o, count
    )
    up_low, up_high = sum_over_groups(mesh, 1, up_own, up_other)
    bwd_scal = (ids, bucket_len, seq_lengths, keep_mask)
    qkv_other, db_o, ig_part = attn_bwd(
        1, bwd_scal, places[2], qa_o, k_o, v_o, da, w_out_o, w_qkv_o, tokens, (dr1, out_grad), count
    )
    qkv_own, db, ig = attn_bwd(0, bwd_scal, places[2], qa, k, v, da, w_out, w_qkv, tokens, (ig_part,), count)
    qkv_low, qkv_high = sum_over_groups(mesh, 2, qkv_own, qkv_other)

    def both_cores(first, second):
        return jnp.where(core == 0, jnp.concatenate([first, second], -1), jnp.concatenate([second, first], -1))

    small = jnp.concatenate(
        [both_cores(db, db_o).reshape(-1), both_cores(bu, bu_o).reshape(-1), vec_a.reshape(-1), vec_f.reshape(-1)]
    ).reshape(-1, width)
    small = lax.psum(small, ("dp", "tensor"))
    pair_rows = 2 * local * cores // width
    up_lines = hidden * cores // width
    grad_bias_qv = lax.dynamic_slice(small[:pair_rows].reshape(2, -1), (0, core * local), (2, local))
    grad_bias_up = lax.dynamic_slice(small[pair_rows : pair_rows + up_lines].reshape(-1), (core * hidden,), (hidden,))
    norms = small[pair_rows + up_lines :]

    def rows_of_both(part):
        other = swap_cores(part, cores)
        return jnp.where(core == 0, jnp.concatenate([part, other]), jnp.concatenate([other, part]))

    size = hidden // count
    grad_w_down = place(
        places[0, 0],
        down_low,
        down_high,
        [shaped((hidden, width), F32)],
        [pl.BlockSpec((size, width), lambda a, _: (a, 0))],
        [[((), 0, size, 0, width)]],
    )[0]
    size, out_size = width // count, local // count
    lines = hidden // width
    grad_w_up, grad_w_out = place(
        places[1, 0],
        up_low,
        up_high,
        [shaped((width, hidden), F32), shaped((local, width), F32)],
        [pl.BlockSpec((size, hidden), lambda a, _: (a, 0)), pl.BlockSpec((out_size, width), lambda a, _: (a, 0))],
        [
            [((), n * size, size, n * width, (n + 1) * width) for n in range(lines)],
            [((), lines * size, out_size, 0, width)],
        ],
    )
    grad_w_qkv = place(
        places[2, 0],
        qkv_low,
        qkv_high,
        [shaped((3, width, local), F32)],
        [pl.BlockSpec((3, size, local), lambda a, _: (0, a, 0))],
        [[((n,), n * size, size, 0, local) for n in range(3)]],
    )[0]
    return (
        rows_of_both(mixed),
        rows_of_both(ig),
        grad_w_qkv,
        grad_bias_qv,
        grad_w_out,
        norms[2],
        norms[0],
        norms[1],
        grad_w_up,
        grad_bias_up,
        grad_w_down,
        norms[5],
        norms[3],
        norms[4],
    )


def solution(mesh):
    in_specs = (
        P("dp", None),
        P(None, None, "tensor"),
        P(None, "tensor"),
        P("tensor", None),
        P(),
        P(),
        P(),
        P(None, "tensor"),
        P("tensor"),
        P("tensor", None),
        P(),
        P(),
        P(),
        P("dp", None),
        P("dp"),
        P("dp", None),
        P("dp", None),
    )
    out_specs = (
        P("dp", None),
        P("dp", None),
        P(None, None, "tensor"),
        P(None, "tensor"),
        P("tensor", None),
        P(),
        P(),
        P(),
        P(None, "tensor"),
        P("tensor"),
        P("tensor", None),
        P(),
        P(),
        P(),
    )
    return jax.shard_map(
        functools.partial(per_device, mesh),
        mesh=mesh,
        in_specs=in_specs,
        out_specs=out_specs,
        check_vma=False,
    )
```

```python
import functools

import jax
import jax.numpy as jnp
from jax import lax
from jax.experimental import pallas as pl
from jax.experimental.pallas import tpu as pltpu
from jax.sharding import PartitionSpec as P

HD = 64
BUCKET_LONG = 512
LANES = 128
EPS = 1e-05
F32 = jnp.float32
BF16 = jnp.bfloat16
NEG = -1e30
MIB = 1 << 20
VMEM_MIB = 16
COVER = 20

STEP_BITS = (
    ((0, 1, 2), (1, 0, 2)),
    ((2, 0, 1), (0, 1, 2)),
    ((1, 0, 2), (2, 1, 0)),
)


def dot_nn(left, right):
    return lax.dot_general(left, right, (((1,), (0,)), ((), ())), preferred_element_type=F32)


def dot_nt(left, right):
    return lax.dot_general(left, right, (((1,), (1,)), ((), ())), preferred_element_type=F32)


def dot_tn(left, right):
    return lax.dot_general(left, right, (((0,), (0,)), ((), ())), preferred_element_type=F32)


def resident():
    return pl.BlockSpec(memory_space=pltpu.VMEM)


def anywhere():
    return pl.BlockSpec(memory_space=pl.ANY)


def shaped(shape, dtype):
    return jax.ShapeDtypeStruct(shape, dtype)


def call(body, outs, scalars, operands, scratch=(), vmem=VMEM_MIB, flops=0, moved=0, trans=0, **kwargs):
    specs = kwargs.pop("in_specs", None) or [resident()] * len(operands)
    return pl.pallas_call(
        body,
        out_shape=outs,
        grid_spec=pltpu.PrefetchScalarGridSpec(
            num_scalar_prefetch=len(scalars),
            grid=(1,),
            in_specs=specs,
            out_specs=kwargs.pop("out_specs", None) or [resident()] * len(outs),
            scratch_shapes=list(scratch),
        ),
        compiler_params=pltpu.CompilerParams(dimension_semantics=("arbitrary",), vmem_limit_bytes=vmem * MIB),
        cost_estimate=pl.CostEstimate(flops=COVER * flops, bytes_accessed=moved, transcendentals=trans),
        **kwargs,
    )(*scalars, *operands)


def chunk_of(index, size):
    return pl.ds(pl.multiple_of(index * size, size), size)


def after(value, *earlier):
    return lax.optimization_barrier((value,) + earlier)[0]


def move_bits(number, pairs):
    out = 0
    for take, put in pairs:
        out = out | lax.shift_left(lax.shift_right_logical(number, take) & 1, put)
    return out


def spot_of(ids, batch, kind, number, count):
    steps = count.bit_length() - 1
    me = ids[1] & (count - 1)
    down = range(steps - 1, -1, -1)
    number = jnp.int32(number) if isinstance(number, int) else number
    spots = []
    for core in range(2):
        bits = STEP_BITS[batch][1 - core if kind == 1 else core][:steps]
        if kind == 2:
            spots.append(move_bits(number, zip(down, bits, strict=True)) ^ me)
        else:
            spots.append(move_bits(number ^ me, zip(bits, down, strict=True)))
    return jnp.where((ids[0] & 1) == 0, spots[0], spots[1])


def bucket_shift(bucket_ref):
    return jnp.where(bucket_ref[0] >= BUCKET_LONG, 9, 7)


def mask_columns(ids_ref, bucket_ref, lens_ref, rows):
    shift = bucket_shift(bucket_ref)
    first = ids_ref[0] * lax.shift_right_logical(BUCKET_LONG, shift)
    place = lax.broadcasted_iota(jnp.int32, (rows, LANES), 0)
    lane = lax.broadcasted_iota(jnp.int32, (rows, LANES), 1) & (HD - 1)
    seq = lax.shift_right_logical(place, jnp.full((rows, LANES), shift, jnp.int32))
    pos = place - lax.shift_left(seq, jnp.full((rows, LANES), shift, jnp.int32))
    length = jnp.full((rows, LANES), lens_ref[0, first], jnp.int32)
    for slot in range(1, 4):
        length = jnp.where(seq == slot, lens_ref[0, first + slot], length)
    hit = seq == lane
    query_cols = jnp.where(hit, 1.0, 0.0)
    key_cols = jnp.where(hit & (pos < length), 0.0, NEG)
    key_cols = jnp.where(lane < 4, key_cols, jnp.where(lane < 7, 1.0, 0.0))
    return query_cols.astype(BF16), key_cols.astype(BF16)


def low_half(rows):
    return lax.broadcasted_iota(jnp.int32, (rows, LANES), 1) < HD


def row_of(vec_ref):
    return vec_ref[...].reshape(1, -1)


def attn_fwd_body(last, ids, bucket, lens, x_ref, w_ref, b_ref, *rest):
    if last:
        (other_o, wo_own, wo_other, bias_out, gain, shift_vec) = rest[:6]
        qa_ref, k_ref, v_ref, o_ref, n_ref, rstd_ref, hb_ref = rest[6:13]
    else:
        qa_ref, k_ref, v_ref, o_ref = rest[:4]
    am_s, bm_s = rest[-2:]
    pairs, rows, _ = k_ref.shape
    am_s[...], bm_s[...] = mask_columns(ids, bucket, lens, rows)
    tile = rows // 2

    def pair(p, carry):
        cols = chunk_of(p, LANES)
        weights = jnp.concatenate([w_ref[n, :, cols] for n in range(3)], axis=1)
        qkv = dot_nn(x_ref[chunk_of(ids[0], rows), :], weights)
        qp = ((qkv[:, :LANES] + b_ref[0:1, cols]).astype(BF16).astype(F32) * 0.125).astype(BF16)
        kp = qkv[:, LANES : 2 * LANES].astype(BF16)
        vp = (qkv[:, 2 * LANES :] + b_ref[1:2, cols]).astype(BF16)
        k_ref[p] = kp
        v_ref[p] = vp
        bm = bm_s[...]
        low_r, low_t = low_half(rows), low_half(tile)
        lane = lax.broadcasted_iota(jnp.int32, (tile, LANES), 1) & (HD - 1)
        for rb in range(2):
            r = slice(rb * tile, (rb + 1) * tile)
            am = am_s[r, :]
            qpr = qp[r, :]
            sums = []
            for par in range(2):
                own_t = low_t if par == 0 else jnp.logical_not(low_t)
                own_r = low_r if par == 0 else jnp.logical_not(low_r)
                scores = dot_nt(jnp.where(own_t, qpr, am), jnp.where(own_r, kp, bm))
                top = jnp.max(scores, axis=1, keepdims=True)
                expo = jnp.exp(scores - top).astype(BF16)
                total = dot_nn(expo, jnp.where(own_r, vp, jnp.ones_like(vp)))
                sums.append(total)
                neg_log = -(top + jnp.log(jnp.where(own_t, 1.0, total)))
                hi = neg_log.astype(BF16)
                mid = (neg_log - hi.astype(F32)).astype(BF16)
                lo = (neg_log - hi.astype(F32) - mid.astype(F32)).astype(BF16)
                parts = jnp.where(lane == 4, hi, jnp.where(lane == 5, mid, jnp.where(lane == 6, lo, am)))
                qa_ref[2 * p + par, r, :] = jnp.where(own_t, qpr, parts)
            total = pltpu.roll(jnp.where(low_t, sums[1], sums[0]), HD, 1)
            o_ref[p, r, :] = (jnp.where(low_t, sums[0], sums[1]) / total).astype(BF16)
        return carry

    lax.fori_loop(0, pairs, pair, 0)
    if last:
        block = rows // 4
        gain_row, shift_row, bias_row = row_of(gain), row_of(shift_vec), row_of(bias_out)

        def norm(i, carry):
            r = chunk_of(i, block)
            heads = [o_ref[n, r, :] for n in range(pairs)] + [other_o[n, r, :] for n in range(pairs)]
            weights = jnp.concatenate([wo_own[...], wo_other[...]], axis=0)
            acc = dot_nn(jnp.concatenate(heads, axis=1), weights)
            acc += x_ref[pl.ds(pl.multiple_of(ids[0] * rows + i * block, block), block), :].astype(F32) + bias_row
            centre = acc - jnp.mean(acc, axis=1, keepdims=True)
            rstd = lax.rsqrt(jnp.mean(centre * centre, axis=1, keepdims=True) + EPS)
            normed = centre * rstd
            n_ref[r, :] = normed
            rstd_ref[r, :] = jnp.broadcast_to(rstd, (block, LANES))
            hb_ref[r, :] = (normed * gain_row + shift_row).astype(BF16)
            return carry

        lax.fori_loop(0, 4, norm, 0)


def attn_fwd(last, scal, tokens, w, b, rows, extra=()):
    width = tokens.shape[1]
    local = w.shape[2]
    pairs = local // LANES
    outs = [shaped((2 * pairs, rows, LANES), BF16)] + [shaped((pairs, rows, LANES), BF16)] * 3
    if last:
        outs += [shaped((rows, width), F32), shaped((rows, LANES), F32), shaped((rows, width), BF16)]
    return call(
        functools.partial(attn_fwd_body, last),
        outs,
        scal,
        (tokens, w, b, *extra),
        [pltpu.VMEM((rows, LANES), BF16)] * 2,
        flops=2 * rows * local * (3 * width + 4 * rows + (2 * width if last else 0)),
        moved=2 * (rows * width + 3 * width * local + 5 * rows * local),
        trans=2 * pairs * rows * rows,
    )


def keep_of(ids, bucket, keep, block):
    shift = bucket_shift(bucket)
    first = ids[0] * lax.shift_right_logical(BUCKET_LONG, shift)
    return keep[0, first + lax.shift_right_logical(block * LANES, shift)] > 0


def fold_rows(array_in):
    rows, cols = array_in.shape
    return jnp.sum(array_in.reshape(rows // 8, 8, cols), axis=0)


def ffn_fwd_body(
    ids, bucket, keep, hb_ref, n_ref, up_own, up_other, bu_own, bu_other, down_own, down_other,
    gain_a, shift_a, bias_down, gain_f, shift_f, x_ref, g_ref,
    gb_own, gb_other, gp_own, gp_other, mixed_ref, dr2_ref, df_ref, vec_ref, acc, fold_s,
):
    rows, width = hb_ref.shape
    acc[...] = n_ref[...] * row_of(gain_a) + (row_of(shift_a) + row_of(bias_down))
    half = rows // 2
    chunk = 256

    def hidden(i, carry):
        cols = chunk_of(i, chunk)
        for r in range(2):
            rs = slice(r * half, (r + 1) * half)
            hb = hb_ref[rs, :]
            total = None
            for up, bu, down, gb, gp in (
                (up_own, bu_own, down_own, gb_own, gp_own),
                (up_other, bu_other, down_other, gb_other, gp_other),
            ):
                u = dot_nn(hb, up[:, cols]) + bu[cols].reshape(1, -1)
                cdf = 0.5 * (1.0 + lax.erf(u * 0.7071067811865476))
                pdf = jnp.exp(-0.5 * u * u) * 0.3989422804014327
                gp[rs, cols] = cdf + u * pdf
                act = (u * cdf).astype(BF16)
                gb[rs, cols] = act
                part = dot_nn(act, down[cols, :])
                total = part if total is None else total + part
            acc[rs, :] += total
        return carry

    lax.fori_loop(0, up_own.shape[1] // chunk, hidden, 0)
    fold_s[...] = jnp.zeros_like(fold_s)
    gain_row, shift_row = row_of(gain_f), row_of(shift_f)

    def norm(blk, carry):
        r = chunk_of(blk, LANES)
        far = pl.ds(pl.multiple_of(ids[0] * rows + blk * LANES, LANES), LANES)
        kept = keep_of(ids, bucket, keep, blk)
        res = acc[r, :]
        centre = res - jnp.mean(res, axis=1, keepdims=True)
        rstd = lax.rsqrt(jnp.mean(centre * centre, axis=1, keepdims=True) + EPS)
        normed = centre * rstd
        final = normed * gain_row + shift_row
        mixed_ref[r, :] = jnp.where(kept, final, x_ref[far, :].astype(F32)).astype(BF16)
        grad = jnp.where(kept, g_ref[far, :].astype(F32), 0.0)
        fold_s[0] += fold_rows(grad * normed)
        fold_s[1] += fold_rows(grad)
        scaled = grad * gain_row
        mean_a = jnp.mean(scaled, axis=1, keepdims=True)
        mean_b = jnp.mean(scaled * normed, axis=1, keepdims=True)
        dr2 = (scaled - mean_a - normed * mean_b) * rstd
        dr2_ref[r, :] = dr2
        df = dr2.astype(BF16)
        df_ref[r, :] = df
        fold_s[2] += fold_rows(df.astype(F32))
        return carry

    lax.fori_loop(0, rows // LANES, norm, 0)
    vec_ref[...] = jnp.sum(fold_s[...], axis=1)


def ffn_fwd(scal, hb, n1, up_own, up_other, bu_own, bu_other, down_own, down_other, vecs, tokens, out_grad):
    rows, width = hb.shape
    hidden = up_own.shape[1]
    outs = [
        shaped((rows, hidden), BF16), shaped((rows, hidden), BF16),
        shaped((rows, hidden), F32), shaped((rows, hidden), F32),
        shaped((rows, width), BF16), shaped((rows, width), F32), shaped((rows, width), BF16),
        shaped((3, width), F32),
    ]
    return call(
        ffn_fwd_body,
        outs,
        scal,
        (hb, n1, up_own, up_other, bu_own, bu_other, down_own, down_other, *vecs, tokens, out_grad),
        [pltpu.VMEM((rows, width), F32), pltpu.VMEM((3, 8, width), F32)],
        flops=8 * rows * width * hidden,
        moved=12 * rows * hidden + 8 * width * hidden + 20 * rows * width,
        trans=4 * rows * hidden,
    )


def down_grad_body(kind, ids, gb_ref, df_ref, out_ref):
    count, size, _ = out_ref.shape
    per = 2 if count % 2 == 0 else 1

    def step(i, carry):
        value = dot_tn(gb_ref[:, chunk_of(i, per * size)], df_ref[...]).astype(BF16)
        for c in range(per):
            out_ref[spot_of(ids, 0, kind, i * per + c, count)] = value[c * size : (c + 1) * size, :]
        return carry

    lax.fori_loop(0, count // per, step, 0)


def down_grad(kind, ids, gb, df, count):
    rows, width = df.shape
    hidden = gb.shape[1]
    return call(
        functools.partial(down_grad_body, kind),
        [shaped((count, hidden // count, width), BF16)],
        (ids,),
        (gb, df),
        flops=2 * rows * width * hidden,
        moved=2 * rows * hidden + 2 * width * hidden + 2 * rows * width,
    )[0]


def ffn_bwd_body(kind, ids, df_ref, hb_ref, gp_ref, down_ref, up_ref, *rest):
    if kind == 1:
        dr2_ref, out_ref, bu_ref, acc = rest
        acc[...] = dr2_ref[...]
    else:
        acc_in, n_ref, rstd_ref, gain_a, out_ref, bu_ref, dr1_ref, da_ref, vec_ref, acc, fold_s = rest
        acc[...] = acc_in[...]
    rows, width = df_ref.shape
    count, lines, _ = out_ref.shape
    hidden = up_ref.shape[1]
    up_rows = width // count
    chunk = 384
    per_line = width // chunk

    def step(i, carry):
        cols = chunk_of(i, chunk)
        du = (dot_nt(df_ref[...], down_ref[cols, :]) * gp_ref[:, cols]).astype(BF16)
        bu_ref[:, cols] = jnp.sum(fold_rows(du.astype(F32)), axis=0, keepdims=True)
        value = dot_tn(hb_ref[...], du).astype(BF16)
        line, col = chunk_of(i // per_line, up_rows), chunk_of(i % per_line, chunk)
        for a in range(count):
            out_ref[spot_of(ids, 1, kind, a, count), line, col] = value[a * up_rows : (a + 1) * up_rows, :]
        acc[...] += dot_nt(du, up_ref[:, cols])
        return carry

    lax.fori_loop(0, hidden // chunk, step, 0)
    if kind == 0:
        fold_s[...] = jnp.zeros_like(fold_s)
        gain_row = row_of(gain_a)

        def norm(blk, carry):
            r = chunk_of(blk, LANES)
            grad = acc[r, :]
            normed = n_ref[r, :]
            fold_s[0] += fold_rows(grad * normed)
            fold_s[1] += fold_rows(grad)
            scaled = grad * gain_row
            mean_a = jnp.mean(scaled, axis=1, keepdims=True)
            mean_b = jnp.mean(scaled * normed, axis=1, keepdims=True)
            dr1 = (scaled - mean_a - normed * mean_b) * rstd_ref[r, 0:1]
            dr1_ref[r, :] = dr1
            da = dr1.astype(BF16)
            da_ref[r, :] = da
            fold_s[2] += fold_rows(da.astype(F32))
            return carry

        lax.fori_loop(0, rows // LANES, norm, 0)
        vec_ref[...] = jnp.sum(fold_s[...], axis=1)


def ffn_bwd(kind, ids, df, hb, gp, down, up, extra, count):
    rows, width = df.shape
    hidden = up.shape[1]
    outs = [shaped((count, width * hidden // (count * width), width), BF16), shaped((1, hidden), F32)]
    scratch = []
    if kind == 1:
        outs += [shaped((rows, width), F32)]
    else:
        outs += [shaped((rows, width), F32), shaped((rows, width), BF16), shaped((3, width), F32)]
        scratch = [pltpu.VMEM((rows, width), F32), pltpu.VMEM((3, 8, width), F32)]
    return call(
        functools.partial(ffn_bwd_body, kind),
        outs,
        (ids,),
        (df, hb, gp, down, up, *extra),
        scratch,
        flops=6 * rows * width * hidden,
        moved=4 * rows * hidden + 6 * width * hidden + 10 * rows * width,
    )


def attn_bwd_body(
    kind, ids, bucket, lens, keep, qa_ref, k_ref, v_ref, o_ref, da_ref, wo_ref, w_ref, x_ref, bu_ref, va_ref, vf_ref, *rest
):
    if kind == 1:
        dr1_ref, g_ref, dw_ref, ig_ref, bm_s = rest
    else:
        ig_in, dw_ref, ig_ref, bm_s = rest
    rows, width = da_ref.shape
    pairs = k_ref.shape[0]
    local = pairs * LANES
    count = dw_ref.shape[0]
    size, out_size, wide = width // count, local // count, width // local
    _, bm_s[...] = mask_columns(ids, bucket, lens, rows)
    if kind == 1:
        for blk in range(rows // LANES):
            r = slice(blk * LANES, (blk + 1) * LANES)
            far = pl.ds(pl.multiple_of(ids[0] * rows + blk * LANES, LANES), LANES)
            kept = keep_of(ids, bucket, keep, blk)
            ig_ref[r, :] = dr1_ref[r, :] + jnp.where(kept, 0.0, g_ref[far, :].astype(F32))
    else:
        ig_ref[...] = ig_in[...]
    tile = rows // 2

    def pair(p, carry):
        cols = chunk_of(p, LANES)
        kp = k_ref[p]
        vp = v_ref[p]
        bm = bm_s[...]
        low_t, low_r = low_half(tile), low_half(rows)
        zero_t, zero_r = jnp.zeros((tile, LANES), BF16), jnp.zeros((rows, LANES), BF16)
        wo = wo_ref[cols, :]
        dk_sum = dv_sum = None
        dqs = []
        for rb in range(2):
            r = slice(rb * tile, (rb + 1) * tile)
            dop = dot_nt(da_ref[r, :], wo).astype(BF16)
            dq = None
            for par in range(2):
                own_t = low_t if par == 0 else jnp.logical_not(low_t)
                own_r = low_r if par == 0 else jnp.logical_not(low_r)
                qa = qa_ref[2 * p + par, r, :]
                doa = jnp.where(own_t, dop, zero_t)
                prob = jnp.exp(dot_nt(jnp.where(own_r, kp, bm), qa))
                dprob = dot_nt(vp, doa)
                inner = jnp.sum(prob * dprob, axis=0, keepdims=True)
                dscore = (prob * (dprob - inner)).astype(BF16)
                dv = dot_nn(prob.astype(BF16), doa)
                dk = dot_nn(dscore, jnp.where(own_t, qa, zero_t))
                dqp = dot_tn(dscore, jnp.where(own_r, kp, zero_r))
                dv_sum = dv if dv_sum is None else dv_sum + dv
                dk_sum = dk if dk_sum is None else dk_sum + dk
                dq = dqp if dq is None else dq + dqp
            dqs.append((dq * 0.125).astype(BF16))
        dqp = jnp.concatenate(dqs, axis=0)
        dvp = dv_sum.astype(BF16)
        grads = jnp.concatenate([dqp, dk_sum.astype(BF16), dvp], axis=1)
        weights = jnp.concatenate([w_ref[n, :, cols] for n in range(3)], axis=1)
        ig_ref[...] += dot_nt(grads, weights)
        value = dot_tn(x_ref[chunk_of(ids[0], rows), :], grads).astype(BF16)
        heads = jnp.concatenate([o_ref[n] for n in range(pairs)], axis=1)
        da = [da_ref[:, pl.ds(pl.multiple_of(n * local + p * LANES, LANES), LANES)] for n in range(wide)]
        out_value = dot_tn(heads, jnp.concatenate(da, axis=1)).astype(BF16)
        small = [jnp.sum(fold_rows(g.astype(F32)), axis=0, keepdims=True) for g in (dqp, dvp)]
        for ref in (bu_ref, va_ref, vf_ref):
            for n in range(ref.shape[0]):
                for c in range(0, ref.shape[1], local):
                    small.append(ref[n : n + 1, pl.ds(pl.multiple_of(c + p * LANES, LANES), LANES)])
        line = lax.broadcasted_iota(jnp.int32, (8, LANES), 0)
        for a in range(count):
            spot = spot_of(ids, 2, kind, a, count)
            for n in range(3):
                part = value[a * size : (a + 1) * size, n * LANES : (n + 1) * LANES]
                dw_ref[spot, n * size : (n + 1) * size, cols] = part
            for n in range(wide):
                part = out_value[a * out_size : (a + 1) * out_size, n * LANES : (n + 1) * LANES]
                at = 3 * size + n * out_size
                dw_ref[spot, at : at + out_size, cols] = part
            tile_s = jnp.zeros((8, LANES), F32)
            for n, row in enumerate(small[a::count]):
                tile_s = jnp.where(line == n, row, tile_s)
            at = 3 * size + wide * out_size
            dw_ref[spot, at : at + 8, cols] = tile_s.astype(BF16)
        return carry

    lax.fori_loop(0, pairs, pair, 0)


def attn_bwd(kind, scal, qa, k, v, o, da, wo, w, tokens, smalls, extra, count):
    rows, width = da.shape
    pairs = k.shape[0]
    local = pairs * LANES
    lines = 4 * width // count + 8
    return call(
        functools.partial(attn_bwd_body, kind),
        [shaped((count, lines, local), BF16), shaped((rows, width), F32)],
        scal,
        (qa, k, v, o, da, wo, w, tokens, *smalls, *extra),
        [pltpu.VMEM((rows, LANES), BF16)],
        flops=2 * rows * local * (8 * width + 10 * rows),
        moved=2 * (rows * local * 4 + width * local * 7 + rows * width * 2) + 8 * rows * width,
        trans=2 * pairs * rows * rows,
    )


def place_body(batch, first, count, plan, small_plan, ids, *refs):
    pieces = refs[: 1 if small_plan is None else 2]
    refs = refs[len(pieces) + (len(plan) if first else 0) :]
    outs, refs = refs[: len(plan)], refs[len(plan) :]
    n_small = 0 if small_plan is None else len(small_plan)
    small_outs, refs = refs[:n_small], refs[n_small:]
    stages, sems = refs[:-1], refs[-1]
    half = pieces[0].shape[0]
    copies = []
    for q in range(half):
        a = spot_of(ids, batch, 2, first + q, count)
        for n, (parts, target) in enumerate(plan):
            for at, start, size in parts:
                stages[n][(q,) + at] = pieces[0][q, start : start + size, :].astype(F32)
            copy = pltpu.make_async_copy(stages[n].at[q], target(outs[n], a), sems.at[n, q])
            copy.start()
            copies.append(copy)
    for n in range(n_small):
        for line, c0, row in small_plan[n]:
            p = spot_of(ids, batch, 0, row % count, count)
            spot = pieces[0].shape[1] - 8 + row // count
            high = pieces[0][p & (half - 1), pieces[0].shape[1] - 8 :, :].astype(F32)
            low = pieces[1][p & (half - 1), pieces[0].shape[1] - 8 :, :].astype(F32)
            tile = jnp.where(p < half, low, high)
            width = tile.shape[1]
            value = tile[row // count : row // count + 1, :]
            if line is None:
                small_outs[n][c0 : c0 + width] = value.reshape(width)
            else:
                small_outs[n][line : line + 1, c0 : c0 + width] = value
    for copy in copies:
        copy.wait()


def place(batch, first, ids, pieces, outs, plan, stages, held=(), small_outs=(), small_plan=None):
    half = pieces[0].shape[0]
    return call(
        functools.partial(place_body, batch, first, 2 * half, plan, small_plan),
        list(outs) + list(small_outs),
        (ids,),
        (*pieces, *held),
        [pltpu.VMEM((half,) + st, F32) for st in stages] + [pltpu.SemaphoreType.DMA((len(outs), half))],
        moved=6 * half * pieces[0].shape[1] * pieces[0].shape[2],
        in_specs=[resident()] * len(pieces) + [anywhere()] * len(held),
        out_specs=[anywhere()] * len(outs) + [resident()] * len(small_outs),
        input_output_aliases={1 + len(pieces) + n: n for n in range(len(held))},
    )


def join_body(cores, ids, *refs):
    n = (len(refs) - 1) // 3
    owns, others, outs, sems = refs[:n], refs[n : 2 * n], refs[2 * n : 3 * n], refs[-1]
    copies = []
    for k in range(n):
        rows = owns[k].shape[0]
        for part, where in ((owns[k], ids[0]), (others[k], cores - 1 - ids[0])):
            target = outs[k].at[pl.ds(pl.multiple_of(where * rows, rows), rows), :]
            copies.append(pltpu.make_async_copy(part, target, sems.at[len(copies)]))
            copies[-1].start()
    for copy in copies:
        copy.wait()


def join(ids, cores, owns, others):
    return call(
        functools.partial(join_body, cores),
        [shaped((cores * o.shape[0], o.shape[1]), o.dtype) for o in owns],
        (ids,),
        (*owns, *others),
        [pltpu.SemaphoreType.DMA((2 * len(owns),))],
        moved=sum(4 * o.size * o.dtype.itemsize for o in owns),
        out_specs=[anywhere()] * len(owns),
    )


def swap_cores(array_in, cores):
    return lax.ppermute(array_in, "tensor", [(c, cores - 1 - c) for c in range(cores)])


class GroupSum:
    def __init__(self, mesh, batch, own, other_received):
        self.mesh, self.batch = mesh, batch
        self.halvings = own.shape[0].bit_length() - 1
        self.doublings = (mesh.shape["dp"] >> self.halvings).bit_length() - 1
        self.terms = [own, other_received]
        self.at = 0
        self.sent = None

    def exchange(self, array_in, bit_of):
        groups, cores = self.mesh.shape["dp"], self.mesh.shape["tensor"]
        pairs = [(i * cores + c, (i ^ (1 << bit_of(c))) * cores + c) for i in range(groups) for c in range(cores)]
        return lax.ppermute(array_in, ("dp", "tensor"), pairs)

    def total(self, terms):
        acc = terms[0].astype(F32)
        for term in terms[1:]:
            acc = acc + term.astype(F32)
        return acc.astype(BF16)

    def step(self, *earlier):
        bits = STEP_BITS[self.batch]
        terms = self.terms
        if earlier:
            terms = terms[:-1] + [after(terms[-1], *earlier)]
        if self.at < self.halvings:
            order = self.at
            half = terms[0].shape[0] // 2
            self.sent = self.total([term[half:] for term in terms])
            received = self.exchange(self.sent, lambda c: bits[c % 2][order])
            self.terms = [term[:half] for term in terms] + [received]
        elif self.at < self.halvings + self.doublings:
            bit = self.at
            self.sent = self.total(terms)
            self.terms = [self.sent, self.exchange(self.sent, lambda c: bit)]
        else:
            order = 2 * self.halvings + self.doublings - 1 - self.at
            first = order == self.halvings - 1
            self.sent = self.total(terms) if first else jnp.concatenate(terms, axis=0)
            self.terms = [self.sent, self.exchange(self.sent, lambda c: bits[c % 2][order])]
        self.at += 1
        return self.sent


def per_device(
    mesh,
    tokens,
    w_qkv,
    bias_qv,
    w_out,
    bias_out,
    gain_attn,
    shift_attn,
    w_up,
    bias_up,
    w_down,
    bias_down,
    gain_ffn,
    shift_ffn,
    out_grad,
    bucket_len,
    seq_lengths,
    keep_mask,
):
    cores = mesh.shape["tensor"]
    count = min(8, mesh.shape["dp"])
    width = tokens.shape[1]
    rows = tokens.shape[0] // cores
    hidden = w_up.shape[1]
    local = w_qkv.shape[2]
    ids = jnp.where(jnp.arange(2) == 0, lax.axis_index("tensor"), lax.axis_index("dp")).astype(jnp.int32)

    w_qkv_o = swap_cores(w_qkv, cores)
    bias_qv_o = swap_cores(bias_qv, cores)
    w_out_o = swap_cores(w_out, cores)
    bias_up_o = swap_cores(bias_up, cores)
    w_up_o = swap_cores(w_up, cores)
    w_down_o = swap_cores(w_down, cores)

    attn_scal = (ids, bucket_len, seq_lengths)
    qa, k, v, o = attn_fwd(False, attn_scal, tokens, w_qkv, bias_qv, rows)
    qa_o, k_o, v_o, o_o, n1, rstd, hb = attn_fwd(
        True,
        attn_scal,
        tokens,
        w_qkv_o,
        bias_qv_o,
        rows,
        (o, w_out_o, w_out, bias_out, gain_attn, shift_attn),
    )
    keep_scal = (ids, bucket_len, keep_mask)
    vecs = (gain_attn, shift_attn, bias_down, gain_ffn, shift_ffn)
    gb, gb_o, gp, gp_o, mixed, dr2, df, vec_f = ffn_fwd(
        keep_scal, hb, n1, w_up, w_up_o, bias_up, bias_up_o, w_down, w_down_o, vecs, tokens, out_grad
    )
    mixed_o = swap_cores(mixed, cores)
    down_other = down_grad(1, ids, gb_o, df, count)
    down_got = swap_cores(down_other, cores)
    down_own = down_grad(0, ids, gb, after(df, down_other), count)
    sum_down = GroupSum(mesh, 0, down_own, down_got)
    sent = sum_down.step()
    up_other, bu_o, dh = ffn_bwd(1, ids, after(df, sent), hb, gp_o, w_down_o, w_up_o, (dr2,), count)
    up_got = swap_cores(up_other, cores)
    up_own, bu, dr1, da, vec_a = ffn_bwd(0, ids, df, hb, gp, w_down, w_up, (dh, n1, rstd, gain_attn), count)
    sum_up = GroupSum(mesh, 1, up_own, up_got)
    sent = (sum_down.step(da), sum_up.step())
    bwd_scal = (ids, bucket_len, seq_lengths, keep_mask)
    qkv_other, ig_part = attn_bwd(
        1, bwd_scal, qa_o, k_o, v_o, o_o, after(da, *sent), w_out_o, w_qkv_o, tokens,
        (bu_o, vec_a, vec_f), (dr1, out_grad), count,
    )
    qkv_got = swap_cores(qkv_other, cores)
    sent = sum_down.step(ig_part)
    qkv_own, ig = attn_bwd(
        0, bwd_scal, qa, k, v, o, after(da, sent), w_out, w_qkv, tokens, (bu, vec_a, vec_f), (ig_part,), count
    )
    ig_o = swap_cores(ig, cores)
    sum_qkv = GroupSum(mesh, 2, qkv_own, qkv_got)
    steps = 2 * sum_down.halvings + sum_down.doublings
    size = hidden // count
    whole_cols = (slice(None), slice(None))

    def rows_at(size):
        return lambda out, a: out.at[pl.ds(pl.multiple_of(a * size, size), size), :]

    down_outs = [shaped((hidden, width), F32)]
    down_args = ([([(whole_cols, 0, size)], rows_at(size))], [(size, width)])
    size, out_size = width // count, local // count
    lines = hidden // width
    up_outs = [shaped((width, hidden), F32)]
    parts = [((slice(None), slice(n * width, (n + 1) * width)), n * size, size) for n in range(lines)]
    up_args = ([(parts, rows_at(size))], [(size, hidden)])
    qkv_outs = [shaped((3, width, local), F32), shaped((local, width), F32)]
    wide = width // local
    parts = [((slice(None), slice(n * local, (n + 1) * local)), 3 * size + n * out_size, out_size) for n in range(wide)]
    qkv_args = (
        [
            (
                [((n,) + whole_cols, n * size, size) for n in range(3)],
                lambda out, a: out.at[:, pl.ds(pl.multiple_of(a * size, size), size), :],
            ),
            (parts, rows_at(out_size)),
        ],
        [(3, size, local), (out_size, width)],
    )
    earlier = []
    for n in range(steps):
        sum_qkv.step(*earlier)
        earlier = [ig] if n == 0 else []
        for each in (sum_down, sum_up):
            if each.at < steps:
                each.step(*earlier[:1] if n == 0 else ())
                earlier.append(each.terms[-1])
                if each is sum_down and each.at == steps:
                    held = place(0, 0, ids, sum_down.terms[:1], down_outs, *down_args)
        if n == 1:
            out_mixed, out_ig = join(ids, cores, (mixed, ig), (mixed_o, ig_o))
            earlier.append(out_ig)
        if n == steps - 3:
            grad_w_down = place(0, count // 2, ids, sum_down.terms[1:], down_outs, *down_args, held)[0]
        if n == steps - 2:
            earlier.append(grad_w_down)
    held = place(1, 0, ids, sum_up.terms[:1], up_outs, *up_args)
    grad_w_up = place(1, count // 2, ids, sum_up.terms[1:], up_outs, *up_args, held)[0]
    held = place(2, 0, ids, sum_qkv.terms[:1], qkv_outs, *qkv_args)
    per_up, per_norm = hidden // local, width // local
    small_plan = [[(n, 0, n) for n in range(2)], [(None, c * local, 2 + c) for c in range(per_up)]]
    for n in range(6):
        small_plan.append([(None, c * local, 2 + per_up + n * per_norm + c) for c in range(per_norm)])
    small_outs = [shaped((2, local), F32), shaped((hidden,), F32)] + [shaped((width,), F32)] * 6
    grad_w_qkv, grad_w_out, grad_bias_qv, grad_bias_up, *norms = place(
        2, count // 2, ids, [sum_qkv.terms[1], sum_qkv.terms[0]], qkv_outs, *qkv_args, held, small_outs, small_plan
    )
    return (
        out_mixed,
        out_ig,
        grad_w_qkv,
        grad_bias_qv,
        grad_w_out,
        norms[2],
        norms[0],
        norms[1],
        grad_w_up,
        grad_bias_up,
        grad_w_down,
        norms[5],
        norms[3],
        norms[4],
    )


def solution(mesh):
    in_specs = (
        P("dp", None),
        P(None, None, "tensor"),
        P(None, "tensor"),
        P("tensor", None),
        P(),
        P(),
        P(),
        P(None, "tensor"),
        P("tensor"),
        P("tensor", None),
        P(),
        P(),
        P(),
        P("dp", None),
        P("dp"),
        P("dp", None),
        P("dp", None),
    )
    out_specs = (
        P("dp", None),
        P("dp", None),
        P(None, None, "tensor"),
        P(None, "tensor"),
        P("tensor", None),
        P(),
        P(),
        P(),
        P(None, "tensor"),
        P("tensor"),
        P("tensor", None),
        P(),
        P(),
        P(),
    )
    return jax.shard_map(
        functools.partial(per_device, mesh),
        mesh=mesh,
        in_specs=in_specs,
        out_specs=out_specs,
        check_vma=False,
    )
```

```python
import functools

import jax
import jax.numpy as jnp
from jax import lax
from jax.experimental import pallas as pl
from jax.experimental.pallas import tpu as pltpu
from jax.sharding import PartitionSpec as P

HD = 64
BUCKET_LONG = 512
LANES = 128
EPS = 1e-05
F32 = jnp.float32
BF16 = jnp.bfloat16
NEG = -1e30
MIB = 1 << 20
VMEM_MIB = 16
COVER = 20

STEP_BITS = ((((0, 2, 1), (2, 1, 0)), ((1, 2, 0), (2, 0, 1))), (((1, 0, 2), (1, 2, 0)), ((0, 1, 2), (0, 1, 2))), (((0, 1, 2), (1, 2, 0)), ((1, 0, 2), (1, 0, 2))))
EARLY = ((0,), (), (0, 1), (0, 1))
ROUNDS = ((2, 1, 0), (2, 1, 0), (2, 1, 0), (2, 1, 0), (2, 1), (2,), (2,))
JOIN_AT = 1


def dot_nn(left, right):
    return lax.dot_general(left, right, (((1,), (0,)), ((), ())), preferred_element_type=F32)


def dot_nt(left, right):
    return lax.dot_general(left, right, (((1,), (1,)), ((), ())), preferred_element_type=F32)


def dot_tn(left, right):
    return lax.dot_general(left, right, (((0,), (0,)), ((), ())), preferred_element_type=F32)


def resident():
    return pl.BlockSpec(memory_space=pltpu.VMEM)


def anywhere():
    return pl.BlockSpec(memory_space=pl.ANY)


def shaped(shape, dtype):
    return jax.ShapeDtypeStruct(shape, dtype)


def call(body, outs, scalars, operands, scratch=(), vmem=VMEM_MIB, flops=0, moved=0, trans=0, **kwargs):
    specs = kwargs.pop("in_specs", None) or [resident()] * len(operands)
    return pl.pallas_call(
        body,
        out_shape=outs,
        grid_spec=pltpu.PrefetchScalarGridSpec(
            num_scalar_prefetch=len(scalars),
            grid=(1,),
            in_specs=specs,
            out_specs=kwargs.pop("out_specs", None) or [resident()] * len(outs),
            scratch_shapes=list(scratch),
        ),
        compiler_params=pltpu.CompilerParams(dimension_semantics=("arbitrary",), vmem_limit_bytes=vmem * MIB),
        cost_estimate=pl.CostEstimate(flops=COVER * flops, bytes_accessed=moved, transcendentals=trans),
        **kwargs,
    )(*scalars, *operands)


def chunk_of(index, size):
    return pl.ds(pl.multiple_of(index * size, size), size)


def after(value, *earlier):
    return lax.optimization_barrier((value,) + earlier)[0]


def move_bits(number, pairs):
    out = 0
    for take, put in pairs:
        out = out | lax.shift_left(lax.shift_right_logical(number, take) & 1, put)
    return out


def step_bits(batch, core, gathering, steps):
    return [bit for bit in STEP_BITS[batch][core % 2][gathering] if bit < steps]


def spot_of(ids, batch, kind, number, count):
    steps = count.bit_length() - 1
    me = ids[1] & (count - 1)
    number = jnp.int32(number) if isinstance(number, int) else number
    spots = []
    for core in range(2):
        bits = step_bits(batch, 1 - core if kind == 1 else core, kind > 1, steps)
        places = range(steps) if kind > 1 else range(steps - 1, -1, -1)
        if kind == 2:
            spots.append(move_bits(number, zip(places, bits, strict=True)) ^ me)
        else:
            spots.append(move_bits(number ^ me, zip(bits, places, strict=True)))
    return jnp.where((ids[0] & 1) == 0, spots[0], spots[1])


def bucket_shift(bucket_ref):
    return jnp.where(bucket_ref[0] >= BUCKET_LONG, 9, 7)


def mask_columns(ids_ref, bucket_ref, lens_ref, rows):
    shift = bucket_shift(bucket_ref)
    first = ids_ref[0] * lax.shift_right_logical(BUCKET_LONG, shift)
    place = lax.broadcasted_iota(jnp.int32, (rows, LANES), 0)
    lane = lax.broadcasted_iota(jnp.int32, (rows, LANES), 1) & (HD - 1)
    seq = lax.shift_right_logical(place, jnp.full((rows, LANES), shift, jnp.int32))
    pos = place - lax.shift_left(seq, jnp.full((rows, LANES), shift, jnp.int32))
    length = jnp.full((rows, LANES), lens_ref[0, first], jnp.int32)
    for slot in range(1, 4):
        length = jnp.where(seq == slot, lens_ref[0, first + slot], length)
    hit = seq == lane
    query_cols = jnp.where(hit, 1.0, 0.0)
    key_cols = jnp.where(hit & (pos < length), 0.0, NEG)
    key_cols = jnp.where(lane < 4, key_cols, jnp.where(lane < 7, 1.0, 0.0))
    return query_cols.astype(BF16), key_cols.astype(BF16)


def low_half(rows):
    return lax.broadcasted_iota(jnp.int32, (rows, LANES), 1) < HD


def row_of(vec_ref):
    return vec_ref[...].reshape(1, -1)


def attn_fwd_body(last, ids, bucket, lens, x_ref, w_ref, b_ref, *rest):
    if last:
        (other_o, wo_own, wo_other, bias_out, gain, shift_vec) = rest[:6]
        qa_ref, k_ref, v_ref, o_ref, n_ref, rstd_ref, hb_ref = rest[6:13]
    else:
        qa_ref, k_ref, v_ref, o_ref = rest[:4]
    am_s, bm_s = rest[-2:]
    pairs, rows, _ = k_ref.shape
    am_s[...], bm_s[...] = mask_columns(ids, bucket, lens, rows)
    tile = rows // 2

    def pair(p, carry):
        cols = chunk_of(p, LANES)
        weights = jnp.concatenate([w_ref[n, :, cols] for n in range(3)], axis=1)
        qkv = dot_nn(x_ref[chunk_of(ids[0], rows), :], weights)
        qp = ((qkv[:, :LANES] + b_ref[0:1, cols]).astype(BF16).astype(F32) * 0.125).astype(BF16)
        kp = qkv[:, LANES : 2 * LANES].astype(BF16)
        vp = (qkv[:, 2 * LANES :] + b_ref[1:2, cols]).astype(BF16)
        k_ref[p] = kp
        v_ref[p] = vp
        bm = bm_s[...]
        low_r, low_t = low_half(rows), low_half(tile)
        lane = lax.broadcasted_iota(jnp.int32, (tile, LANES), 1) & (HD - 1)
        for rb in range(2):
            r = slice(rb * tile, (rb + 1) * tile)
            am = am_s[r, :]
            qpr = qp[r, :]
            sums = []
            for par in range(2):
                own_t = low_t if par == 0 else jnp.logical_not(low_t)
                own_r = low_r if par == 0 else jnp.logical_not(low_r)
                scores = dot_nt(jnp.where(own_t, qpr, am), jnp.where(own_r, kp, bm))
                top = jnp.max(scores, axis=1, keepdims=True)
                expo = jnp.exp(scores - top).astype(BF16)
                total = dot_nn(expo, jnp.where(own_r, vp, jnp.ones_like(vp)))
                sums.append(total)
                neg_log = -(top + jnp.log(jnp.where(own_t, 1.0, total)))
                hi = neg_log.astype(BF16)
                mid = (neg_log - hi.astype(F32)).astype(BF16)
                lo = (neg_log - hi.astype(F32) - mid.astype(F32)).astype(BF16)
                parts = jnp.where(lane == 4, hi, jnp.where(lane == 5, mid, jnp.where(lane == 6, lo, am)))
                qa_ref[2 * p + par, r, :] = jnp.where(own_t, qpr, parts)
            total = pltpu.roll(jnp.where(low_t, sums[1], sums[0]), HD, 1)
            o_ref[p, r, :] = (jnp.where(low_t, sums[0], sums[1]) / total).astype(BF16)
        return carry

    lax.fori_loop(0, pairs, pair, 0)
    if last:
        block = rows // 4
        gain_row, shift_row, bias_row = row_of(gain), row_of(shift_vec), row_of(bias_out)

        def norm(i, carry):
            r = chunk_of(i, block)
            heads = [o_ref[n, r, :] for n in range(pairs)] + [other_o[n, r, :] for n in range(pairs)]
            weights = jnp.concatenate([wo_own[...], wo_other[...]], axis=0)
            acc = dot_nn(jnp.concatenate(heads, axis=1), weights)
            acc += x_ref[pl.ds(pl.multiple_of(ids[0] * rows + i * block, block), block), :].astype(F32) + bias_row
            centre = acc - jnp.mean(acc, axis=1, keepdims=True)
            rstd = lax.rsqrt(jnp.mean(centre * centre, axis=1, keepdims=True) + EPS)
            normed = centre * rstd
            n_ref[r, :] = normed
            rstd_ref[r, :] = jnp.broadcast_to(rstd, (block, LANES))
            hb_ref[r, :] = (normed * gain_row + shift_row).astype(BF16)
            return carry

        lax.fori_loop(0, 4, norm, 0)


def attn_fwd(last, scal, tokens, w, b, rows, extra=()):
    width = tokens.shape[1]
    local = w.shape[2]
    pairs = local // LANES
    outs = [shaped((2 * pairs, rows, LANES), BF16)] + [shaped((pairs, rows, LANES), BF16)] * 3
    if last:
        outs += [shaped((rows, width), F32), shaped((rows, LANES), F32), shaped((rows, width), BF16)]
    return call(
        functools.partial(attn_fwd_body, last),
        outs,
        scal,
        (tokens, w, b, *extra),
        [pltpu.VMEM((rows, LANES), BF16)] * 2,
        flops=2 * rows * local * (3 * width + 4 * rows + (2 * width if last else 0)),
        moved=2 * (rows * width + 3 * width * local + 5 * rows * local),
        trans=2 * pairs * rows * rows,
    )


def keep_of(ids, bucket, keep, block):
    shift = bucket_shift(bucket)
    first = ids[0] * lax.shift_right_logical(BUCKET_LONG, shift)
    return keep[0, first + lax.shift_right_logical(block * LANES, shift)] > 0


def fold_rows(array_in):
    rows, cols = array_in.shape
    return jnp.sum(array_in.reshape(rows // 8, 8, cols), axis=0)


def ffn_fwd_body(
    ids, bucket, keep, hb_ref, n_ref, up_own, up_other, bu_own, bu_other, down_own, down_other,
    gain_a, shift_a, bias_down, gain_f, shift_f, x_ref, g_ref,
    gb_own, gb_other, gp_own, gp_other, mixed_ref, dr2_ref, df_ref, vec_ref, acc, fold_s,
):
    rows, width = hb_ref.shape
    acc[...] = n_ref[...] * row_of(gain_a) + (row_of(shift_a) + row_of(bias_down))
    half = rows // 2
    chunk = 256

    def hidden(i, carry):
        cols = chunk_of(i, chunk)
        for r in range(2):
            rs = slice(r * half, (r + 1) * half)
            hb = hb_ref[rs, :]
            total = None
            for up, bu, down, gb, gp in (
                (up_own, bu_own, down_own, gb_own, gp_own),
                (up_other, bu_other, down_other, gb_other, gp_other),
            ):
                u = dot_nn(hb, up[:, cols]) + bu[cols].reshape(1, -1)
                cdf = 0.5 * (1.0 + lax.erf(u * 0.7071067811865476))
                pdf = jnp.exp(-0.5 * u * u) * 0.3989422804014327
                gp[rs, cols] = cdf + u * pdf
                act = (u * cdf).astype(BF16)
                gb[rs, cols] = act
                part = dot_nn(act, down[cols, :])
                total = part if total is None else total + part
            acc[rs, :] += total
        return carry

    lax.fori_loop(0, up_own.shape[1] // chunk, hidden, 0)
    fold_s[...] = jnp.zeros_like(fold_s)
    gain_row, shift_row = row_of(gain_f), row_of(shift_f)

    def norm(blk, carry):
        r = chunk_of(blk, LANES)
        far = pl.ds(pl.multiple_of(ids[0] * rows + blk * LANES, LANES), LANES)
        kept = keep_of(ids, bucket, keep, blk)
        res = acc[r, :]
        centre = res - jnp.mean(res, axis=1, keepdims=True)
        rstd = lax.rsqrt(jnp.mean(centre * centre, axis=1, keepdims=True) + EPS)
        normed = centre * rstd
        final = normed * gain_row + shift_row
        mixed_ref[r, :] = jnp.where(kept, final, x_ref[far, :].astype(F32)).astype(BF16)
        grad = jnp.where(kept, g_ref[far, :].astype(F32), 0.0)
        fold_s[0] += fold_rows(grad * normed)
        fold_s[1] += fold_rows(grad)
        scaled = grad * gain_row
        mean_a = jnp.mean(scaled, axis=1, keepdims=True)
        mean_b = jnp.mean(scaled * normed, axis=1, keepdims=True)
        dr2 = (scaled - mean_a - normed * mean_b) * rstd
        dr2_ref[r, :] = dr2
        df = dr2.astype(BF16)
        df_ref[r, :] = df
        fold_s[2] += fold_rows(df.astype(F32))
        return carry

    lax.fori_loop(0, rows // LANES, norm, 0)
    vec_ref[...] = jnp.sum(fold_s[...], axis=1)


def ffn_fwd(scal, hb, n1, up_own, up_other, bu_own, bu_other, down_own, down_other, vecs, tokens, out_grad):
    rows, width = hb.shape
    hidden = up_own.shape[1]
    outs = [
        shaped((rows, hidden), BF16), shaped((rows, hidden), BF16),
        shaped((rows, hidden), F32), shaped((rows, hidden), F32),
        shaped((rows, width), BF16), shaped((rows, width), F32), shaped((rows, width), BF16),
        shaped((3, width), F32),
    ]
    return call(
        ffn_fwd_body,
        outs,
        scal,
        (hb, n1, up_own, up_other, bu_own, bu_other, down_own, down_other, *vecs, tokens, out_grad),
        [pltpu.VMEM((rows, width), F32), pltpu.VMEM((3, 8, width), F32)],
        flops=8 * rows * width * hidden,
        moved=12 * rows * hidden + 8 * width * hidden + 20 * rows * width,
        trans=4 * rows * hidden,
    )


def down_grad_body(kind, ids, gb_ref, df_ref, out_ref):
    count, size, _ = out_ref.shape
    per = 2 if count % 2 == 0 else 1

    def step(i, carry):
        value = dot_tn(gb_ref[:, chunk_of(i, per * size)], df_ref[...]).astype(BF16)
        for c in range(per):
            out_ref[spot_of(ids, 0, kind, i * per + c, count)] = value[c * size : (c + 1) * size, :]
        return carry

    lax.fori_loop(0, count // per, step, 0)


def down_grad(kind, ids, gb, df, count):
    rows, width = df.shape
    hidden = gb.shape[1]
    return call(
        functools.partial(down_grad_body, kind),
        [shaped((count, hidden // count, width), BF16)],
        (ids,),
        (gb, df),
        flops=2 * rows * width * hidden,
        moved=2 * rows * hidden + 2 * width * hidden + 2 * rows * width,
    )[0]


def ffn_bwd_body(kind, ids, df_ref, hb_ref, gp_ref, down_ref, up_ref, *rest):
    if kind == 1:
        dr2_ref, out_ref, bu_ref, acc = rest
        acc[...] = dr2_ref[...]
    else:
        acc_in, n_ref, rstd_ref, gain_a, out_ref, bu_ref, dr1_ref, da_ref, vec_ref, acc, fold_s = rest
        acc[...] = acc_in[...]
    rows, width = df_ref.shape
    count, lines, _ = out_ref.shape
    hidden = up_ref.shape[1]
    up_rows = width // count
    chunk = 384
    per_line = width // chunk

    def step(i, carry):
        cols = chunk_of(i, chunk)
        du = (dot_nt(df_ref[...], down_ref[cols, :]) * gp_ref[:, cols]).astype(BF16)
        bu_ref[:, cols] = jnp.sum(fold_rows(du.astype(F32)), axis=0, keepdims=True)
        value = dot_tn(hb_ref[...], du).astype(BF16)
        line, col = chunk_of(i // per_line, up_rows), chunk_of(i % per_line, chunk)
        for a in range(count):
            out_ref[spot_of(ids, 1, kind, a, count), line, col] = value[a * up_rows : (a + 1) * up_rows, :]
        acc[...] += dot_nt(du, up_ref[:, cols])
        return carry

    lax.fori_loop(0, hidden // chunk, step, 0)
    if kind == 0:
        fold_s[...] = jnp.zeros_like(fold_s)
        gain_row = row_of(gain_a)

        def norm(blk, carry):
            r = chunk_of(blk, LANES)
            grad = acc[r, :]
            normed = n_ref[r, :]
            fold_s[0] += fold_rows(grad * normed)
            fold_s[1] += fold_rows(grad)
            scaled = grad * gain_row
            mean_a = jnp.mean(scaled, axis=1, keepdims=True)
            mean_b = jnp.mean(scaled * normed, axis=1, keepdims=True)
            dr1 = (scaled - mean_a - normed * mean_b) * rstd_ref[r, 0:1]
            dr1_ref[r, :] = dr1
            da = dr1.astype(BF16)
            da_ref[r, :] = da
            fold_s[2] += fold_rows(da.astype(F32))
            return carry

        lax.fori_loop(0, rows // LANES, norm, 0)
        vec_ref[...] = jnp.sum(fold_s[...], axis=1)


def ffn_bwd(kind, ids, df, hb, gp, down, up, extra, count):
    rows, width = df.shape
    hidden = up.shape[1]
    outs = [shaped((count, width * hidden // (count * width), width), BF16), shaped((1, hidden), F32)]
    scratch = []
    if kind == 1:
        outs += [shaped((rows, width), F32)]
    else:
        outs += [shaped((rows, width), F32), shaped((rows, width), BF16), shaped((3, width), F32)]
        scratch = [pltpu.VMEM((rows, width), F32), pltpu.VMEM((3, 8, width), F32)]
    return call(
        functools.partial(ffn_bwd_body, kind),
        outs,
        (ids,),
        (df, hb, gp, down, up, *extra),
        scratch,
        flops=6 * rows * width * hidden,
        moved=4 * rows * hidden + 6 * width * hidden + 10 * rows * width,
    )


def attn_bwd_body(
    kind, ids, bucket, lens, keep, qa_ref, k_ref, v_ref, o_ref, da_ref, wo_ref, w_ref, x_ref, bu_ref, va_ref, vf_ref, *rest
):
    if kind == 1:
        dr1_ref, g_ref, dw_ref, ig_ref, bm_s = rest
    else:
        ig_in, dw_ref, ig_ref, bm_s = rest
    rows, width = da_ref.shape
    pairs = k_ref.shape[0]
    local = pairs * LANES
    count = dw_ref.shape[0]
    size, out_size, wide = width // count, local // count, width // local
    _, bm_s[...] = mask_columns(ids, bucket, lens, rows)
    if kind == 1:
        for blk in range(rows // LANES):
            r = slice(blk * LANES, (blk + 1) * LANES)
            far = pl.ds(pl.multiple_of(ids[0] * rows + blk * LANES, LANES), LANES)
            kept = keep_of(ids, bucket, keep, blk)
            ig_ref[r, :] = dr1_ref[r, :] + jnp.where(kept, 0.0, g_ref[far, :].astype(F32))
    else:
        ig_ref[...] = ig_in[...]
    tile = rows // 2

    def pair(p, carry):
        cols = chunk_of(p, LANES)
        kp = k_ref[p]
        vp = v_ref[p]
        bm = bm_s[...]
        low_t, low_r = low_half(tile), low_half(rows)
        zero_t, zero_r = jnp.zeros((tile, LANES), BF16), jnp.zeros((rows, LANES), BF16)
        wo = wo_ref[cols, :]
        dk_sum = dv_sum = None
        dqs = []
        for rb in range(2):
            r = slice(rb * tile, (rb + 1) * tile)
            dop = dot_nt(da_ref[r, :], wo).astype(BF16)
            dq = None
            for par in range(2):
                own_t = low_t if par == 0 else jnp.logical_not(low_t)
                own_r = low_r if par == 0 else jnp.logical_not(low_r)
                qa = qa_ref[2 * p + par, r, :]
                doa = jnp.where(own_t, dop, zero_t)
                prob = jnp.exp(dot_nt(jnp.where(own_r, kp, bm), qa))
                dprob = dot_nt(vp, doa)
                inner = jnp.sum(prob * dprob, axis=0, keepdims=True)
                dscore = (prob * (dprob - inner)).astype(BF16)
                dv = dot_nn(prob.astype(BF16), doa)
                dk = dot_nn(dscore, jnp.where(own_t, qa, zero_t))
                dqp = dot_tn(dscore, jnp.where(own_r, kp, zero_r))
                dv_sum = dv if dv_sum is None else dv_sum + dv
                dk_sum = dk if dk_sum is None else dk_sum + dk
                dq = dqp if dq is None else dq + dqp
            dqs.append((dq * 0.125).astype(BF16))
        dqp = jnp.concatenate(dqs, axis=0)
        dvp = dv_sum.astype(BF16)
        grads = jnp.concatenate([dqp, dk_sum.astype(BF16), dvp], axis=1)
        weights = jnp.concatenate([w_ref[n, :, cols] for n in range(3)], axis=1)
        ig_ref[...] += dot_nt(grads, weights)
        value = dot_tn(x_ref[chunk_of(ids[0], rows), :], grads).astype(BF16)
        heads = jnp.concatenate([o_ref[n] for n in range(pairs)], axis=1)
        da = [da_ref[:, pl.ds(pl.multiple_of(n * local + p * LANES, LANES), LANES)] for n in range(wide)]
        out_value = dot_tn(heads, jnp.concatenate(da, axis=1)).astype(BF16)
        small = [jnp.sum(fold_rows(g.astype(F32)), axis=0, keepdims=True) for g in (dqp, dvp)]
        for ref in (bu_ref, va_ref, vf_ref):
            for n in range(ref.shape[0]):
                for c in range(0, ref.shape[1], local):
                    small.append(ref[n : n + 1, pl.ds(pl.multiple_of(c + p * LANES, LANES), LANES)])
        line = lax.broadcasted_iota(jnp.int32, (8, LANES), 0)
        for a in range(count):
            spot = spot_of(ids, 2, kind, a, count)
            for n in range(3):
                part = value[a * size : (a + 1) * size, n * LANES : (n + 1) * LANES]
                dw_ref[spot, n * size : (n + 1) * size, cols] = part
            for n in range(wide):
                part = out_value[a * out_size : (a + 1) * out_size, n * LANES : (n + 1) * LANES]
                at = 3 * size + n * out_size
                dw_ref[spot, at : at + out_size, cols] = part
            tile_s = jnp.zeros((8, LANES), F32)
            for n, row in enumerate(small[a::count]):
                tile_s = jnp.where(line == n, row, tile_s)
            at = 3 * size + wide * out_size
            dw_ref[spot, at : at + 8, cols] = tile_s.astype(BF16)
        return carry

    lax.fori_loop(0, pairs, pair, 0)


def attn_bwd(kind, scal, qa, k, v, o, da, wo, w, tokens, smalls, extra, count):
    rows, width = da.shape
    pairs = k.shape[0]
    local = pairs * LANES
    lines = 4 * width // count + 8
    return call(
        functools.partial(attn_bwd_body, kind),
        [shaped((count, lines, local), BF16), shaped((rows, width), F32)],
        scal,
        (qa, k, v, o, da, wo, w, tokens, *smalls, *extra),
        [pltpu.VMEM((rows, LANES), BF16)],
        flops=2 * rows * local * (8 * width + 10 * rows),
        moved=2 * (rows * local * 4 + width * local * 7 + rows * width * 2) + 8 * rows * width,
        trans=2 * pairs * rows * rows,
    )


def place_body(batch, first, count, plan, small_plan, ids, *refs):
    pieces = refs[: 1 if small_plan is None else 2]
    refs = refs[len(pieces) + (len(plan) if first else 0) :]
    outs, refs = refs[: len(plan)], refs[len(plan) :]
    n_small = 0 if small_plan is None else len(small_plan)
    small_outs, refs = refs[:n_small], refs[n_small:]
    stages, sems = refs[:-1], refs[-1]
    half = pieces[0].shape[0]
    copies = []
    for q in range(half):
        a = spot_of(ids, batch, 2, first + q, count)
        for n, (parts, target) in enumerate(plan):
            for at, start, size in parts:
                stages[n][(q,) + at] = pieces[0][q, start : start + size, :].astype(F32)
            copy = pltpu.make_async_copy(stages[n].at[q], target(outs[n], a), sems.at[n, q])
            copy.start()
            copies.append(copy)
    for n in range(n_small):
        for line, c0, row in small_plan[n]:
            p = spot_of(ids, batch, 3, row % count, count)
            spot = pieces[0].shape[1] - 8 + row // count
            high = pieces[0][p & (half - 1), pieces[0].shape[1] - 8 :, :].astype(F32)
            low = pieces[1][p & (half - 1), pieces[0].shape[1] - 8 :, :].astype(F32)
            tile = jnp.where(p < half, low, high)
            width = tile.shape[1]
            value = tile[row // count : row // count + 1, :]
            if line is None:
                small_outs[n][c0 : c0 + width] = value.reshape(width)
            else:
                small_outs[n][line : line + 1, c0 : c0 + width] = value
    for copy in copies:
        copy.wait()


def place(batch, first, ids, pieces, outs, plan, stages, held=(), small_outs=(), small_plan=None):
    half = pieces[0].shape[0]
    return call(
        functools.partial(place_body, batch, first, 2 * half, plan, small_plan),
        list(outs) + list(small_outs),
        (ids,),
        (*pieces, *held),
        [pltpu.VMEM((half,) + st, F32) for st in stages] + [pltpu.SemaphoreType.DMA((len(outs), half))],
        moved=6 * half * pieces[0].shape[1] * pieces[0].shape[2],
        in_specs=[resident()] * len(pieces) + [anywhere()] * len(held),
        out_specs=[anywhere()] * len(outs) + [resident()] * len(small_outs),
        input_output_aliases={1 + len(pieces) + n: n for n in range(len(held))},
    )


def join_body(cores, ids, *refs):
    n = (len(refs) - 1) // 3
    owns, others, outs, sems = refs[:n], refs[n : 2 * n], refs[2 * n : 3 * n], refs[-1]
    copies = []
    for k in range(n):
        rows = owns[k].shape[0]
        for part, where in ((owns[k], ids[0]), (others[k], cores - 1 - ids[0])):
            target = outs[k].at[pl.ds(pl.multiple_of(where * rows, rows), rows), :]
            copies.append(pltpu.make_async_copy(part, target, sems.at[len(copies)]))
            copies[-1].start()
    for copy in copies:
        copy.wait()


def join(ids, cores, owns, others):
    return call(
        functools.partial(join_body, cores),
        [shaped((cores * o.shape[0], o.shape[1]), o.dtype) for o in owns],
        (ids,),
        (*owns, *others),
        [pltpu.SemaphoreType.DMA((2 * len(owns),))],
        moved=sum(4 * o.size * o.dtype.itemsize for o in owns),
        out_specs=[anywhere()] * len(owns),
    )


def swap_cores(array_in, cores):
    return lax.ppermute(array_in, "tensor", [(c, cores - 1 - c) for c in range(cores)])


class GroupSum:
    def __init__(self, mesh, batch, own, other_received):
        self.mesh, self.batch = mesh, batch
        self.halvings = own.shape[0].bit_length() - 1
        self.steps = 2 * self.halvings + 1
        self.terms = [own, other_received]
        self.at = 0
        self.sent = None

    def exchange(self, array_in, bit_of):
        groups, cores = self.mesh.shape["dp"], self.mesh.shape["tensor"]
        pairs = [(i * cores + c, (i ^ (1 << bit_of(c))) * cores + c) for i in range(groups) for c in range(cores)]
        return lax.ppermute(array_in, ("dp", "tensor"), pairs)

    def total(self, terms):
        acc = terms[0].astype(F32)
        for term in terms[1:]:
            acc = acc + term.astype(F32)
        return acc.astype(BF16)

    def step(self, *earlier):
        terms = self.terms
        if earlier:
            terms = terms[:-1] + [after(terms[-1], *earlier)]
        n = self.at
        if n < self.halvings:
            half = terms[0].shape[0] // 2
            self.sent = self.total([term[half:] for term in terms])
            received = self.exchange(self.sent, lambda c: step_bits(self.batch, c, 0, self.halvings)[n])
            self.terms = [term[:half] for term in terms] + [received]
        elif n == self.halvings:
            doublings = (self.mesh.shape["dp"] >> self.halvings).bit_length() - 1
            for k in range(doublings):
                self.sent = self.total(terms)
                terms = [self.sent, self.exchange(self.sent, lambda c, k=k: self.halvings + k)]
            self.terms = terms
        else:
            n -= self.halvings + 1
            self.sent = self.total(terms) if n == 0 else jnp.concatenate(terms, axis=0)
            received = self.exchange(self.sent, lambda c: step_bits(self.batch, c, 1, self.halvings)[n])
            self.terms = [self.sent, received]
        self.at += 1
        return self.sent


def per_device(
    mesh,
    tokens,
    w_qkv,
    bias_qv,
    w_out,
    bias_out,
    gain_attn,
    shift_attn,
    w_up,
    bias_up,
    w_down,
    bias_down,
    gain_ffn,
    shift_ffn,
    out_grad,
    bucket_len,
    seq_lengths,
    keep_mask,
):
    cores = mesh.shape["tensor"]
    count = min(8, mesh.shape["dp"])
    width = tokens.shape[1]
    rows = tokens.shape[0] // cores
    hidden = w_up.shape[1]
    local = w_qkv.shape[2]
    ids = jnp.where(jnp.arange(2) == 0, lax.axis_index("tensor"), lax.axis_index("dp")).astype(jnp.int32)

    w_qkv_o = swap_cores(w_qkv, cores)
    bias_qv_o = swap_cores(bias_qv, cores)
    w_out_o = swap_cores(w_out, cores)
    bias_up_o = swap_cores(bias_up, cores)
    w_up_o = swap_cores(w_up, cores)
    w_down_o = swap_cores(w_down, cores)

    attn_scal = (ids, bucket_len, seq_lengths)
    qa, k, v, o = attn_fwd(False, attn_scal, tokens, w_qkv, bias_qv, rows)
    qa_o, k_o, v_o, o_o, n1, rstd, hb = attn_fwd(
        True,
        attn_scal,
        tokens,
        w_qkv_o,
        bias_qv_o,
        rows,
        (o, w_out_o, w_out, bias_out, gain_attn, shift_attn),
    )
    keep_scal = (ids, bucket_len, keep_mask)
    vecs = (gain_attn, shift_attn, bias_down, gain_ffn, shift_ffn)
    gb, gb_o, gp, gp_o, mixed, dr2, df, vec_f = ffn_fwd(
        keep_scal, hb, n1, w_up, w_up_o, bias_up, bias_up_o, w_down, w_down_o, vecs, tokens, out_grad
    )
    mixed_o = swap_cores(mixed, cores)
    down_other = down_grad(1, ids, gb_o, df, count)
    down_got = swap_cores(down_other, cores)
    down_own = down_grad(0, ids, gb, after(df, down_other), count)
    sums = [GroupSum(mesh, 0, down_own, down_got)]

    landed = []

    def exchange_all(batches, *earlier):
        earlier += tuple(landed)
        landed.clear()
        sents = [sums[batch].step(*earlier) for batch in batches]
        landed.extend(sums[batch].terms[-1] for batch in batches)
        return sents

    sent = exchange_all(EARLY[0])
    up_other, bu_o, dh = ffn_bwd(1, ids, after(df, *sent), hb, gp_o, w_down_o, w_up_o, (dr2,), count)
    up_got = swap_cores(up_other, cores)
    sent = exchange_all(EARLY[1], dh) if EARLY[1] else []
    up_own, bu, dr1, da, vec_a = ffn_bwd(
        0, ids, after(df, *sent), hb, gp, w_down, w_up, (dh, n1, rstd, gain_attn), count
    )
    sums.append(GroupSum(mesh, 1, up_own, up_got))
    sent = exchange_all(EARLY[2], da)
    bwd_scal = (ids, bucket_len, seq_lengths, keep_mask)
    qkv_other, ig_part = attn_bwd(
        1, bwd_scal, qa_o, k_o, v_o, o_o, after(da, *sent), w_out_o, w_qkv_o, tokens,
        (bu_o, vec_a, vec_f), (dr1, out_grad), count,
    )
    qkv_got = swap_cores(qkv_other, cores)
    sent = exchange_all(EARLY[3], ig_part, mixed_o)
    qkv_own, ig = attn_bwd(
        0, bwd_scal, qa, k, v, o, after(da, *sent), w_out, w_qkv, tokens, (bu, vec_a, vec_f), (ig_part,), count
    )
    ig_o = swap_cores(ig, cores)
    sums.append(GroupSum(mesh, 2, qkv_own, qkv_got))
    size = hidden // count
    whole_cols = (slice(None), slice(None))

    def rows_at(size):
        return lambda out, a: out.at[pl.ds(pl.multiple_of(a * size, size), size), :]

    down_outs = [shaped((hidden, width), F32)]
    down_args = ([([(whole_cols, 0, size)], rows_at(size))], [(size, width)])
    size, out_size = width // count, local // count
    lines = hidden // width
    up_outs = [shaped((width, hidden), F32)]
    parts = [((slice(None), slice(n * width, (n + 1) * width)), n * size, size) for n in range(lines)]
    up_args = ([(parts, rows_at(size))], [(size, hidden)])
    qkv_outs = [shaped((3, width, local), F32), shaped((local, width), F32)]
    wide = width // local
    parts = [((slice(None), slice(n * local, (n + 1) * local)), 3 * size + n * out_size, out_size) for n in range(wide)]
    qkv_args = (
        [
            (
                [((n,) + whole_cols, n * size, size) for n in range(3)],
                lambda out, a: out.at[:, pl.ds(pl.multiple_of(a * size, size), size), :],
            ),
            (parts, rows_at(out_size)),
        ],
        [(3, size, local), (out_size, width)],
    )
    per_up, per_norm = hidden // local, width // local
    small_plan = [[(n, 0, n) for n in range(2)], [(None, c * local, 2 + c) for c in range(per_up)]]
    for n in range(6):
        small_plan.append([(None, c * local, 2 + per_up + n * per_norm + c) for c in range(per_norm)])
    small_outs = [shaped((2, local), F32), shaped((hidden,), F32)] + [shaped((width,), F32)] * 6
    plans = ((down_outs, *down_args), (up_outs, *up_args), (qkv_outs, *qkv_args))
    held, placed = {}, {}
    fillers = [ig]
    for number, batches in enumerate(ROUNDS):
        ready = tuple(landed) + tuple(fillers)
        later = []
        if number == JOIN_AT:
            out_mixed, out_ig = join(ids, cores, (mixed, after(ig, *ready)), (mixed_o, ig_o))
            later.append(out_ig)
        for batch in (0, 1):
            each = sums[batch]
            if each.at == each.steps and batch not in placed:
                pieces = [after(each.terms[1], *ready)]
                placed[batch] = place(batch, count // 2, ids, pieces, *plans[batch], held[batch])
                later.append(placed[batch][0])
        exchange_all([batch for batch in batches if sums[batch].at < sums[batch].steps], *fillers)
        fillers = later
        for batch, each in enumerate(sums):
            if each.at == each.steps and batch not in held:
                held[batch] = place(batch, 0, ids, each.terms[:1], *plans[batch])
    for batch in range(3):
        if batch not in placed:
            pieces = [sums[batch].terms[1]]
            if batch < 2:
                placed[batch] = place(batch, count // 2, ids, pieces, *plans[batch], held[batch])
            else:
                pieces += sums[2].terms[:1]
                placed[2] = place(2, count // 2, ids, pieces, *plans[2], held[2], small_outs, small_plan)
    grad_w_down, grad_w_up = placed[0][0], placed[1][0]
    grad_w_qkv, grad_w_out, grad_bias_qv, grad_bias_up, *norms = placed[2]
    return (
        out_mixed,
        out_ig,
        grad_w_qkv,
        grad_bias_qv,
        grad_w_out,
        norms[2],
        norms[0],
        norms[1],
        grad_w_up,
        grad_bias_up,
        grad_w_down,
        norms[5],
        norms[3],
        norms[4],
    )


def solution(mesh):
    in_specs = (
        P("dp", None),
        P(None, None, "tensor"),
        P(None, "tensor"),
        P("tensor", None),
        P(),
        P(),
        P(),
        P(None, "tensor"),
        P("tensor"),
        P("tensor", None),
        P(),
        P(),
        P(),
        P("dp", None),
        P("dp"),
        P("dp", None),
        P("dp", None),
    )
    out_specs = (
        P("dp", None),
        P("dp", None),
        P(None, None, "tensor"),
        P(None, "tensor"),
        P("tensor", None),
        P(),
        P(),
        P(),
        P(None, "tensor"),
        P("tensor"),
        P("tensor", None),
        P(),
        P(),
        P(),
    )
    return jax.shard_map(
        functools.partial(per_device, mesh),
        mesh=mesh,
        in_specs=in_specs,
        out_specs=out_specs,
        check_vma=False,
    )
```

```python
import functools

import jax
import jax.numpy as jnp
from jax import lax
from jax.experimental import pallas as pl
from jax.experimental.pallas import tpu as pltpu
from jax.sharding import PartitionSpec as P

HD = 64
BUCKET_LONG = 512
LANES = 128
EPS = 1e-05
F32 = jnp.float32
BF16 = jnp.bfloat16
NEG = -1e30
MIB = 1 << 20
VMEM_MIB = 16
COVER = 20

STEP_BITS = ((((1, 0, 2), (2, 1, 0)), ((0, 1, 2), (2, 0, 1))), (((1, 2, 0), (2, 1, 0)), ((0, 2, 1), (2, 0, 1))), (((0, 1, 2), (2, 0, 1)), ((1, 0, 2), (1, 0, 2))), (((0, 1, 2), (0, 2, 1)), ((1, 0, 2), (2, 1, 0))), (((0, 1, 2), (2, 0, 1)), ((1, 0, 2), (0, 1, 2))), (((0, 1, 2), (0, 1, 2)), ((1, 0, 2), (2, 0, 1))))
PARTS = 2
EARLY = (((0,), (1,)), ((0,),), ((0, 2), (1, 3)), ((0, 2), (1, 3)))
TURNS = ((4, 2, 0), (5, 3, 1)) * 7
JOIN_AT = 3


def dot_nn(left, right):
    return lax.dot_general(left, right, (((1,), (0,)), ((), ())), preferred_element_type=F32)


def dot_nt(left, right):
    return lax.dot_general(left, right, (((1,), (1,)), ((), ())), preferred_element_type=F32)


def dot_tn(left, right):
    return lax.dot_general(left, right, (((0,), (0,)), ((), ())), preferred_element_type=F32)


def resident():
    return pl.BlockSpec(memory_space=pltpu.VMEM)


def anywhere():
    return pl.BlockSpec(memory_space=pl.ANY)


def shaped(shape, dtype):
    return jax.ShapeDtypeStruct(shape, dtype)


def call(body, outs, scalars, operands, scratch=(), vmem=VMEM_MIB, flops=0, moved=0, trans=0, **kwargs):
    specs = kwargs.pop("in_specs", None) or [resident()] * len(operands)
    return pl.pallas_call(
        body,
        out_shape=outs,
        grid_spec=pltpu.PrefetchScalarGridSpec(
            num_scalar_prefetch=len(scalars),
            grid=(1,),
            in_specs=specs,
            out_specs=kwargs.pop("out_specs", None) or [resident()] * len(outs),
            scratch_shapes=list(scratch),
        ),
        compiler_params=pltpu.CompilerParams(dimension_semantics=("arbitrary",), vmem_limit_bytes=vmem * MIB),
        cost_estimate=pl.CostEstimate(flops=COVER * flops, bytes_accessed=moved, transcendentals=trans),
        **kwargs,
    )(*scalars, *operands)


def chunk_of(index, size):
    return pl.ds(pl.multiple_of(index * size, size), size)


def after(value, *earlier):
    return lax.optimization_barrier((value,) + earlier)[0]


def move_bits(number, pairs):
    out = 0
    for take, put in pairs:
        out = out | lax.shift_left(lax.shift_right_logical(number, take) & 1, put)
    return out


def step_bits(batch, core, gathering, steps):
    return [bit for bit in STEP_BITS[batch][core % 2][gathering] if bit < steps]


def spot_of(ids, batch, kind, number, count):
    steps = count.bit_length() - 1
    me = ids[1] & (count - 1)
    number = jnp.int32(number) if isinstance(number, int) else number
    spots = []
    for core in range(2):
        bits = step_bits(batch, 1 - core if kind == 1 else core, kind > 1, steps)
        places = range(steps) if kind > 1 else range(steps - 1, -1, -1)
        if kind == 2:
            spots.append(move_bits(number, zip(places, bits, strict=True)) ^ me)
        else:
            spots.append(move_bits(number ^ me, zip(bits, places, strict=True)))
    return jnp.where((ids[0] & 1) == 0, spots[0], spots[1])


def bucket_shift(bucket_ref):
    return jnp.where(bucket_ref[0] >= BUCKET_LONG, 9, 7)


def mask_columns(ids_ref, bucket_ref, lens_ref, rows):
    shift = bucket_shift(bucket_ref)
    first = ids_ref[0] * lax.shift_right_logical(BUCKET_LONG, shift)
    place = lax.broadcasted_iota(jnp.int32, (rows, LANES), 0)
    lane = lax.broadcasted_iota(jnp.int32, (rows, LANES), 1) & (HD - 1)
    seq = lax.shift_right_logical(place, jnp.full((rows, LANES), shift, jnp.int32))
    pos = place - lax.shift_left(seq, jnp.full((rows, LANES), shift, jnp.int32))
    length = jnp.full((rows, LANES), lens_ref[0, first], jnp.int32)
    for slot in range(1, 4):
        length = jnp.where(seq == slot, lens_ref[0, first + slot], length)
    hit = seq == lane
    query_cols = jnp.where(hit, 1.0, 0.0)
    key_cols = jnp.where(hit & (pos < length), 0.0, NEG)
    key_cols = jnp.where(lane < 4, key_cols, jnp.where(lane < 7, 1.0, 0.0))
    return query_cols.astype(BF16), key_cols.astype(BF16)


def low_half(rows):
    return lax.broadcasted_iota(jnp.int32, (rows, LANES), 1) < HD


def row_of(vec_ref):
    return vec_ref[...].reshape(1, -1)


def attn_fwd_body(last, ids, bucket, lens, x_ref, w_ref, b_ref, *rest):
    if last:
        (other_o, wo_own, wo_other, bias_out, gain, shift_vec) = rest[:6]
        qa_ref, k_ref, v_ref, o_ref, n_ref, rstd_ref, hb_ref = rest[6:13]
    else:
        qa_ref, k_ref, v_ref, o_ref = rest[:4]
    am_s, bm_s = rest[-2:]
    pairs, rows, _ = k_ref.shape
    am_s[...], bm_s[...] = mask_columns(ids, bucket, lens, rows)
    tile = rows // 2

    def pair(p, carry):
        cols = chunk_of(p, LANES)
        weights = jnp.concatenate([w_ref[n, :, cols] for n in range(3)], axis=1)
        qkv = dot_nn(x_ref[chunk_of(ids[0], rows), :], weights)
        qp = ((qkv[:, :LANES] + b_ref[0:1, cols]).astype(BF16).astype(F32) * 0.125).astype(BF16)
        kp = qkv[:, LANES : 2 * LANES].astype(BF16)
        vp = (qkv[:, 2 * LANES :] + b_ref[1:2, cols]).astype(BF16)
        k_ref[p] = kp
        v_ref[p] = vp
        bm = bm_s[...]
        low_r, low_t = low_half(rows), low_half(tile)
        lane = lax.broadcasted_iota(jnp.int32, (tile, LANES), 1) & (HD - 1)
        for rb in range(2):
            r = slice(rb * tile, (rb + 1) * tile)
            am = am_s[r, :]
            qpr = qp[r, :]
            sums = []
            for par in range(2):
                own_t = low_t if par == 0 else jnp.logical_not(low_t)
                own_r = low_r if par == 0 else jnp.logical_not(low_r)
                scores = dot_nt(jnp.where(own_t, qpr, am), jnp.where(own_r, kp, bm))
                top = jnp.max(scores, axis=1, keepdims=True)
                expo = jnp.exp(scores - top).astype(BF16)
                total = dot_nn(expo, jnp.where(own_r, vp, jnp.ones_like(vp)))
                sums.append(total)
                neg_log = -(top + jnp.log(jnp.where(own_t, 1.0, total)))
                hi = neg_log.astype(BF16)
                mid = (neg_log - hi.astype(F32)).astype(BF16)
                lo = (neg_log - hi.astype(F32) - mid.astype(F32)).astype(BF16)
                parts = jnp.where(lane == 4, hi, jnp.where(lane == 5, mid, jnp.where(lane == 6, lo, am)))
                qa_ref[2 * p + par, r, :] = jnp.where(own_t, qpr, parts)
            total = pltpu.roll(jnp.where(low_t, sums[1], sums[0]), HD, 1)
            o_ref[p, r, :] = (jnp.where(low_t, sums[0], sums[1]) / total).astype(BF16)
        return carry

    lax.fori_loop(0, pairs, pair, 0)
    if last:
        block = rows // 4
        gain_row, shift_row, bias_row = row_of(gain), row_of(shift_vec), row_of(bias_out)

        def norm(i, carry):
            r = chunk_of(i, block)
            heads = [o_ref[n, r, :] for n in range(pairs)] + [other_o[n, r, :] for n in range(pairs)]
            weights = jnp.concatenate([wo_own[...], wo_other[...]], axis=0)
            acc = dot_nn(jnp.concatenate(heads, axis=1), weights)
            acc += x_ref[pl.ds(pl.multiple_of(ids[0] * rows + i * block, block), block), :].astype(F32) + bias_row
            centre = acc - jnp.mean(acc, axis=1, keepdims=True)
            rstd = lax.rsqrt(jnp.mean(centre * centre, axis=1, keepdims=True) + EPS)
            normed = centre * rstd
            n_ref[r, :] = normed
            rstd_ref[r, :] = jnp.broadcast_to(rstd, (block, LANES))
            hb_ref[r, :] = (normed * gain_row + shift_row).astype(BF16)
            return carry

        lax.fori_loop(0, 4, norm, 0)


def attn_fwd(last, scal, tokens, w, b, rows, extra=()):
    width = tokens.shape[1]
    local = w.shape[2]
    pairs = local // LANES
    outs = [shaped((2 * pairs, rows, LANES), BF16)] + [shaped((pairs, rows, LANES), BF16)] * 3
    if last:
        outs += [shaped((rows, width), F32), shaped((rows, LANES), F32), shaped((rows, width), BF16)]
    return call(
        functools.partial(attn_fwd_body, last),
        outs,
        scal,
        (tokens, w, b, *extra),
        [pltpu.VMEM((rows, LANES), BF16)] * 2,
        flops=2 * rows * local * (3 * width + 4 * rows + (2 * width if last else 0)),
        moved=2 * (rows * width + 3 * width * local + 5 * rows * local),
        trans=2 * pairs * rows * rows,
    )


def keep_of(ids, bucket, keep, block):
    shift = bucket_shift(bucket)
    first = ids[0] * lax.shift_right_logical(BUCKET_LONG, shift)
    return keep[0, first + lax.shift_right_logical(block * LANES, shift)] > 0


def fold_rows(array_in):
    rows, cols = array_in.shape
    return jnp.sum(array_in.reshape(rows // 8, 8, cols), axis=0)


def ffn_fwd_body(
    ids, bucket, keep, hb_ref, n_ref, up_own, up_other, bu_own, bu_other, down_own, down_other,
    gain_a, shift_a, bias_down, gain_f, shift_f, x_ref, g_ref,
    gb_own, gb_other, gp_own, gp_other, mixed_ref, dr2_ref, df_ref, vec_ref, acc, fold_s,
):
    rows, width = hb_ref.shape
    acc[...] = n_ref[...] * row_of(gain_a) + (row_of(shift_a) + row_of(bias_down))
    half = rows // 2
    chunk = 256

    def hidden(i, carry):
        cols = chunk_of(i, chunk)
        for r in range(2):
            rs = slice(r * half, (r + 1) * half)
            hb = hb_ref[rs, :]
            total = None
            for up, bu, down, gb, gp in (
                (up_own, bu_own, down_own, gb_own, gp_own),
                (up_other, bu_other, down_other, gb_other, gp_other),
            ):
                u = dot_nn(hb, up[:, cols]) + bu[cols].reshape(1, -1)
                cdf = 0.5 * (1.0 + lax.erf(u * 0.7071067811865476))
                pdf = jnp.exp(-0.5 * u * u) * 0.3989422804014327
                gp[rs, cols] = cdf + u * pdf
                act = (u * cdf).astype(BF16)
                gb[rs, cols] = act
                part = dot_nn(act, down[cols, :])
                total = part if total is None else total + part
            acc[rs, :] += total
        return carry

    lax.fori_loop(0, up_own.shape[1] // chunk, hidden, 0)
    fold_s[...] = jnp.zeros_like(fold_s)
    gain_row, shift_row = row_of(gain_f), row_of(shift_f)

    def norm(blk, carry):
        r = chunk_of(blk, LANES)
        far = pl.ds(pl.multiple_of(ids[0] * rows + blk * LANES, LANES), LANES)
        kept = keep_of(ids, bucket, keep, blk)
        res = acc[r, :]
        centre = res - jnp.mean(res, axis=1, keepdims=True)
        rstd = lax.rsqrt(jnp.mean(centre * centre, axis=1, keepdims=True) + EPS)
        normed = centre * rstd
        final = normed * gain_row + shift_row
        mixed_ref[r, :] = jnp.where(kept, final, x_ref[far, :].astype(F32)).astype(BF16)
        grad = jnp.where(kept, g_ref[far, :].astype(F32), 0.0)
        fold_s[0] += fold_rows(grad * normed)
        fold_s[1] += fold_rows(grad)
        scaled = grad * gain_row
        mean_a = jnp.mean(scaled, axis=1, keepdims=True)
        mean_b = jnp.mean(scaled * normed, axis=1, keepdims=True)
        dr2 = (scaled - mean_a - normed * mean_b) * rstd
        dr2_ref[r, :] = dr2
        df = dr2.astype(BF16)
        df_ref[r, :] = df
        fold_s[2] += fold_rows(df.astype(F32))
        return carry

    lax.fori_loop(0, rows // LANES, norm, 0)
    vec_ref[...] = jnp.sum(fold_s[...], axis=1)


def ffn_fwd(scal, hb, n1, up_own, up_other, bu_own, bu_other, down_own, down_other, vecs, tokens, out_grad):
    rows, width = hb.shape
    hidden = up_own.shape[1]
    outs = [
        shaped((rows, hidden), BF16), shaped((rows, hidden), BF16),
        shaped((rows, hidden), F32), shaped((rows, hidden), F32),
        shaped((rows, width), BF16), shaped((rows, width), F32), shaped((rows, width), BF16),
        shaped((3, width), F32),
    ]
    return call(
        ffn_fwd_body,
        outs,
        scal,
        (hb, n1, up_own, up_other, bu_own, bu_other, down_own, down_other, *vecs, tokens, out_grad),
        [pltpu.VMEM((rows, width), F32), pltpu.VMEM((3, 8, width), F32)],
        flops=8 * rows * width * hidden,
        moved=12 * rows * hidden + 8 * width * hidden + 20 * rows * width,
        trans=4 * rows * hidden,
    )


def down_grad_body(kind, ids, gb_ref, df_ref, out_ref):
    _, count, size, _ = out_ref.shape
    per = 2 if count % 2 == 0 else 1

    def step(i, carry):
        value = dot_tn(gb_ref[:, chunk_of(i, per * PARTS * size)], df_ref[...]).astype(BF16)
        for c in range(per):
            for part in range(PARTS):
                first = (c * PARTS + part) * size
                out_ref[part, spot_of(ids, part, kind, i * per + c, count)] = value[first : first + size, :]
        return carry

    lax.fori_loop(0, count // per, step, 0)


def down_grad(kind, ids, gb, df, count):
    rows, width = df.shape
    hidden = gb.shape[1]
    return call(
        functools.partial(down_grad_body, kind),
        [shaped((PARTS, count, hidden // (count * PARTS), width), BF16)],
        (ids,),
        (gb, df),
        flops=2 * rows * width * hidden,
        moved=2 * rows * hidden + 2 * width * hidden + 2 * rows * width,
    )[0]


def ffn_bwd_body(kind, ids, df_ref, hb_ref, gp_ref, down_ref, up_ref, *rest):
    if kind == 1:
        dr2_ref, out_ref, bu_ref, acc = rest
        acc[...] = dr2_ref[...]
    else:
        acc_in, n_ref, rstd_ref, gain_a, out_ref, bu_ref, dr1_ref, da_ref, vec_ref, acc, fold_s = rest
        acc[...] = acc_in[...]
    rows, width = df_ref.shape
    _, count, _, _ = out_ref.shape
    hidden = up_ref.shape[1]
    up_rows = width // count
    chunk = 384
    per_line = width // chunk

    def step(i, carry):
        cols = chunk_of(i, chunk)
        du = (dot_nt(df_ref[...], down_ref[cols, :]) * gp_ref[:, cols]).astype(BF16)
        bu_ref[:, cols] = jnp.sum(fold_rows(du.astype(F32)), axis=0, keepdims=True)
        value = dot_tn(hb_ref[...], du).astype(BF16)
        part, col = i // per_line, chunk_of(i % per_line, chunk)
        for a in range(count):
            spots = [spot_of(ids, 2 + n, kind, a, count) for n in range(PARTS)]
            spot = jnp.where(part == 0, spots[0], spots[1])
            out_ref[part, spot, :, col] = value[a * up_rows : (a + 1) * up_rows, :]
        acc[...] += dot_nt(du, up_ref[:, cols])
        return carry

    lax.fori_loop(0, hidden // chunk, step, 0)
    if kind == 0:
        fold_s[...] = jnp.zeros_like(fold_s)
        gain_row = row_of(gain_a)

        def norm(blk, carry):
            r = chunk_of(blk, LANES)
            grad = acc[r, :]
            normed = n_ref[r, :]
            fold_s[0] += fold_rows(grad * normed)
            fold_s[1] += fold_rows(grad)
            scaled = grad * gain_row
            mean_a = jnp.mean(scaled, axis=1, keepdims=True)
            mean_b = jnp.mean(scaled * normed, axis=1, keepdims=True)
            dr1 = (scaled - mean_a - normed * mean_b) * rstd_ref[r, 0:1]
            dr1_ref[r, :] = dr1
            da = dr1.astype(BF16)
            da_ref[r, :] = da
            fold_s[2] += fold_rows(da.astype(F32))
            return carry

        lax.fori_loop(0, rows // LANES, norm, 0)
        vec_ref[...] = jnp.sum(fold_s[...], axis=1)


def ffn_bwd(kind, ids, df, hb, gp, down, up, extra, count):
    rows, width = df.shape
    hidden = up.shape[1]
    outs = [shaped((hidden // width, count, width // count, width), BF16), shaped((1, hidden), F32)]
    scratch = []
    if kind == 1:
        outs += [shaped((rows, width), F32)]
    else:
        outs += [shaped((rows, width), F32), shaped((rows, width), BF16), shaped((3, width), F32)]
        scratch = [pltpu.VMEM((rows, width), F32), pltpu.VMEM((3, 8, width), F32)]
    return call(
        functools.partial(ffn_bwd_body, kind),
        outs,
        (ids,),
        (df, hb, gp, down, up, *extra),
        scratch,
        flops=6 * rows * width * hidden,
        moved=4 * rows * hidden + 6 * width * hidden + 10 * rows * width,
    )


def attn_bwd_body(
    kind, ids, bucket, lens, keep, qa_ref, k_ref, v_ref, o_ref, da_ref, wo_ref, w_ref, x_ref, bu_ref, va_ref, vf_ref, *rest
):
    if kind == 1:
        dr1_ref, g_ref, dw_ref, ig_ref, bm_s = rest
    else:
        ig_in, dw_ref, ig_ref, bm_s = rest
    rows, width = da_ref.shape
    pairs = k_ref.shape[0]
    local = pairs * LANES
    count = dw_ref.shape[1]
    size, out_size, wide = width // count, local // count, width // local
    _, bm_s[...] = mask_columns(ids, bucket, lens, rows)
    if kind == 1:
        for blk in range(rows // LANES):
            r = slice(blk * LANES, (blk + 1) * LANES)
            far = pl.ds(pl.multiple_of(ids[0] * rows + blk * LANES, LANES), LANES)
            kept = keep_of(ids, bucket, keep, blk)
            ig_ref[r, :] = dr1_ref[r, :] + jnp.where(kept, 0.0, g_ref[far, :].astype(F32))
    else:
        ig_ref[...] = ig_in[...]
    tile = rows // 2

    def pair(p, carry):
        cols = chunk_of(p, LANES)
        kp = k_ref[p]
        vp = v_ref[p]
        bm = bm_s[...]
        low_t, low_r = low_half(tile), low_half(rows)
        zero_t, zero_r = jnp.zeros((tile, LANES), BF16), jnp.zeros((rows, LANES), BF16)
        wo = wo_ref[cols, :]
        dk_sum = dv_sum = None
        dqs = []
        for rb in range(2):
            r = slice(rb * tile, (rb + 1) * tile)
            dop = dot_nt(da_ref[r, :], wo).astype(BF16)
            dq = None
            for par in range(2):
                own_t = low_t if par == 0 else jnp.logical_not(low_t)
                own_r = low_r if par == 0 else jnp.logical_not(low_r)
                qa = qa_ref[2 * p + par, r, :]
                doa = jnp.where(own_t, dop, zero_t)
                prob = jnp.exp(dot_nt(jnp.where(own_r, kp, bm), qa))
                dprob = dot_nt(vp, doa)
                inner = jnp.sum(prob * dprob, axis=0, keepdims=True)
                dscore = (prob * (dprob - inner)).astype(BF16)
                dv = dot_nn(prob.astype(BF16), doa)
                dk = dot_nn(dscore, jnp.where(own_t, qa, zero_t))
                dqp = dot_tn(dscore, jnp.where(own_r, kp, zero_r))
                dv_sum = dv if dv_sum is None else dv_sum + dv
                dk_sum = dk if dk_sum is None else dk_sum + dk
                dq = dqp if dq is None else dq + dqp
            dqs.append((dq * 0.125).astype(BF16))
        dqp = jnp.concatenate(dqs, axis=0)
        dvp = dv_sum.astype(BF16)
        grads = jnp.concatenate([dqp, dk_sum.astype(BF16), dvp], axis=1)
        weights = jnp.concatenate([w_ref[n, :, cols] for n in range(3)], axis=1)
        ig_ref[...] += dot_nt(grads, weights)
        value = dot_tn(x_ref[chunk_of(ids[0], rows), :], grads).astype(BF16)
        heads = jnp.concatenate([o_ref[n] for n in range(pairs)], axis=1)
        da = [da_ref[:, pl.ds(pl.multiple_of(n * local + p * LANES, LANES), LANES)] for n in range(wide)]
        out_value = dot_tn(heads, jnp.concatenate(da, axis=1)).astype(BF16)
        small = [jnp.sum(fold_rows(g.astype(F32)), axis=0, keepdims=True) for g in (dqp, dvp)]
        for ref in (bu_ref, va_ref, vf_ref):
            for n in range(ref.shape[0]):
                for c in range(0, ref.shape[1], local):
                    small.append(ref[n : n + 1, pl.ds(pl.multiple_of(c + p * LANES, LANES), LANES)])
        line = lax.broadcasted_iota(jnp.int32, (8, LANES), 0)
        for a in range(count):
            spots = [spot_of(ids, 4 + n, kind, a, count) for n in range(PARTS)]
            rows_a = slice(a * size, (a + 1) * size)
            dw_ref[0, spots[0], 0:size, cols] = value[rows_a, 0:LANES]
            dw_ref[0, spots[0], size : 2 * size, cols] = value[rows_a, LANES : 2 * LANES]
            dw_ref[1, spots[1], 0:size, cols] = value[rows_a, 2 * LANES :]
            for n in range(wide):
                part = out_value[a * out_size : (a + 1) * out_size, n * LANES : (n + 1) * LANES]
                at = size + n * out_size
                dw_ref[1, spots[1], at : at + out_size, cols] = part
            tile_s = jnp.zeros((8, LANES), F32)
            dw_ref[0, spots[0], 2 * size : 2 * size + 8, cols] = tile_s.astype(BF16)
            for n, row in enumerate(small[a::count]):
                tile_s = jnp.where(line == n, row, tile_s)
            dw_ref[1, spots[1], 2 * size : 2 * size + 8, cols] = tile_s.astype(BF16)
        return carry

    lax.fori_loop(0, pairs, pair, 0)


def attn_bwd(kind, scal, qa, k, v, o, da, wo, w, tokens, smalls, extra, count):
    rows, width = da.shape
    pairs = k.shape[0]
    local = pairs * LANES
    lines = 2 * width // count + 8
    return call(
        functools.partial(attn_bwd_body, kind),
        [shaped((PARTS, count, lines, local), BF16), shaped((rows, width), F32)],
        scal,
        (qa, k, v, o, da, wo, w, tokens, *smalls, *extra),
        [pltpu.VMEM((rows, LANES), BF16)],
        flops=2 * rows * local * (8 * width + 10 * rows),
        moved=2 * (rows * local * 4 + width * local * 7 + rows * width * 2) + 8 * rows * width,
        trans=2 * pairs * rows * rows,
    )


def place_body(part, first, count, plan, n_held, small_plan, ids, *refs):
    pieces = refs[: 1 if small_plan is None else 2]
    refs = refs[len(pieces) + n_held :]
    outs, refs = refs[: len(plan)], refs[len(plan) :]
    n_small = 0 if small_plan is None else len(small_plan)
    small_outs, refs = refs[:n_small], refs[n_small:]
    stages, sems = refs[:-1], refs[-1]
    half, lines, _ = pieces[0].shape
    copies = []
    for q in range(half):
        a = spot_of(ids, part, 2, first + q, count)
        for n, (parts, target) in enumerate(plan):
            for at, start, size in parts:
                stages[n][(q,) + at] = pieces[0][q, start : start + size, :].astype(F32)
            copy = pltpu.make_async_copy(stages[n].at[q], target(outs[n], a), sems.at[n, q])
            copy.start()
            copies.append(copy)
    for n in range(n_small):
        for line, c0, row in small_plan[n]:
            p = spot_of(ids, part, 3, row % count, count)
            high = pieces[0][p & (half - 1), lines - 8 :, :].astype(F32)
            low = pieces[1][p & (half - 1), lines - 8 :, :].astype(F32)
            tile = jnp.where(p < half, low, high)
            width = tile.shape[1]
            value = tile[row // count : row // count + 1, :]
            if line is None:
                small_outs[n][c0 : c0 + width] = value.reshape(width)
            else:
                small_outs[n][line : line + 1, c0 : c0 + width] = value
    for copy in copies:
        copy.wait()


def place(part, first, ids, pieces, plan, held=(), small_outs=(), small_plan=None):
    half = pieces[0].shape[0]
    outs = [shaped(entry[0], F32) for entry in plan]
    return call(
        functools.partial(place_body, part, first, 2 * half, [entry[2:] for entry in plan], len(held), small_plan),
        outs + list(small_outs),
        (ids,),
        (*pieces, *held),
        [pltpu.VMEM((half,) + entry[1], F32) for entry in plan] + [pltpu.SemaphoreType.DMA((len(outs), half))],
        moved=6 * half * pieces[0].shape[1] * pieces[0].shape[2],
        in_specs=[resident()] * len(pieces) + [anywhere()] * len(held),
        out_specs=[anywhere()] * len(outs) + [resident()] * len(small_outs),
        input_output_aliases={1 + len(pieces) + n: n for n in range(len(held))},
    )


def join_body(cores, ids, *refs):
    n = (len(refs) - 1) // 3
    owns, others, outs, sems = refs[:n], refs[n : 2 * n], refs[2 * n : 3 * n], refs[-1]
    copies = []
    for k in range(n):
        rows = owns[k].shape[0]
        for part, where in ((owns[k], ids[0]), (others[k], cores - 1 - ids[0])):
            target = outs[k].at[pl.ds(pl.multiple_of(where * rows, rows), rows), :]
            copies.append(pltpu.make_async_copy(part, target, sems.at[len(copies)]))
            copies[-1].start()
    for copy in copies:
        copy.wait()


def join(ids, cores, owns, others):
    return call(
        functools.partial(join_body, cores),
        [shaped((cores * o.shape[0], o.shape[1]), o.dtype) for o in owns],
        (ids,),
        (*owns, *others),
        [pltpu.SemaphoreType.DMA((2 * len(owns),))],
        moved=sum(4 * o.size * o.dtype.itemsize for o in owns),
        out_specs=[anywhere()] * len(owns),
    )


def swap_cores(array_in, cores):
    return lax.ppermute(array_in, "tensor", [(c, cores - 1 - c) for c in range(cores)])


class GroupSum:
    def __init__(self, mesh, batch, own, other_received):
        self.mesh, self.batch = mesh, batch
        self.halvings = own.shape[0].bit_length() - 1
        self.steps = 2 * self.halvings + 1
        self.terms = [own, other_received]
        self.at = 0
        self.sent = None

    def exchange(self, array_in, bit_of):
        groups, cores = self.mesh.shape["dp"], self.mesh.shape["tensor"]
        pairs = [(i * cores + c, (i ^ (1 << bit_of(c))) * cores + c) for i in range(groups) for c in range(cores)]
        return lax.ppermute(array_in, ("dp", "tensor"), pairs)

    def total(self, terms):
        acc = terms[0].astype(F32)
        for term in terms[1:]:
            acc = acc + term.astype(F32)
        return acc.astype(BF16)

    def step(self, *earlier):
        terms = self.terms
        if earlier:
            terms = terms[:-1] + [after(terms[-1], *earlier)]
        n = self.at
        if n < self.halvings:
            half = terms[0].shape[0] // 2
            self.sent = self.total([term[half:] for term in terms])
            received = self.exchange(self.sent, lambda c: step_bits(self.batch, c, 0, self.halvings)[n])
            self.terms = [term[:half] for term in terms] + [received]
        elif n == self.halvings:
            doublings = (self.mesh.shape["dp"] >> self.halvings).bit_length() - 1
            for k in range(doublings):
                self.sent = self.total(terms)
                terms = [self.sent, self.exchange(self.sent, lambda c, k=k: self.halvings + k)]
            self.terms = terms
        else:
            n -= self.halvings + 1
            self.sent = self.total(terms) if n == 0 else jnp.concatenate(terms, axis=0)
            received = self.exchange(self.sent, lambda c: step_bits(self.batch, c, 1, self.halvings)[n])
            self.terms = [self.sent, received]
        self.at += 1
        return self.sent


def per_device(
    mesh,
    tokens,
    w_qkv,
    bias_qv,
    w_out,
    bias_out,
    gain_attn,
    shift_attn,
    w_up,
    bias_up,
    w_down,
    bias_down,
    gain_ffn,
    shift_ffn,
    out_grad,
    bucket_len,
    seq_lengths,
    keep_mask,
):
    cores = mesh.shape["tensor"]
    count = min(8, mesh.shape["dp"])
    width = tokens.shape[1]
    rows = tokens.shape[0] // cores
    hidden = w_up.shape[1]
    local = w_qkv.shape[2]
    ids = jnp.where(jnp.arange(2) == 0, lax.axis_index("tensor"), lax.axis_index("dp")).astype(jnp.int32)

    w_qkv_o = swap_cores(w_qkv, cores)
    bias_qv_o = swap_cores(bias_qv, cores)
    w_out_o = swap_cores(w_out, cores)
    bias_up_o = swap_cores(bias_up, cores)
    w_up_o = swap_cores(w_up, cores)
    w_down_o = swap_cores(w_down, cores)

    attn_scal = (ids, bucket_len, seq_lengths)
    qa, k, v, o = attn_fwd(False, attn_scal, tokens, w_qkv, bias_qv, rows)
    qa_o, k_o, v_o, o_o, n1, rstd, hb = attn_fwd(
        True,
        attn_scal,
        tokens,
        w_qkv_o,
        bias_qv_o,
        rows,
        (o, w_out_o, w_out, bias_out, gain_attn, shift_attn),
    )
    keep_scal = (ids, bucket_len, keep_mask)
    vecs = (gain_attn, shift_attn, bias_down, gain_ffn, shift_ffn)
    gb, gb_o, gp, gp_o, mixed, dr2, df, vec_f = ffn_fwd(
        keep_scal, hb, n1, w_up, w_up_o, bias_up, bias_up_o, w_down, w_down_o, vecs, tokens, out_grad
    )
    mixed_o = swap_cores(mixed, cores)
    down_other = down_grad(1, ids, gb_o, df, count)
    down_got = swap_cores(down_other, cores)
    down_own = down_grad(0, ids, gb, after(df, down_other), count)
    sums = []

    def add_sums(own, received):
        for part in range(PARTS):
            sums.append(GroupSum(mesh, len(sums), own[part], received[part]))

    add_sums(down_own, down_got)
    landed, sents = [[], []], [[], []]

    def exchange(parts, *earlier):
        which = parts[0] % 2
        earlier += tuple(landed[which]) + tuple(sents[1 - which])
        sents[which] = [sums[part].step(*earlier) for part in parts]
        landed[which] = [sums[part].terms[-1] for part in parts]

    def exchange_all(stage, *earlier):
        for parts in EARLY[stage]:
            exchange(parts, *earlier)
        return sents[0] + sents[1]

    sent = exchange_all(0, df)
    up_other, bu_o, dh = ffn_bwd(1, ids, after(df, *sent), hb, gp_o, w_down_o, w_up_o, (dr2,), count)
    up_got = swap_cores(up_other, cores)
    sent = exchange_all(1, dh)
    up_own, bu, dr1, da, vec_a = ffn_bwd(
        0, ids, after(df, *sent), hb, gp, w_down, w_up, (dh, n1, rstd, gain_attn), count
    )
    add_sums(up_own, up_got)
    sent = exchange_all(2, da)
    bwd_scal = (ids, bucket_len, seq_lengths, keep_mask)
    qkv_other, ig_part = attn_bwd(
        1, bwd_scal, qa_o, k_o, v_o, o_o, after(da, *sent), w_out_o, w_qkv_o, tokens,
        (bu_o, vec_a, vec_f), (dr1, out_grad), count,
    )
    qkv_got = swap_cores(qkv_other, cores)
    sent = exchange_all(3, ig_part, mixed_o)
    qkv_own, ig = attn_bwd(
        0, bwd_scal, qa, k, v, o, after(da, *sent), w_out, w_qkv, tokens, (bu, vec_a, vec_f), (ig_part,), count
    )
    ig_o = swap_cores(ig, cores)
    add_sums(qkv_own, qkv_got)

    def rows_at(each, size, shift=0, cols=slice(None)):
        def target(out, a):
            start = pl.multiple_of(a * each, each)
            return out.at[pl.ds(start + shift, size), cols]

        return target

    every = (slice(None), slice(None))
    size, out_size, wide = width // count, local // count, width // local
    half_rows = hidden // (count * PARTS)
    plans = []
    for part in range(PARTS):
        target = rows_at(PARTS * half_rows, half_rows, part * half_rows)
        plans.append([((hidden, width), (half_rows, width), [(every, 0, half_rows)], target)])
    for part in range(hidden // width):
        target = rows_at(size, size, 0, slice(part * width, (part + 1) * width))
        plans.append([((width, hidden), (size, width), [(every, 0, size)], target)])

    def planes_at(first, planes):
        return lambda out, a: out.at[first : first + planes, pl.ds(pl.multiple_of(a * size, size), size), :]

    shape = (3, width, local)
    plans.append([(shape, (2, size, local), [((n,) + every, n * size, size) for n in range(2)], planes_at(0, 2))])
    pieces = [((slice(None), slice(n * local, (n + 1) * local)), size + n * out_size, out_size) for n in range(wide)]
    plans.append(
        [
            (shape, (1, size, local), [((0,) + every, 0, size)], planes_at(2, 1)),
            ((local, width), (out_size, width), pieces, rows_at(out_size, out_size)),
        ]
    )
    per_up, per_norm = hidden // local, width // local
    small_plan = [[(n, 0, n) for n in range(2)], [(None, c * local, 2 + c) for c in range(per_up)]]
    for n in range(6):
        small_plan.append([(None, c * local, 2 + per_up + n * per_norm + c) for c in range(per_norm)])
    small_outs = [shaped((2, local), F32), shaped((hidden,), F32)] + [shaped((width,), F32)] * 6
    held = {0: [], 1: [], 2: []}
    small = []

    def put(part, late, *earlier):
        each = sums[part]
        pieces = [after(each.terms[1] if late else each.terms[0], *earlier)] if earlier else [each.terms[1 if late else 0]]
        first = count // 2 if late else 0
        batch = part // PARTS
        extra = held[batch][: len(plans[part])]
        if late and part == len(plans) - 1:
            placed = place(part, first, ids, pieces + [each.terms[0]], plans[part], extra, small_outs, small_plan)
            small.extend(placed[len(plans[part]) :])
            placed = placed[: len(plans[part])]
        else:
            placed = place(part, first, ids, pieces, plans[part], extra)
        held[batch] = list(placed) + held[batch][len(placed) :]
        return placed[0]

    put_early, put_late = set(), set()
    fillers = [ig]
    for turn, parts in enumerate(TURNS):
        active = [part for part in parts if sums[part].at < sums[part].steps]
        earlier, later = fillers, []
        if turn == JOIN_AT:
            out_mixed, out_ig = join(ids, cores, (mixed, after(ig, *sents[0])), (mixed_o, ig_o))
            later.append(out_ig)
        for part in parts:
            if sums[part].at == sums[part].steps and part not in put_late and part < 4:
                later.append(put(part, True, *landed[part % 2]))
                put_late.add(part)
        if active:
            exchange(active, *earlier)
        for part in parts:
            if sums[part].at == sums[part].steps and part not in put_early:
                put(part, False)
                put_early.add(part)
        fillers = later
    for part in range(len(plans)):
        if part not in put_late:
            put(part, True)
    grad_w_down, grad_w_up = held[0][0], held[1][0]
    grad_w_qkv, grad_w_out = held[2]
    grad_bias_qv, grad_bias_up, *norms = small
    return (
        out_mixed,
        out_ig,
        grad_w_qkv,
        grad_bias_qv,
        grad_w_out,
        norms[2],
        norms[0],
        norms[1],
        grad_w_up,
        grad_bias_up,
        grad_w_down,
        norms[5],
        norms[3],
        norms[4],
    )


def solution(mesh):
    in_specs = (
        P("dp", None),
        P(None, None, "tensor"),
        P(None, "tensor"),
        P("tensor", None),
        P(),
        P(),
        P(),
        P(None, "tensor"),
        P("tensor"),
        P("tensor", None),
        P(),
        P(),
        P(),
        P("dp", None),
        P("dp"),
        P("dp", None),
        P("dp", None),
    )
    out_specs = (
        P("dp", None),
        P("dp", None),
        P(None, None, "tensor"),
        P(None, "tensor"),
        P("tensor", None),
        P(),
        P(),
        P(),
        P(None, "tensor"),
        P("tensor"),
        P("tensor", None),
        P(),
        P(),
        P(),
    )
    return jax.shard_map(
        functools.partial(per_device, mesh),
        mesh=mesh,
        in_specs=in_specs,
        out_specs=out_specs,
        check_vma=False,
    )
```

```python
import functools

import jax
import jax.numpy as jnp
from jax import lax
from jax.experimental import pallas as pl
from jax.experimental.pallas import tpu as pltpu
from jax.sharding import PartitionSpec as P

HD = 64
BUCKET_LONG = 512
LANES = 128
EPS = 1e-05
F32 = jnp.float32
BF16 = jnp.bfloat16
NEG = -1e30
MIB = 1 << 20
VMEM_MIB = 16
COVER = 20

STEP_BITS = ((((1, 0, 2), (2, 1, 0)), ((0, 1, 2), (2, 0, 1))), (((1, 2, 0), (2, 1, 0)), ((0, 2, 1), (2, 0, 1))), (((0, 1, 2), (2, 0, 1)), ((1, 0, 2), (1, 0, 2))), (((0, 1, 2), (0, 2, 1)), ((1, 0, 2), (2, 1, 0))), (((0, 1, 2), (2, 0, 1)), ((1, 0, 2), (0, 1, 2))), (((0, 1, 2), (0, 1, 2)), ((1, 0, 2), (2, 0, 1))))
PARTS = 2
EARLY = (((0,), (1,)), ((0,),), ((0, 2), (1, 3)), ((0, 2), (1, 3)))
TURNS = ((4, 2, 0), (5, 3, 1)) * 7
JOIN_AT = 2


def dot_nn(left, right):
    return lax.dot_general(left, right, (((1,), (0,)), ((), ())), preferred_element_type=F32)


def dot_nt(left, right):
    return lax.dot_general(left, right, (((1,), (1,)), ((), ())), preferred_element_type=F32)


def dot_tn(left, right):
    return lax.dot_general(left, right, (((0,), (0,)), ((), ())), preferred_element_type=F32)


def resident():
    return pl.BlockSpec(memory_space=pltpu.VMEM)


def anywhere():
    return pl.BlockSpec(memory_space=pl.ANY)


def shaped(shape, dtype):
    return jax.ShapeDtypeStruct(shape, dtype)


def call(body, outs, scalars, operands, scratch=(), vmem=VMEM_MIB, flops=0, moved=0, trans=0, **kwargs):
    specs = kwargs.pop("in_specs", None) or [resident()] * len(operands)
    return pl.pallas_call(
        body,
        out_shape=outs,
        grid_spec=pltpu.PrefetchScalarGridSpec(
            num_scalar_prefetch=len(scalars),
            grid=(1,),
            in_specs=specs,
            out_specs=kwargs.pop("out_specs", None) or [resident()] * len(outs),
            scratch_shapes=list(scratch),
        ),
        compiler_params=pltpu.CompilerParams(dimension_semantics=("arbitrary",), vmem_limit_bytes=vmem * MIB),
        cost_estimate=pl.CostEstimate(flops=COVER * flops, bytes_accessed=moved, transcendentals=trans),
        **kwargs,
    )(*scalars, *operands)


def chunk_of(index, size):
    return pl.ds(pl.multiple_of(index * size, size), size)


def after(value, *earlier):
    return lax.optimization_barrier((value,) + earlier)[0]


def move_bits(number, pairs):
    out = 0
    for take, put in pairs:
        out = out | lax.shift_left(lax.shift_right_logical(number, take) & 1, put)
    return out


def step_bits(batch, core, gathering, steps):
    return [bit for bit in STEP_BITS[batch][core % 2][gathering] if bit < steps]


def spot_of(ids, batch, kind, number, count):
    steps = count.bit_length() - 1
    me = ids[1] & (count - 1)
    number = jnp.int32(number) if isinstance(number, int) else number
    spots = []
    for core in range(2):
        bits = step_bits(batch, 1 - core if kind == 1 else core, kind > 1, steps)
        places = range(steps) if kind > 1 else range(steps - 1, -1, -1)
        if kind == 2:
            spots.append(move_bits(number, zip(places, bits, strict=True)) ^ me)
        else:
            spots.append(move_bits(number ^ me, zip(bits, places, strict=True)))
    return jnp.where((ids[0] & 1) == 0, spots[0], spots[1])


def bucket_shift(bucket_ref):
    return jnp.where(bucket_ref[0] >= BUCKET_LONG, 9, 7)


def mask_columns(ids_ref, bucket_ref, lens_ref, rows):
    shift = bucket_shift(bucket_ref)
    first = ids_ref[0] * lax.shift_right_logical(BUCKET_LONG, shift)
    place = lax.broadcasted_iota(jnp.int32, (rows, LANES), 0)
    lane = lax.broadcasted_iota(jnp.int32, (rows, LANES), 1) & (HD - 1)
    seq = lax.shift_right_logical(place, jnp.full((rows, LANES), shift, jnp.int32))
    pos = place - lax.shift_left(seq, jnp.full((rows, LANES), shift, jnp.int32))
    length = jnp.full((rows, LANES), lens_ref[0, first], jnp.int32)
    for slot in range(1, 4):
        length = jnp.where(seq == slot, lens_ref[0, first + slot], length)
    hit = seq == lane
    query_cols = jnp.where(hit, 1.0, 0.0)
    key_cols = jnp.where(hit & (pos < length), 0.0, NEG)
    key_cols = jnp.where(lane < 4, key_cols, jnp.where(lane < 7, 1.0, 0.0))
    return query_cols.astype(BF16), key_cols.astype(BF16)


def low_half(rows):
    return lax.broadcasted_iota(jnp.int32, (rows, LANES), 1) < HD


def row_of(vec_ref):
    return vec_ref[...].reshape(1, -1)


def attn_fwd_body(last, ids, bucket, lens, x_ref, w_ref, b_ref, *rest):
    if last:
        (other_o, wo_own, wo_other, bias_out, gain, shift_vec) = rest[:6]
        qa_ref, k_ref, v_ref, o_ref, n_ref, rstd_ref, hb_ref = rest[6:13]
        am_s, bm_s = rest[13:]
    else:
        qa_ref, k_ref, v_ref, o_ref, am_s, bm_s, x_s, w_s, b_s, sems = rest
    pairs, rows, _ = k_ref.shape
    if not last:
        copies = [pltpu.make_async_copy(x_ref.at[chunk_of(ids[0], rows), :], x_s, sems.at[0])]
        copies.append(pltpu.make_async_copy(b_ref, b_s, sems.at[1]))
        for p in range(pairs):
            cols = slice(p * LANES, (p + 1) * LANES)
            copies.append(pltpu.make_async_copy(w_ref.at[:, :, cols], w_s.at[p], sems.at[2 + p]))
        for copy in copies:
            copy.start()
        b_ref = b_s
    am_s[...], bm_s[...] = mask_columns(ids, bucket, lens, rows)
    tile = rows // 2
    if not last:
        copies[0].wait()
        copies[1].wait()

    def pair(p, carry):
        cols = chunk_of(p, LANES)
        if last:
            weights = jnp.concatenate([w_ref[n, :, cols] for n in range(3)], axis=1)
            qkv = dot_nn(x_ref[chunk_of(ids[0], rows), :], weights)
        else:
            pltpu.make_async_copy(w_ref.at[:, :, slice(0, LANES)], w_s.at[p], sems.at[2 + p]).wait()
            qkv = dot_nn(x_s[...], jnp.concatenate([w_s[p, n] for n in range(3)], axis=1))
        qp = ((qkv[:, :LANES] + b_ref[0:1, cols]).astype(BF16).astype(F32) * 0.125).astype(BF16)
        kp = qkv[:, LANES : 2 * LANES].astype(BF16)
        vp = (qkv[:, 2 * LANES :] + b_ref[1:2, cols]).astype(BF16)
        k_ref[p] = kp
        v_ref[p] = vp
        bm = bm_s[...]
        low_r, low_t = low_half(rows), low_half(tile)
        lane = lax.broadcasted_iota(jnp.int32, (tile, LANES), 1) & (HD - 1)
        for rb in range(2):
            r = slice(rb * tile, (rb + 1) * tile)
            am = am_s[r, :]
            qpr = qp[r, :]
            sums = []
            for par in range(2):
                own_t = low_t if par == 0 else jnp.logical_not(low_t)
                own_r = low_r if par == 0 else jnp.logical_not(low_r)
                scores = dot_nt(jnp.where(own_t, qpr, am), jnp.where(own_r, kp, bm))
                top = jnp.max(scores, axis=1, keepdims=True)
                expo = jnp.exp(scores - top).astype(BF16)
                total = dot_nn(expo, jnp.where(own_r, vp, jnp.ones_like(vp)))
                sums.append(total)
                neg_log = -(top + jnp.log(jnp.where(own_t, 1.0, total)))
                hi = neg_log.astype(BF16)
                mid = (neg_log - hi.astype(F32)).astype(BF16)
                lo = (neg_log - hi.astype(F32) - mid.astype(F32)).astype(BF16)
                parts = jnp.where(lane == 4, hi, jnp.where(lane == 5, mid, jnp.where(lane == 6, lo, am)))
                qa_ref[2 * p + par, r, :] = jnp.where(own_t, qpr, parts)
            total = pltpu.roll(jnp.where(low_t, sums[1], sums[0]), HD, 1)
            o_ref[p, r, :] = (jnp.where(low_t, sums[0], sums[1]) / total).astype(BF16)
        return carry

    lax.fori_loop(0, pairs, pair, 0)
    if last:
        block = rows // 4
        gain_row, shift_row, bias_row = row_of(gain), row_of(shift_vec), row_of(bias_out)

        def norm(i, carry):
            r = chunk_of(i, block)
            heads = [o_ref[n, r, :] for n in range(pairs)] + [other_o[n, r, :] for n in range(pairs)]
            weights = jnp.concatenate([wo_own[...], wo_other[...]], axis=0)
            acc = dot_nn(jnp.concatenate(heads, axis=1), weights)
            acc += x_ref[pl.ds(pl.multiple_of(ids[0] * rows + i * block, block), block), :].astype(F32) + bias_row
            centre = acc - jnp.mean(acc, axis=1, keepdims=True)
            rstd = lax.rsqrt(jnp.mean(centre * centre, axis=1, keepdims=True) + EPS)
            normed = centre * rstd
            n_ref[r, :] = normed
            rstd_ref[r, :] = jnp.broadcast_to(rstd, (block, LANES))
            hb_ref[r, :] = (normed * gain_row + shift_row).astype(BF16)
            return carry

        lax.fori_loop(0, 4, norm, 0, unroll=True)


def attn_fwd(last, scal, tokens, w, b, rows, extra=()):
    width = tokens.shape[1]
    local = w.shape[2]
    pairs = local // LANES
    outs = [shaped((2 * pairs, rows, LANES), BF16)] + [shaped((pairs, rows, LANES), BF16)] * 3
    if last:
        outs += [shaped((rows, width), F32), shaped((rows, LANES), F32), shaped((rows, width), BF16)]
    scratch = [pltpu.VMEM((rows, LANES), BF16)] * 2
    specs = None
    if not last:
        scratch += [pltpu.VMEM((rows, width), BF16), pltpu.VMEM((pairs, 3, width, LANES), BF16)]
        scratch += [pltpu.VMEM(b.shape, F32), pltpu.SemaphoreType.DMA((2 + pairs,))]
        specs = [anywhere()] * 3
        tokens, w, b = (pltpu.with_memory_space_constraint(each, pltpu.HBM) for each in (tokens, w, b))
    return call(
        functools.partial(attn_fwd_body, last),
        outs,
        scal,
        (tokens, w, b, *extra),
        scratch,
        in_specs=specs,
        flops=2 * rows * local * (3 * width + 4 * rows + (2 * width if last else 0)),
        moved=2 * (rows * width + 3 * width * local + 5 * rows * local),
        trans=2 * pairs * rows * rows,
    )


def keep_of(ids, bucket, keep, block):
    shift = bucket_shift(bucket)
    first = ids[0] * lax.shift_right_logical(BUCKET_LONG, shift)
    return keep[0, first + lax.shift_right_logical(block * LANES, shift)] > 0


def fold_rows(array_in):
    rows, cols = array_in.shape
    return jnp.sum(array_in.reshape(rows // 8, 8, cols), axis=0)


def ffn_fwd_body(
    ids, bucket, keep, hb_ref, n_ref, up_own, up_other, bu_own, bu_other, down_own, down_other,
    gain_a, shift_a, bias_down, gain_f, shift_f, x_ref, g_ref,
    gb_own, gb_other, gp_own, gp_other, mixed_ref, dr2_ref, df_ref, vec_ref, acc, fold_s,
):
    rows, width = hb_ref.shape
    acc[...] = n_ref[...] * row_of(gain_a) + (row_of(shift_a) + row_of(bias_down))
    half = rows // 2
    chunk = 256

    def hidden(i, carry):
        cols = chunk_of(i, chunk)
        for r in range(2):
            rs = slice(r * half, (r + 1) * half)
            hb = hb_ref[rs, :]
            total = None
            for up, bu, down, gb, gp in (
                (up_own, bu_own, down_own, gb_own, gp_own),
                (up_other, bu_other, down_other, gb_other, gp_other),
            ):
                u = dot_nn(hb, up[:, cols]) + bu[cols].reshape(1, -1)
                cdf = 0.5 * (1.0 + lax.erf(u * 0.7071067811865476))
                pdf = jnp.exp(-0.5 * u * u) * 0.3989422804014327
                gp[rs, cols] = cdf + u * pdf
                act = (u * cdf).astype(BF16)
                gb[rs, cols] = act
                part = dot_nn(act, down[cols, :])
                total = part if total is None else total + part
            acc[rs, :] += total
        return carry

    lax.fori_loop(0, up_own.shape[1] // chunk, hidden, 0, unroll=2)
    fold_s[...] = jnp.zeros_like(fold_s)
    gain_row, shift_row = row_of(gain_f), row_of(shift_f)

    def norm(blk, carry):
        r = chunk_of(blk, LANES)
        far = pl.ds(pl.multiple_of(ids[0] * rows + blk * LANES, LANES), LANES)
        kept = keep_of(ids, bucket, keep, blk)
        res = acc[r, :]
        centre = res - jnp.mean(res, axis=1, keepdims=True)
        rstd = lax.rsqrt(jnp.mean(centre * centre, axis=1, keepdims=True) + EPS)
        normed = centre * rstd
        final = normed * gain_row + shift_row
        mixed_ref[r, :] = jnp.where(kept, final, x_ref[far, :].astype(F32)).astype(BF16)
        grad = jnp.where(kept, g_ref[far, :].astype(F32), 0.0)
        fold_s[0] += fold_rows(grad * normed)
        fold_s[1] += fold_rows(grad)
        scaled = grad * gain_row
        mean_a = jnp.mean(scaled, axis=1, keepdims=True)
        mean_b = jnp.mean(scaled * normed, axis=1, keepdims=True)
        dr2 = (scaled - mean_a - normed * mean_b) * rstd
        dr2_ref[r, :] = dr2
        df = dr2.astype(BF16)
        df_ref[r, :] = df
        fold_s[2] += fold_rows(df.astype(F32))
        return carry

    lax.fori_loop(0, rows // LANES, norm, 0, unroll=True)
    vec_ref[...] = jnp.sum(fold_s[...], axis=1)


def ffn_fwd(scal, hb, n1, up_own, up_other, bu_own, bu_other, down_own, down_other, vecs, tokens, out_grad):
    rows, width = hb.shape
    hidden = up_own.shape[1]
    outs = [
        shaped((rows, hidden), BF16), shaped((rows, hidden), BF16),
        shaped((rows, hidden), F32), shaped((rows, hidden), F32),
        shaped((rows, width), BF16), shaped((rows, width), F32), shaped((rows, width), BF16),
        shaped((3, width), F32),
    ]
    return call(
        ffn_fwd_body,
        outs,
        scal,
        (hb, n1, up_own, up_other, bu_own, bu_other, down_own, down_other, *vecs, tokens, out_grad),
        [pltpu.VMEM((rows, width), F32), pltpu.VMEM((3, 8, width), F32)],
        flops=8 * rows * width * hidden,
        moved=12 * rows * hidden + 8 * width * hidden + 20 * rows * width,
        trans=4 * rows * hidden,
    )


def down_grad_body(kind, ids, gb_ref, df_ref, out_ref):
    _, count, size, _ = out_ref.shape
    per = 2 if count % 2 == 0 else 1

    def step(i, carry):
        value = dot_tn(gb_ref[:, chunk_of(i, per * PARTS * size)], df_ref[...]).astype(BF16)
        for c in range(per):
            for part in range(PARTS):
                first = (c * PARTS + part) * size
                out_ref[part, spot_of(ids, part, kind, i * per + c, count)] = value[first : first + size, :]
        return carry

    lax.fori_loop(0, count // per, step, 0, unroll=4)


def down_grad(kind, ids, gb, df, count):
    rows, width = df.shape
    hidden = gb.shape[1]
    return call(
        functools.partial(down_grad_body, kind),
        [shaped((PARTS, count, hidden // (count * PARTS), width), BF16)],
        (ids,),
        (gb, df),
        flops=2 * rows * width * hidden,
        moved=2 * rows * hidden + 2 * width * hidden + 2 * rows * width,
    )[0]


def ffn_bwd_body(kind, ids, df_ref, hb_ref, gp_ref, down_ref, up_ref, *rest):
    if kind == 1:
        dr2_ref, out_ref, bu_ref, acc = rest
        acc[...] = dr2_ref[...]
    else:
        acc_in, n_ref, rstd_ref, gain_a, out_ref, bu_ref, dr1_ref, da_ref, vec_ref, acc, fold_s = rest
        acc[...] = acc_in[...]
    rows, width = df_ref.shape
    _, count, _, _ = out_ref.shape
    hidden = up_ref.shape[1]
    up_rows = width // count
    chunk = 384
    per_line = width // chunk

    def step(i, carry):
        cols = chunk_of(i, chunk)
        du = (dot_nt(df_ref[...], down_ref[cols, :]) * gp_ref[:, cols]).astype(BF16)
        bu_ref[:, cols] = jnp.sum(fold_rows(du.astype(F32)), axis=0, keepdims=True)
        value = dot_tn(hb_ref[...], du).astype(BF16)
        part, col = i // per_line, chunk_of(i % per_line, chunk)
        for a in range(count):
            spots = [spot_of(ids, 2 + n, kind, a, count) for n in range(PARTS)]
            spot = jnp.where(part == 0, spots[0], spots[1])
            out_ref[part, spot, :, col] = value[a * up_rows : (a + 1) * up_rows, :]
        acc[...] += dot_nt(du, up_ref[:, cols])
        return carry

    lax.fori_loop(0, hidden // chunk, step, 0, unroll=2)
    if kind == 0:
        fold_s[...] = jnp.zeros_like(fold_s)
        gain_row = row_of(gain_a)

        def norm(blk, carry):
            r = chunk_of(blk, LANES)
            grad = acc[r, :]
            normed = n_ref[r, :]
            fold_s[0] += fold_rows(grad * normed)
            fold_s[1] += fold_rows(grad)
            scaled = grad * gain_row
            mean_a = jnp.mean(scaled, axis=1, keepdims=True)
            mean_b = jnp.mean(scaled * normed, axis=1, keepdims=True)
            dr1 = (scaled - mean_a - normed * mean_b) * rstd_ref[r, 0:1]
            dr1_ref[r, :] = dr1
            da = dr1.astype(BF16)
            da_ref[r, :] = da
            fold_s[2] += fold_rows(da.astype(F32))
            return carry

        lax.fori_loop(0, rows // LANES, norm, 0, unroll=True)
        vec_ref[...] = jnp.sum(fold_s[...], axis=1)


def ffn_bwd(kind, ids, df, hb, gp, down, up, extra, count):
    rows, width = df.shape
    hidden = up.shape[1]
    outs = [shaped((hidden // width, count, width // count, width), BF16), shaped((1, hidden), F32)]
    scratch = []
    if kind == 1:
        outs += [shaped((rows, width), F32)]
    else:
        outs += [shaped((rows, width), F32), shaped((rows, width), BF16), shaped((3, width), F32)]
        scratch = [pltpu.VMEM((rows, width), F32), pltpu.VMEM((3, 8, width), F32)]
    return call(
        functools.partial(ffn_bwd_body, kind),
        outs,
        (ids,),
        (df, hb, gp, down, up, *extra),
        scratch,
        flops=6 * rows * width * hidden,
        moved=4 * rows * hidden + 6 * width * hidden + 10 * rows * width,
    )


def attn_bwd_body(
    kind, ids, bucket, lens, keep, qa_ref, k_ref, v_ref, o_ref, da_ref, wo_ref, w_ref, x_ref, bu_ref, va_ref, vf_ref, *rest
):
    if kind == 1:
        dr1_ref, g_ref, dw_ref, ig_ref, bm_s = rest
    else:
        ig_in, dw_ref, ig_ref, bm_s = rest
    rows, width = da_ref.shape
    pairs = k_ref.shape[0]
    local = pairs * LANES
    count = dw_ref.shape[1]
    size, out_size, wide = width // count, local // count, width // local
    _, bm_s[...] = mask_columns(ids, bucket, lens, rows)
    if kind == 1:
        for blk in range(rows // LANES):
            r = slice(blk * LANES, (blk + 1) * LANES)
            far = pl.ds(pl.multiple_of(ids[0] * rows + blk * LANES, LANES), LANES)
            kept = keep_of(ids, bucket, keep, blk)
            ig_ref[r, :] = dr1_ref[r, :] + jnp.where(kept, 0.0, g_ref[far, :].astype(F32))
    else:
        ig_ref[...] = ig_in[...]
    tile = rows // 2

    def pair(p, carry):
        cols = chunk_of(p, LANES)
        kp = k_ref[p]
        vp = v_ref[p]
        bm = bm_s[...]
        low_t, low_r = low_half(tile), low_half(rows)
        zero_t, zero_r = jnp.zeros((tile, LANES), BF16), jnp.zeros((rows, LANES), BF16)
        wo = wo_ref[cols, :]
        dk_sum = dv_sum = None
        dqs = []
        for rb in range(2):
            r = slice(rb * tile, (rb + 1) * tile)
            dop = dot_nt(da_ref[r, :], wo).astype(BF16)
            dq = None
            for par in range(2):
                own_t = low_t if par == 0 else jnp.logical_not(low_t)
                own_r = low_r if par == 0 else jnp.logical_not(low_r)
                qa = qa_ref[2 * p + par, r, :]
                doa = jnp.where(own_t, dop, zero_t)
                prob = jnp.exp(dot_nt(jnp.where(own_r, kp, bm), qa))
                dprob = dot_nt(vp, doa)
                inner = jnp.sum(prob * dprob, axis=0, keepdims=True)
                dscore = (prob * (dprob - inner)).astype(BF16)
                dv = dot_nn(prob.astype(BF16), doa)
                dk = dot_nn(dscore, jnp.where(own_t, qa, zero_t))
                dqp = dot_tn(dscore, jnp.where(own_r, kp, zero_r))
                dv_sum = dv if dv_sum is None else dv_sum + dv
                dk_sum = dk if dk_sum is None else dk_sum + dk
                dq = dqp if dq is None else dq + dqp
            dqs.append((dq * 0.125).astype(BF16))
        dqp = jnp.concatenate(dqs, axis=0)
        dvp = dv_sum.astype(BF16)
        grads = jnp.concatenate([dqp, dk_sum.astype(BF16), dvp], axis=1)
        weights = jnp.concatenate([w_ref[n, :, cols] for n in range(3)], axis=1)
        ig_ref[...] += dot_nt(grads, weights)
        value = dot_tn(x_ref[chunk_of(ids[0], rows), :], grads).astype(BF16)
        heads = jnp.concatenate([o_ref[n] for n in range(pairs)], axis=1)
        da = [da_ref[:, pl.ds(pl.multiple_of(n * local + p * LANES, LANES), LANES)] for n in range(wide)]
        out_value = dot_tn(heads, jnp.concatenate(da, axis=1)).astype(BF16)
        small = [jnp.sum(fold_rows(g.astype(F32)), axis=0, keepdims=True) for g in (dqp, dvp)]
        for ref in (bu_ref, va_ref, vf_ref):
            for n in range(ref.shape[0]):
                for c in range(0, ref.shape[1], local):
                    small.append(ref[n : n + 1, pl.ds(pl.multiple_of(c + p * LANES, LANES), LANES)])
        line = lax.broadcasted_iota(jnp.int32, (8, LANES), 0)
        for a in range(count):
            spots = [spot_of(ids, 4 + n, kind, a, count) for n in range(PARTS)]
            rows_a = slice(a * size, (a + 1) * size)
            dw_ref[0, spots[0], 0:size, cols] = value[rows_a, 0:LANES]
            dw_ref[0, spots[0], size : 2 * size, cols] = value[rows_a, LANES : 2 * LANES]
            dw_ref[1, spots[1], 0:size, cols] = value[rows_a, 2 * LANES :]
            for n in range(wide):
                part = out_value[a * out_size : (a + 1) * out_size, n * LANES : (n + 1) * LANES]
                at = size + n * out_size
                dw_ref[1, spots[1], at : at + out_size, cols] = part
            tile_s = jnp.zeros((8, LANES), F32)
            dw_ref[0, spots[0], 2 * size : 2 * size + 8, cols] = tile_s.astype(BF16)
            for n, row in enumerate(small[a::count]):
                tile_s = jnp.where(line == n, row, tile_s)
            dw_ref[1, spots[1], 2 * size : 2 * size + 8, cols] = tile_s.astype(BF16)
        return carry

    lax.fori_loop(0, pairs, pair, 0)


def attn_bwd(kind, scal, qa, k, v, o, da, wo, w, tokens, smalls, extra, count):
    rows, width = da.shape
    pairs = k.shape[0]
    local = pairs * LANES
    lines = 2 * width // count + 8
    return call(
        functools.partial(attn_bwd_body, kind),
        [shaped((PARTS, count, lines, local), BF16), shaped((rows, width), F32)],
        scal,
        (qa, k, v, o, da, wo, w, tokens, *smalls, *extra),
        [pltpu.VMEM((rows, LANES), BF16)],
        flops=2 * rows * local * (8 * width + 10 * rows),
        moved=2 * (rows * local * 4 + width * local * 7 + rows * width * 2) + 8 * rows * width,
        trans=2 * pairs * rows * rows,
    )


def place_body(part, first, count, plan, n_held, small_plan, ids, *refs):
    pieces = refs[: 1 if small_plan is None else 2]
    refs = refs[len(pieces) + n_held :]
    outs, refs = refs[: len(plan)], refs[len(plan) :]
    n_small = 0 if small_plan is None else len(small_plan)
    small_outs, refs = refs[:n_small], refs[n_small:]
    stages, sems = refs[:-1], refs[-1]
    half, lines, _ = pieces[0].shape
    copies = []
    for q in range(half):
        a = spot_of(ids, part, 2, first + q, count)
        for n, (parts, target) in enumerate(plan):
            for at, start, size in parts:
                stages[n][(q,) + at] = pieces[0][q, start : start + size, :].astype(F32)
            copy = pltpu.make_async_copy(stages[n].at[q], target(outs[n], a), sems.at[n, q])
            copy.start()
            copies.append(copy)
    for n in range(n_small):
        for line, c0, row in small_plan[n]:
            p = spot_of(ids, part, 3, row % count, count)
            high = pieces[0][p & (half - 1), lines - 8 :, :].astype(F32)
            low = pieces[1][p & (half - 1), lines - 8 :, :].astype(F32)
            tile = jnp.where(p < half, low, high)
            width = tile.shape[1]
            value = tile[row // count : row // count + 1, :]
            if line is None:
                small_outs[n][c0 : c0 + width] = value.reshape(width)
            else:
                small_outs[n][line : line + 1, c0 : c0 + width] = value
    for copy in copies:
        copy.wait()


def place(part, first, ids, pieces, plan, held=(), small_outs=(), small_plan=None):
    half = pieces[0].shape[0]
    outs = [shaped(entry[0], F32) for entry in plan]
    return call(
        functools.partial(place_body, part, first, 2 * half, [entry[2:] for entry in plan], len(held), small_plan),
        outs + list(small_outs),
        (ids,),
        (*pieces, *held),
        [pltpu.VMEM((half,) + entry[1], F32) for entry in plan] + [pltpu.SemaphoreType.DMA((len(outs), half))],
        moved=6 * half * pieces[0].shape[1] * pieces[0].shape[2],
        in_specs=[resident()] * len(pieces) + [anywhere()] * len(held),
        out_specs=[anywhere()] * len(outs) + [resident()] * len(small_outs),
        input_output_aliases={1 + len(pieces) + n: n for n in range(len(held))},
    )


def join_body(cores, ids, *refs):
    n = (len(refs) - 1) // 3
    owns, others, outs, sems = refs[:n], refs[n : 2 * n], refs[2 * n : 3 * n], refs[-1]
    copies = []
    for k in range(n):
        rows = owns[k].shape[0]
        for part, where in ((owns[k], ids[0]), (others[k], cores - 1 - ids[0])):
            target = outs[k].at[pl.ds(pl.multiple_of(where * rows, rows), rows), :]
            copies.append(pltpu.make_async_copy(part, target, sems.at[len(copies)]))
            copies[-1].start()
    for copy in copies:
        copy.wait()


def join(ids, cores, owns, others):
    return call(
        functools.partial(join_body, cores),
        [shaped((cores * o.shape[0], o.shape[1]), o.dtype) for o in owns],
        (ids,),
        (*owns, *others),
        [pltpu.SemaphoreType.DMA((2 * len(owns),))],
        moved=sum(4 * o.size * o.dtype.itemsize for o in owns),
        out_specs=[anywhere()] * len(owns),
    )


def swap_cores(array_in, cores):
    return lax.ppermute(array_in, "tensor", [(c, cores - 1 - c) for c in range(cores)])


class GroupSum:
    def __init__(self, mesh, batch, own, other_received):
        self.mesh, self.batch = mesh, batch
        self.halvings = own.shape[0].bit_length() - 1
        self.steps = 2 * self.halvings + 1
        self.terms = [own, other_received]
        self.at = 0
        self.sent = None

    def exchange(self, array_in, bit_of):
        groups, cores = self.mesh.shape["dp"], self.mesh.shape["tensor"]
        pairs = [(i * cores + c, (i ^ (1 << bit_of(c))) * cores + c) for i in range(groups) for c in range(cores)]
        return lax.ppermute(array_in, ("dp", "tensor"), pairs)

    def total(self, terms):
        acc = terms[0].astype(F32)
        for term in terms[1:]:
            acc = acc + term.astype(F32)
        return acc.astype(BF16)

    def step(self, *earlier):
        terms = self.terms
        if earlier:
            terms = terms[:-1] + [after(terms[-1], *earlier)]
        n = self.at
        if n < self.halvings:
            half = terms[0].shape[0] // 2
            self.sent = self.total([term[half:] for term in terms])
            received = self.exchange(self.sent, lambda c: step_bits(self.batch, c, 0, self.halvings)[n])
            self.terms = [term[:half] for term in terms] + [received]
        elif n == self.halvings:
            doublings = (self.mesh.shape["dp"] >> self.halvings).bit_length() - 1
            for k in range(doublings):
                self.sent = self.total(terms)
                terms = [self.sent, self.exchange(self.sent, lambda c, k=k: self.halvings + k)]
            self.terms = terms
        else:
            n -= self.halvings + 1
            self.sent = self.total(terms) if n == 0 else jnp.concatenate(terms, axis=0)
            received = self.exchange(self.sent, lambda c: step_bits(self.batch, c, 1, self.halvings)[n])
            self.terms = [self.sent, received]
        self.at += 1
        return self.sent


def per_device(
    mesh,
    tokens,
    w_qkv,
    bias_qv,
    w_out,
    bias_out,
    gain_attn,
    shift_attn,
    w_up,
    bias_up,
    w_down,
    bias_down,
    gain_ffn,
    shift_ffn,
    out_grad,
    bucket_len,
    seq_lengths,
    keep_mask,
):
    cores = mesh.shape["tensor"]
    count = min(8, mesh.shape["dp"])
    width = tokens.shape[1]
    rows = tokens.shape[0] // cores
    hidden = w_up.shape[1]
    local = w_qkv.shape[2]
    ids = jnp.where(jnp.arange(2) == 0, lax.axis_index("tensor"), lax.axis_index("dp")).astype(jnp.int32)

    w_qkv_o = swap_cores(w_qkv, cores)
    bias_qv_o = swap_cores(bias_qv, cores)
    w_out_o = swap_cores(w_out, cores)
    bias_up_o = swap_cores(bias_up, cores)
    w_up_o = swap_cores(w_up, cores)
    w_down_o = swap_cores(w_down, cores)

    attn_scal = (ids, bucket_len, seq_lengths)
    qa, k, v, o = attn_fwd(False, attn_scal, tokens, w_qkv, bias_qv, rows)
    qa_o, k_o, v_o, o_o, n1, rstd, hb = attn_fwd(
        True,
        attn_scal,
        tokens,
        w_qkv_o,
        bias_qv_o,
        rows,
        (o, w_out_o, w_out, bias_out, gain_attn, shift_attn),
    )
    keep_scal = (ids, bucket_len, keep_mask)
    vecs = (gain_attn, shift_attn, bias_down, gain_ffn, shift_ffn)
    gb, gb_o, gp, gp_o, mixed, dr2, df, vec_f = ffn_fwd(
        keep_scal, hb, n1, w_up, w_up_o, bias_up, bias_up_o, w_down, w_down_o, vecs, tokens, out_grad
    )
    mixed_o = swap_cores(mixed, cores)
    down_other = down_grad(1, ids, gb_o, df, count)
    down_got = swap_cores(down_other, cores)
    down_own = down_grad(0, ids, gb, after(df, down_other), count)
    sums = []

    def add_sums(own, received):
        for part in range(PARTS):
            sums.append(GroupSum(mesh, len(sums), own[part], received[part]))

    add_sums(down_own, down_got)
    landed, sents, final = [[], []], [[], []], [[], []]

    def exchange(parts, *earlier):
        which = parts[0] % 2
        earlier += tuple(landed[which]) + tuple(sents[1 - which])
        sents[which] = [sums[part].step(*earlier) for part in parts]
        landed[which] = final[which] + [sums[part].terms[-1] for part in parts if sums[part].at < sums[part].steps]
        final[which] = [sums[part].terms[-1] for part in parts if sums[part].at == sums[part].steps]

    def exchange_all(stage, *earlier):
        for parts in EARLY[stage]:
            exchange(parts, *earlier)
        return sents[0] + sents[1]

    sent = exchange_all(0, df)
    up_other, bu_o, dh = ffn_bwd(1, ids, after(df, *sent), hb, gp_o, w_down_o, w_up_o, (dr2,), count)
    up_got = swap_cores(up_other, cores)
    sent = exchange_all(1, dh)
    up_own, bu, dr1, da, vec_a = ffn_bwd(
        0, ids, after(df, *sent), hb, gp, w_down, w_up, (dh, n1, rstd, gain_attn), count
    )
    add_sums(up_own, up_got)
    sent = exchange_all(2, da)
    bwd_scal = (ids, bucket_len, seq_lengths, keep_mask)
    qkv_other, ig_part = attn_bwd(
        1, bwd_scal, qa_o, k_o, v_o, o_o, after(da, *sent), w_out_o, w_qkv_o, tokens,
        (bu_o, vec_a, vec_f), (dr1, out_grad), count,
    )
    qkv_got = swap_cores(qkv_other, cores)
    sent = exchange_all(3, ig_part, mixed_o)
    qkv_own, ig = attn_bwd(
        0, bwd_scal, qa, k, v, o, after(da, *sent), w_out, w_qkv, tokens, (bu, vec_a, vec_f), (ig_part,), count
    )
    ig_o = swap_cores(ig, cores)
    add_sums(qkv_own, qkv_got)

    def rows_at(each, size, shift=0, cols=slice(None)):
        def target(out, a):
            start = pl.multiple_of(a * each, each)
            return out.at[pl.ds(start + shift, size), cols]

        return target

    every = (slice(None), slice(None))
    size, out_size, wide = width // count, local // count, width // local
    half_rows = hidden // (count * PARTS)
    plans = []
    for part in range(PARTS):
        target = rows_at(PARTS * half_rows, half_rows, part * half_rows)
        plans.append([((hidden, width), (half_rows, width), [(every, 0, half_rows)], target)])
    for part in range(hidden // width):
        target = rows_at(size, size, 0, slice(part * width, (part + 1) * width))
        plans.append([((width, hidden), (size, width), [(every, 0, size)], target)])

    def planes_at(first, planes):
        return lambda out, a: out.at[first : first + planes, pl.ds(pl.multiple_of(a * size, size), size), :]

    shape = (3, width, local)
    plans.append([(shape, (2, size, local), [((n,) + every, n * size, size) for n in range(2)], planes_at(0, 2))])
    pieces = [((slice(None), slice(n * local, (n + 1) * local)), size + n * out_size, out_size) for n in range(wide)]
    plans.append(
        [
            (shape, (1, size, local), [((0,) + every, 0, size)], planes_at(2, 1)),
            ((local, width), (out_size, width), pieces, rows_at(out_size, out_size)),
        ]
    )
    per_up, per_norm = hidden // local, width // local
    small_plan = [[(n, 0, n) for n in range(2)], [(None, c * local, 2 + c) for c in range(per_up)]]
    for n in range(6):
        small_plan.append([(None, c * local, 2 + per_up + n * per_norm + c) for c in range(per_norm)])
    small_outs = [shaped((2, local), F32), shaped((hidden,), F32)] + [shaped((width,), F32)] * 6
    held = {0: [], 1: [], 2: []}
    small = []

    def put(part, late, *earlier):
        each = sums[part]
        pieces = [after(each.terms[1] if late else each.terms[0], *earlier)] if earlier else [each.terms[1 if late else 0]]
        first = count // 2 if late else 0
        batch = part // PARTS
        extra = held[batch][: len(plans[part])]
        if late and part == len(plans) - 1:
            placed = place(part, first, ids, pieces + [each.terms[0]], plans[part], extra, small_outs, small_plan)
            small.extend(placed[len(plans[part]) :])
            placed = placed[: len(plans[part])]
        else:
            placed = place(part, first, ids, pieces, plans[part], extra)
        held[batch] = list(placed) + held[batch][len(placed) :]
        return placed[0]

    put_early, put_late = set(), set()
    fillers = [ig]
    for turn, parts in enumerate(TURNS):
        active = [part for part in parts if sums[part].at < sums[part].steps]
        earlier, later = fillers, []
        if turn == JOIN_AT:
            out_mixed, out_ig = join(ids, cores, (mixed, after(ig, *sents[0])), (mixed_o, ig_o))
            later.append(out_ig)
        for part in parts:
            if sums[part].at == sums[part].steps and part not in put_late and part < 4:
                later.append(put(part, True, *landed[part % 2]))
                put_late.add(part)
        if active:
            exchange(active, *earlier)
        for part in parts:
            if sums[part].at == sums[part].steps and part not in put_early:
                put(part, False)
                put_early.add(part)
        fillers = later
    for part in range(len(plans)):
        if part not in put_late:
            put(part, True)
    grad_w_down, grad_w_up = held[0][0], held[1][0]
    grad_w_qkv, grad_w_out = held[2]
    grad_bias_qv, grad_bias_up, *norms = small
    return (
        out_mixed,
        out_ig,
        grad_w_qkv,
        grad_bias_qv,
        grad_w_out,
        norms[2],
        norms[0],
        norms[1],
        grad_w_up,
        grad_bias_up,
        grad_w_down,
        norms[5],
        norms[3],
        norms[4],
    )


def solution(mesh):
    in_specs = (
        P("dp", None),
        P(None, None, "tensor"),
        P(None, "tensor"),
        P("tensor", None),
        P(),
        P(),
        P(),
        P(None, "tensor"),
        P("tensor"),
        P("tensor", None),
        P(),
        P(),
        P(),
        P("dp", None),
        P("dp"),
        P("dp", None),
        P("dp", None),
    )
    out_specs = (
        P("dp", None),
        P("dp", None),
        P(None, None, "tensor"),
        P(None, "tensor"),
        P("tensor", None),
        P(),
        P(),
        P(),
        P(None, "tensor"),
        P("tensor"),
        P("tensor", None),
        P(),
        P(),
        P(),
    )
    return jax.shard_map(
        functools.partial(per_device, mesh),
        mesh=mesh,
        in_specs=in_specs,
        out_specs=out_specs,
        check_vma=False,
    )
```

```python
import functools

import jax
import jax.numpy as jnp
from jax import lax
from jax.experimental import pallas as pl
from jax.experimental.pallas import tpu as pltpu
from jax.sharding import PartitionSpec as P

HD = 64
BUCKET_LONG = 512
LANES = 128
EPS = 1e-05
F32 = jnp.float32
BF16 = jnp.bfloat16
NEG = -1e30
MIB = 1 << 20
VMEM_MIB = 16
COVER = 20

STEP_BITS = ((((1, 0, 2), (2, 1, 0)), ((0, 1, 2), (2, 0, 1))), (((1, 2, 0), (2, 1, 0)), ((0, 2, 1), (2, 0, 1))), (((0, 1, 2), (2, 0, 1)), ((1, 0, 2), (1, 0, 2))), (((0, 1, 2), (0, 2, 1)), ((1, 0, 2), (2, 1, 0))), (((0, 1, 2), (2, 0, 1)), ((1, 0, 2), (0, 1, 2))), (((0, 1, 2), (0, 1, 2)), ((1, 0, 2), (1, 2, 0))))
PARTS = 2
EARLY = (((0,), (1,)), ((0,),), ((0, 2), (1, 3)), ((0, 2), (1, 3)))
TURNS = ((4, 2, 0), (5, 3, 1)) * 7
JOIN_AT = 2


def dot_nn(left, right):
    return lax.dot_general(left, right, (((1,), (0,)), ((), ())), preferred_element_type=F32)


def dot_nt(left, right):
    return lax.dot_general(left, right, (((1,), (1,)), ((), ())), preferred_element_type=F32)


def dot_tn(left, right):
    return lax.dot_general(left, right, (((0,), (0,)), ((), ())), preferred_element_type=F32)


def resident():
    return pl.BlockSpec(memory_space=pltpu.VMEM)


def anywhere():
    return pl.BlockSpec(memory_space=pl.ANY)


def shaped(shape, dtype):
    return jax.ShapeDtypeStruct(shape, dtype)


def call(body, outs, scalars, operands, scratch=(), vmem=VMEM_MIB, flops=0, moved=0, trans=0, **kwargs):
    specs = kwargs.pop("in_specs", None) or [resident()] * len(operands)
    return pl.pallas_call(
        body,
        out_shape=outs,
        grid_spec=pltpu.PrefetchScalarGridSpec(
            num_scalar_prefetch=len(scalars),
            grid=(1,),
            in_specs=specs,
            out_specs=kwargs.pop("out_specs", None) or [resident()] * len(outs),
            scratch_shapes=list(scratch),
        ),
        compiler_params=pltpu.CompilerParams(dimension_semantics=("arbitrary",), vmem_limit_bytes=vmem * MIB),
        cost_estimate=pl.CostEstimate(flops=COVER * flops, bytes_accessed=moved, transcendentals=trans),
        **kwargs,
    )(*scalars, *operands)


def chunk_of(index, size):
    return pl.ds(pl.multiple_of(index * size, size), size)


def after(value, *earlier):
    return lax.optimization_barrier((value,) + earlier)[0]


def move_bits(number, pairs):
    out = 0
    for take, put in pairs:
        out = out | lax.shift_left(lax.shift_right_logical(number, take) & 1, put)
    return out


def step_bits(batch, core, gathering, steps):
    return [bit for bit in STEP_BITS[batch][core % 2][gathering] if bit < steps]


def spot_of(ids, batch, kind, number, count):
    steps = count.bit_length() - 1
    me = ids[1] & (count - 1)
    number = jnp.int32(number) if isinstance(number, int) else number
    spots = []
    for core in range(2):
        bits = step_bits(batch, 1 - core if kind == 1 else core, kind > 1, steps)
        places = range(steps) if kind > 1 else range(steps - 1, -1, -1)
        if kind == 2:
            spots.append(move_bits(number, zip(places, bits, strict=True)) ^ me)
        else:
            spots.append(move_bits(number ^ me, zip(bits, places, strict=True)))
    return jnp.where((ids[0] & 1) == 0, spots[0], spots[1])


def bucket_shift(bucket_ref):
    return jnp.where(bucket_ref[0] >= BUCKET_LONG, 9, 7)


def mask_columns(ids_ref, bucket_ref, lens_ref, rows):
    shift = bucket_shift(bucket_ref)
    first = ids_ref[0] * lax.shift_right_logical(BUCKET_LONG, shift)
    place = lax.broadcasted_iota(jnp.int32, (rows, LANES), 0)
    lane = lax.broadcasted_iota(jnp.int32, (rows, LANES), 1) & (HD - 1)
    seq = lax.shift_right_logical(place, jnp.full((rows, LANES), shift, jnp.int32))
    pos = place - lax.shift_left(seq, jnp.full((rows, LANES), shift, jnp.int32))
    length = jnp.full((rows, LANES), lens_ref[0, first], jnp.int32)
    for slot in range(1, 4):
        length = jnp.where(seq == slot, lens_ref[0, first + slot], length)
    hit = seq == lane
    query_cols = jnp.where(hit, 1.0, 0.0)
    key_cols = jnp.where(hit & (pos < length), 0.0, NEG)
    key_cols = jnp.where(lane < 4, key_cols, jnp.where(lane < 7, 1.0, 0.0))
    return query_cols.astype(BF16), key_cols.astype(BF16)


def low_half(rows):
    return lax.broadcasted_iota(jnp.int32, (rows, LANES), 1) < HD


def row_of(vec_ref):
    return vec_ref[...].reshape(1, -1)


def attn_fwd_body(last, ids, bucket, lens, x_ref, w_ref, b_ref, *rest):
    if last:
        (other_o, wo_own, wo_other, bias_out, gain, shift_vec) = rest[:6]
        qa_ref, k_ref, v_ref, o_ref, n_ref, rstd_ref, hb_ref = rest[6:13]
        am_s, bm_s = rest[13:]
    else:
        qa_ref, k_ref, v_ref, o_ref, am_s, bm_s, x_s, w_s, b_s, sems = rest
    pairs, rows, _ = k_ref.shape
    if not last:
        copies = [pltpu.make_async_copy(x_ref.at[chunk_of(ids[0], rows), :], x_s, sems.at[0])]
        copies.append(pltpu.make_async_copy(b_ref, b_s, sems.at[1]))
        for p in range(pairs):
            cols = slice(p * LANES, (p + 1) * LANES)
            copies.append(pltpu.make_async_copy(w_ref.at[:, :, cols], w_s.at[p], sems.at[2 + p]))
        for copy in copies:
            copy.start()
        b_ref = b_s
    am_s[...], bm_s[...] = mask_columns(ids, bucket, lens, rows)
    tile = rows // 2
    if not last:
        copies[0].wait()
        copies[1].wait()

    def pair(p, carry):
        cols = chunk_of(p, LANES)
        if last:
            weights = jnp.concatenate([w_ref[n, :, cols] for n in range(3)], axis=1)
            qkv = dot_nn(x_ref[chunk_of(ids[0], rows), :], weights)
        else:
            pltpu.make_async_copy(w_ref.at[:, :, slice(0, LANES)], w_s.at[p], sems.at[2 + p]).wait()
            qkv = dot_nn(x_s[...], jnp.concatenate([w_s[p, n] for n in range(3)], axis=1))
        qp = ((qkv[:, :LANES] + b_ref[0:1, cols]).astype(BF16).astype(F32) * 0.125).astype(BF16)
        kp = qkv[:, LANES : 2 * LANES].astype(BF16)
        vp = (qkv[:, 2 * LANES :] + b_ref[1:2, cols]).astype(BF16)
        k_ref[p] = kp
        v_ref[p] = vp
        bm = bm_s[...]
        low_r, low_t = low_half(rows), low_half(tile)
        lane = lax.broadcasted_iota(jnp.int32, (tile, LANES), 1) & (HD - 1)
        for rb in range(2):
            r = slice(rb * tile, (rb + 1) * tile)
            am = am_s[r, :]
            qpr = qp[r, :]
            sums = []
            for par in range(2):
                own_t = low_t if par == 0 else jnp.logical_not(low_t)
                own_r = low_r if par == 0 else jnp.logical_not(low_r)
                scores = dot_nt(jnp.where(own_t, qpr, am), jnp.where(own_r, kp, bm))
                top = jnp.max(scores, axis=1, keepdims=True)
                expo = jnp.exp(scores - top).astype(BF16)
                total = dot_nn(expo, jnp.where(own_r, vp, jnp.ones_like(vp)))
                sums.append(total)
                neg_log = -(top + jnp.log(jnp.where(own_t, 1.0, total)))
                hi = neg_log.astype(BF16)
                mid = (neg_log - hi.astype(F32)).astype(BF16)
                lo = (neg_log - hi.astype(F32) - mid.astype(F32)).astype(BF16)
                parts = jnp.where(lane == 4, hi, jnp.where(lane == 5, mid, jnp.where(lane == 6, lo, am)))
                qa_ref[2 * p + par, r, :] = jnp.where(own_t, qpr, parts)
            total = pltpu.roll(jnp.where(low_t, sums[1], sums[0]), HD, 1)
            o_ref[p, r, :] = (jnp.where(low_t, sums[0], sums[1]) / total).astype(BF16)
        return carry

    lax.fori_loop(0, pairs, pair, 0)
    if last:
        block = rows // 4
        gain_row, shift_row, bias_row = row_of(gain), row_of(shift_vec), row_of(bias_out)

        def norm(i, carry):
            r = chunk_of(i, block)
            heads = [o_ref[n, r, :] for n in range(pairs)] + [other_o[n, r, :] for n in range(pairs)]
            weights = jnp.concatenate([wo_own[...], wo_other[...]], axis=0)
            acc = dot_nn(jnp.concatenate(heads, axis=1), weights)
            acc += x_ref[pl.ds(pl.multiple_of(ids[0] * rows + i * block, block), block), :].astype(F32) + bias_row
            centre = acc - jnp.mean(acc, axis=1, keepdims=True)
            rstd = lax.rsqrt(jnp.mean(centre * centre, axis=1, keepdims=True) + EPS)
            normed = centre * rstd
            n_ref[r, :] = normed
            rstd_ref[r, :] = jnp.broadcast_to(rstd, (block, LANES))
            hb_ref[r, :] = (normed * gain_row + shift_row).astype(BF16)
            return carry

        lax.fori_loop(0, 4, norm, 0, unroll=True)


def attn_fwd(last, scal, tokens, w, b, rows, extra=()):
    width = tokens.shape[1]
    local = w.shape[2]
    pairs = local // LANES
    outs = [shaped((2 * pairs, rows, LANES), BF16)] + [shaped((pairs, rows, LANES), BF16)] * 3
    if last:
        outs += [shaped((rows, width), F32), shaped((rows, LANES), F32), shaped((rows, width), BF16)]
    scratch = [pltpu.VMEM((rows, LANES), BF16)] * 2
    specs = None
    if not last:
        scratch += [pltpu.VMEM((rows, width), BF16), pltpu.VMEM((pairs, 3, width, LANES), BF16)]
        scratch += [pltpu.VMEM(b.shape, F32), pltpu.SemaphoreType.DMA((2 + pairs,))]
        specs = [anywhere()] * 3
        tokens, w, b = (pltpu.with_memory_space_constraint(each, pltpu.HBM) for each in (tokens, w, b))
    return call(
        functools.partial(attn_fwd_body, last),
        outs,
        scal,
        (tokens, w, b, *extra),
        scratch,
        in_specs=specs,
        flops=2 * rows * local * (3 * width + 4 * rows + (2 * width if last else 0)),
        moved=2 * (rows * width + 3 * width * local + 5 * rows * local),
        trans=2 * pairs * rows * rows,
    )


def keep_of(ids, bucket, keep, block):
    shift = bucket_shift(bucket)
    first = ids[0] * lax.shift_right_logical(BUCKET_LONG, shift)
    return keep[0, first + lax.shift_right_logical(block * LANES, shift)] > 0


def fold_rows(array_in):
    rows, cols = array_in.shape
    return jnp.sum(array_in.reshape(rows // 8, 8, cols), axis=0)


def ffn_fwd_body(
    ids, bucket, keep, hb_ref, n_ref, up_own, up_other, bu_own, bu_other, down_own, down_other,
    gain_a, shift_a, bias_down, gain_f, shift_f, x_ref, g_ref,
    gb_own, gb_other, gp_own, gp_other, mixed_ref, dr2_ref, df_ref, vec_ref, acc, fold_s,
):
    rows, width = hb_ref.shape
    acc[...] = n_ref[...] * row_of(gain_a) + (row_of(shift_a) + row_of(bias_down))
    half = rows // 2
    chunk = 256

    def hidden(i, carry):
        cols = chunk_of(i, chunk)
        for r in range(2):
            rs = slice(r * half, (r + 1) * half)
            hb = hb_ref[rs, :]
            total = None
            for up, bu, down, gb, gp in (
                (up_own, bu_own, down_own, gb_own, gp_own),
                (up_other, bu_other, down_other, gb_other, gp_other),
            ):
                u = dot_nn(hb, up[:, cols]) + bu[cols].reshape(1, -1)
                cdf = 0.5 * (1.0 + lax.erf(u * 0.7071067811865476))
                pdf = jnp.exp(-0.5 * u * u) * 0.3989422804014327
                gp[rs, cols] = cdf + u * pdf
                act = (u * cdf).astype(BF16)
                gb[rs, cols] = act
                part = dot_nn(act, down[cols, :])
                total = part if total is None else total + part
            acc[rs, :] += total
        return carry

    lax.fori_loop(0, up_own.shape[1] // chunk, hidden, 0, unroll=2)
    fold_s[...] = jnp.zeros_like(fold_s)
    gain_row, shift_row = row_of(gain_f), row_of(shift_f)

    def norm(blk, carry):
        r = chunk_of(blk, LANES)
        far = pl.ds(pl.multiple_of(ids[0] * rows + blk * LANES, LANES), LANES)
        kept = keep_of(ids, bucket, keep, blk)
        res = acc[r, :]
        centre = res - jnp.mean(res, axis=1, keepdims=True)
        rstd = lax.rsqrt(jnp.mean(centre * centre, axis=1, keepdims=True) + EPS)
        normed = centre * rstd
        final = normed * gain_row + shift_row
        mixed_ref[r, :] = jnp.where(kept, final, x_ref[far, :].astype(F32)).astype(BF16)
        grad = jnp.where(kept, g_ref[far, :].astype(F32), 0.0)
        fold_s[0] += fold_rows(grad * normed)
        fold_s[1] += fold_rows(grad)
        scaled = grad * gain_row
        mean_a = jnp.mean(scaled, axis=1, keepdims=True)
        mean_b = jnp.mean(scaled * normed, axis=1, keepdims=True)
        dr2 = (scaled - mean_a - normed * mean_b) * rstd
        dr2_ref[r, :] = dr2
        df = dr2.astype(BF16)
        df_ref[r, :] = df
        fold_s[2] += fold_rows(df.astype(F32))
        return carry

    lax.fori_loop(0, rows // LANES, norm, 0, unroll=True)
    vec_ref[...] = jnp.sum(fold_s[...], axis=1)


def ffn_fwd(scal, hb, n1, up_own, up_other, bu_own, bu_other, down_own, down_other, vecs, tokens, out_grad):
    rows, width = hb.shape
    hidden = up_own.shape[1]
    outs = [
        shaped((rows, hidden), BF16), shaped((rows, hidden), BF16),
        shaped((rows, hidden), F32), shaped((rows, hidden), F32),
        shaped((rows, width), BF16), shaped((rows, width), F32), shaped((rows, width), BF16),
        shaped((3, width), F32),
    ]
    return call(
        ffn_fwd_body,
        outs,
        scal,
        (hb, n1, up_own, up_other, bu_own, bu_other, down_own, down_other, *vecs, tokens, out_grad),
        [pltpu.VMEM((rows, width), F32), pltpu.VMEM((3, 8, width), F32)],
        flops=8 * rows * width * hidden,
        moved=12 * rows * hidden + 8 * width * hidden + 20 * rows * width,
        trans=4 * rows * hidden,
    )


def down_grad_body(kind, ids, gb_ref, df_ref, out_ref):
    _, count, size, _ = out_ref.shape
    per = 2 if count % 2 == 0 else 1

    def step(i, carry):
        value = dot_tn(gb_ref[:, chunk_of(i, per * PARTS * size)], df_ref[...]).astype(BF16)
        for c in range(per):
            for part in range(PARTS):
                first = (c * PARTS + part) * size
                out_ref[part, spot_of(ids, part, kind, i * per + c, count)] = value[first : first + size, :]
        return carry

    lax.fori_loop(0, count // per, step, 0, unroll=4)


def down_grad(kind, ids, gb, df, count):
    rows, width = df.shape
    hidden = gb.shape[1]
    return call(
        functools.partial(down_grad_body, kind),
        [shaped((PARTS, count, hidden // (count * PARTS), width), BF16)],
        (ids,),
        (gb, df),
        flops=2 * rows * width * hidden,
        moved=2 * rows * hidden + 2 * width * hidden + 2 * rows * width,
    )[0]


def ffn_bwd_body(kind, ids, df_ref, hb_ref, gp_ref, down_ref, up_ref, *rest):
    if kind == 1:
        dr2_ref, out_ref, bu_ref, acc = rest
        acc[...] = dr2_ref[...]
    else:
        acc_in, n_ref, rstd_ref, gain_a, out_ref, bu_ref, dr1_ref, da_ref, vec_ref, acc, fold_s = rest
        acc[...] = acc_in[...]
    rows, width = df_ref.shape
    _, count, _, _ = out_ref.shape
    hidden = up_ref.shape[1]
    up_rows = width // count
    chunk = 384
    per_line = width // chunk

    def step(i, carry):
        cols = chunk_of(i, chunk)
        du = (dot_nt(df_ref[...], down_ref[cols, :]) * gp_ref[:, cols]).astype(BF16)
        bu_ref[:, cols] = jnp.sum(fold_rows(du.astype(F32)), axis=0, keepdims=True)
        value = dot_tn(hb_ref[...], du).astype(BF16)
        part, col = i // per_line, chunk_of(i % per_line, chunk)
        for a in range(count):
            spots = [spot_of(ids, 2 + n, kind, a, count) for n in range(PARTS)]
            spot = jnp.where(part == 0, spots[0], spots[1])
            out_ref[part, spot, :, col] = value[a * up_rows : (a + 1) * up_rows, :]
        acc[...] += dot_nt(du, up_ref[:, cols])
        return carry

    lax.fori_loop(0, hidden // chunk, step, 0, unroll=2)
    if kind == 0:
        fold_s[...] = jnp.zeros_like(fold_s)
        gain_row = row_of(gain_a)

        def norm(blk, carry):
            r = chunk_of(blk, LANES)
            grad = acc[r, :]
            normed = n_ref[r, :]
            fold_s[0] += fold_rows(grad * normed)
            fold_s[1] += fold_rows(grad)
            scaled = grad * gain_row
            mean_a = jnp.mean(scaled, axis=1, keepdims=True)
            mean_b = jnp.mean(scaled * normed, axis=1, keepdims=True)
            dr1 = (scaled - mean_a - normed * mean_b) * rstd_ref[r, 0:1]
            dr1_ref[r, :] = dr1
            da = dr1.astype(BF16)
            da_ref[r, :] = da
            fold_s[2] += fold_rows(da.astype(F32))
            return carry

        lax.fori_loop(0, rows // LANES, norm, 0, unroll=True)
        vec_ref[...] = jnp.sum(fold_s[...], axis=1)


def ffn_bwd(kind, ids, df, hb, gp, down, up, extra, count):
    rows, width = df.shape
    hidden = up.shape[1]
    outs = [shaped((hidden // width, count, width // count, width), BF16), shaped((1, hidden), F32)]
    scratch = []
    if kind == 1:
        outs += [shaped((rows, width), F32)]
    else:
        outs += [shaped((rows, width), F32), shaped((rows, width), BF16), shaped((3, width), F32)]
        scratch = [pltpu.VMEM((rows, width), F32), pltpu.VMEM((3, 8, width), F32)]
    return call(
        functools.partial(ffn_bwd_body, kind),
        outs,
        (ids,),
        (df, hb, gp, down, up, *extra),
        scratch,
        flops=6 * rows * width * hidden,
        moved=4 * rows * hidden + 6 * width * hidden + 10 * rows * width,
    )


def attn_bwd_body(
    kind, ids, bucket, lens, keep, qa_ref, k_ref, v_ref, o_ref, da_ref, wo_ref, w_ref, x_ref, bu_ref, va_ref, vf_ref, *rest
):
    if kind == 1:
        dr1_ref, g_ref, dw_ref, ig_ref, bm_s = rest
    else:
        ig_in, dw_ref, ig_ref, bm_s = rest
    rows, width = da_ref.shape
    pairs = k_ref.shape[0]
    local = pairs * LANES
    count = dw_ref.shape[1]
    size, out_size, wide = width // count, local // count, width // local
    _, bm_s[...] = mask_columns(ids, bucket, lens, rows)
    if kind == 1:
        for blk in range(rows // LANES):
            r = slice(blk * LANES, (blk + 1) * LANES)
            far = pl.ds(pl.multiple_of(ids[0] * rows + blk * LANES, LANES), LANES)
            kept = keep_of(ids, bucket, keep, blk)
            ig_ref[r, :] = dr1_ref[r, :] + jnp.where(kept, 0.0, g_ref[far, :].astype(F32))
    else:
        ig_ref[...] = ig_in[...]
    tile = rows // 2

    def pair(p, carry):
        cols = chunk_of(p, LANES)
        kp = k_ref[p]
        vp = v_ref[p]
        bm = bm_s[...]
        low_t, low_r = low_half(tile), low_half(rows)
        zero_t, zero_r = jnp.zeros((tile, LANES), BF16), jnp.zeros((rows, LANES), BF16)
        wo = wo_ref[cols, :]
        dk_sum = dv_sum = None
        dqs = []
        for rb in range(2):
            r = slice(rb * tile, (rb + 1) * tile)
            dop = dot_nt(da_ref[r, :], wo).astype(BF16)
            dq = None
            for par in range(2):
                own_t = low_t if par == 0 else jnp.logical_not(low_t)
                own_r = low_r if par == 0 else jnp.logical_not(low_r)
                qa = qa_ref[2 * p + par, r, :]
                doa = jnp.where(own_t, dop, zero_t)
                prob = jnp.exp(dot_nt(jnp.where(own_r, kp, bm), qa))
                dprob = dot_nt(vp, doa)
                inner = jnp.sum(prob * dprob, axis=0, keepdims=True)
                dscore = (prob * (dprob - inner)).astype(BF16)
                dv = dot_nn(prob.astype(BF16), doa)
                dk = dot_nn(dscore, jnp.where(own_t, qa, zero_t))
                dqp = dot_tn(dscore, jnp.where(own_r, kp, zero_r))
                dv_sum = dv if dv_sum is None else dv_sum + dv
                dk_sum = dk if dk_sum is None else dk_sum + dk
                dq = dqp if dq is None else dq + dqp
            dqs.append((dq * 0.125).astype(BF16))
        dqp = jnp.concatenate(dqs, axis=0)
        dvp = dv_sum.astype(BF16)
        grads = jnp.concatenate([dqp, dk_sum.astype(BF16), dvp], axis=1)
        weights = jnp.concatenate([w_ref[n, :, cols] for n in range(3)], axis=1)
        ig_ref[...] += dot_nt(grads, weights)
        value = dot_tn(x_ref[chunk_of(ids[0], rows), :], grads).astype(BF16)
        heads = jnp.concatenate([o_ref[n] for n in range(pairs)], axis=1)
        da = [da_ref[:, pl.ds(pl.multiple_of(n * local + p * LANES, LANES), LANES)] for n in range(wide)]
        out_value = dot_tn(heads, jnp.concatenate(da, axis=1)).astype(BF16)
        small = [jnp.sum(fold_rows(g.astype(F32)), axis=0, keepdims=True) for g in (dqp, dvp)]
        for ref in (bu_ref, va_ref, vf_ref):
            for n in range(ref.shape[0]):
                for c in range(0, ref.shape[1], local):
                    small.append(ref[n : n + 1, pl.ds(pl.multiple_of(c + p * LANES, LANES), LANES)])
        line = lax.broadcasted_iota(jnp.int32, (8, LANES), 0)
        for a in range(count):
            spots = [spot_of(ids, 4 + n, kind, a, count) for n in range(PARTS)]
            rows_a = slice(a * size, (a + 1) * size)
            dw_ref[0, spots[0], 0:size, cols] = value[rows_a, 0:LANES]
            dw_ref[0, spots[0], size : 2 * size, cols] = value[rows_a, LANES : 2 * LANES]
            dw_ref[1, spots[1], 0:size, cols] = value[rows_a, 2 * LANES :]
            for n in range(wide):
                part = out_value[a * out_size : (a + 1) * out_size, n * LANES : (n + 1) * LANES]
                at = size + n * out_size
                dw_ref[1, spots[1], at : at + out_size, cols] = part
            tile_s = jnp.zeros((8, LANES), F32)
            dw_ref[0, spots[0], 2 * size : 2 * size + 8, cols] = tile_s.astype(BF16)
            for n, row in enumerate(small[a::count]):
                tile_s = jnp.where(line == n, row, tile_s)
            dw_ref[1, spots[1], 2 * size : 2 * size + 8, cols] = tile_s.astype(BF16)
        return carry

    lax.fori_loop(0, pairs, pair, 0)


def attn_bwd(kind, scal, qa, k, v, o, da, wo, w, tokens, smalls, extra, count):
    rows, width = da.shape
    pairs = k.shape[0]
    local = pairs * LANES
    lines = 2 * width // count + 8
    return call(
        functools.partial(attn_bwd_body, kind),
        [shaped((PARTS, count, lines, local), BF16), shaped((rows, width), F32)],
        scal,
        (qa, k, v, o, da, wo, w, tokens, *smalls, *extra),
        [pltpu.VMEM((rows, LANES), BF16)],
        flops=2 * rows * local * (8 * width + 10 * rows),
        moved=2 * (rows * local * 4 + width * local * 7 + rows * width * 2) + 8 * rows * width,
        trans=2 * pairs * rows * rows,
    )


def place_body(part, first, count, plan, n_held, small_plan, ids, *refs):
    pieces = refs[: 1 if small_plan is None else 2]
    refs = refs[len(pieces) + n_held :]
    outs, refs = refs[: len(plan)], refs[len(plan) :]
    n_small = 0 if small_plan is None else len(small_plan)
    small_outs, refs = refs[:n_small], refs[n_small:]
    stages, sems = refs[:-1], refs[-1]
    half, lines, _ = pieces[0].shape
    copies = []
    for q in range(half):
        a = spot_of(ids, part, 2, first + q, count)
        for n, (parts, target) in enumerate(plan):
            for at, start, size in parts:
                stages[n][(q,) + at] = pieces[0][q, start : start + size, :].astype(F32)
            copy = pltpu.make_async_copy(stages[n].at[q], target(outs[n], a), sems.at[n, q])
            copy.start()
            copies.append(copy)
    for n in range(n_small):
        for line, c0, row in small_plan[n]:
            p = spot_of(ids, part, 3, row % count, count)
            high = pieces[0][p & (half - 1), lines - 8 :, :].astype(F32)
            low = pieces[1][p & (half - 1), lines - 8 :, :].astype(F32)
            tile = jnp.where(p < half, low, high)
            width = tile.shape[1]
            value = tile[row // count : row // count + 1, :]
            if line is None:
                small_outs[n][c0 : c0 + width] = value.reshape(width)
            else:
                small_outs[n][line : line + 1, c0 : c0 + width] = value
    for copy in copies:
        copy.wait()


def place(part, first, ids, pieces, plan, held=(), small_outs=(), small_plan=None):
    half = pieces[0].shape[0]
    outs = [shaped(entry[0], F32) for entry in plan]
    return call(
        functools.partial(place_body, part, first, 2 * half, [entry[2:] for entry in plan], len(held), small_plan),
        outs + list(small_outs),
        (ids,),
        (*pieces, *held),
        [pltpu.VMEM((half,) + entry[1], F32) for entry in plan] + [pltpu.SemaphoreType.DMA((len(outs), half))],
        moved=6 * half * pieces[0].shape[1] * pieces[0].shape[2],
        in_specs=[resident()] * len(pieces) + [anywhere()] * len(held),
        out_specs=[anywhere()] * len(outs) + [resident()] * len(small_outs),
        input_output_aliases={1 + len(pieces) + n: n for n in range(len(held))},
    )


def join_body(cores, ids, *refs):
    n = (len(refs) - 1) // 3
    owns, others, outs, sems = refs[:n], refs[n : 2 * n], refs[2 * n : 3 * n], refs[-1]
    copies = []
    for k in range(n):
        rows = owns[k].shape[0]
        for part, where in ((owns[k], ids[0]), (others[k], cores - 1 - ids[0])):
            target = outs[k].at[pl.ds(pl.multiple_of(where * rows, rows), rows), :]
            copies.append(pltpu.make_async_copy(part, target, sems.at[len(copies)]))
            copies[-1].start()
    for copy in copies:
        copy.wait()


def join(ids, cores, owns, others):
    return call(
        functools.partial(join_body, cores),
        [shaped((cores * o.shape[0], o.shape[1]), o.dtype) for o in owns],
        (ids,),
        (*owns, *others),
        [pltpu.SemaphoreType.DMA((2 * len(owns),))],
        moved=sum(4 * o.size * o.dtype.itemsize for o in owns),
        out_specs=[anywhere()] * len(owns),
    )


def swap_cores(array_in, cores):
    return lax.ppermute(array_in, "tensor", [(c, cores - 1 - c) for c in range(cores)])


class GroupSum:
    def __init__(self, mesh, batch, own, other_received):
        self.mesh, self.batch = mesh, batch
        self.halvings = own.shape[0].bit_length() - 1
        self.steps = 2 * self.halvings + 1
        self.terms = [own, other_received]
        self.at = 0
        self.sent = None

    def exchange(self, array_in, bit_of):
        groups, cores = self.mesh.shape["dp"], self.mesh.shape["tensor"]
        pairs = [(i * cores + c, (i ^ (1 << bit_of(c))) * cores + c) for i in range(groups) for c in range(cores)]
        return lax.ppermute(array_in, ("dp", "tensor"), pairs)

    def total(self, terms):
        acc = terms[0].astype(F32)
        for term in terms[1:]:
            acc = acc + term.astype(F32)
        return acc.astype(BF16)

    def step(self, *earlier):
        terms = self.terms
        if earlier:
            terms = terms[:-1] + [after(terms[-1], *earlier)]
        n = self.at
        if n < self.halvings:
            half = terms[0].shape[0] // 2
            self.sent = self.total([term[half:] for term in terms])
            received = self.exchange(self.sent, lambda c: step_bits(self.batch, c, 0, self.halvings)[n])
            self.terms = [term[:half] for term in terms] + [received]
        elif n == self.halvings:
            doublings = (self.mesh.shape["dp"] >> self.halvings).bit_length() - 1
            for k in range(doublings):
                self.sent = self.total(terms)
                terms = [self.sent, self.exchange(self.sent, lambda c, k=k: self.halvings + k)]
            self.terms = terms
        else:
            n -= self.halvings + 1
            self.sent = self.total(terms) if n == 0 else jnp.concatenate(terms, axis=0)
            received = self.exchange(self.sent, lambda c: step_bits(self.batch, c, 1, self.halvings)[n])
            self.terms = [self.sent, received]
        self.at += 1
        return self.sent


def per_device(
    mesh,
    tokens,
    w_qkv,
    bias_qv,
    w_out,
    bias_out,
    gain_attn,
    shift_attn,
    w_up,
    bias_up,
    w_down,
    bias_down,
    gain_ffn,
    shift_ffn,
    out_grad,
    bucket_len,
    seq_lengths,
    keep_mask,
):
    cores = mesh.shape["tensor"]
    count = min(8, mesh.shape["dp"])
    width = tokens.shape[1]
    rows = tokens.shape[0] // cores
    hidden = w_up.shape[1]
    local = w_qkv.shape[2]
    ids = jnp.where(jnp.arange(2) == 0, lax.axis_index("tensor"), lax.axis_index("dp")).astype(jnp.int32)

    w_qkv_o = swap_cores(w_qkv, cores)
    bias_qv_o = swap_cores(bias_qv, cores)
    w_out_o = swap_cores(w_out, cores)
    bias_up_o = swap_cores(bias_up, cores)
    w_up_o = swap_cores(w_up, cores)
    w_down_o = swap_cores(w_down, cores)

    attn_scal = (ids, bucket_len, seq_lengths)
    qa, k, v, o = attn_fwd(False, attn_scal, tokens, w_qkv, bias_qv, rows)
    qa_o, k_o, v_o, o_o, n1, rstd, hb = attn_fwd(
        True,
        attn_scal,
        tokens,
        w_qkv_o,
        bias_qv_o,
        rows,
        (o, w_out_o, w_out, bias_out, gain_attn, shift_attn),
    )
    keep_scal = (ids, bucket_len, keep_mask)
    vecs = (gain_attn, shift_attn, bias_down, gain_ffn, shift_ffn)
    gb, gb_o, gp, gp_o, mixed, dr2, df, vec_f = ffn_fwd(
        keep_scal, hb, n1, w_up, w_up_o, bias_up, bias_up_o, w_down, w_down_o, vecs, tokens, out_grad
    )
    mixed_o = swap_cores(mixed, cores)
    down_other = down_grad(1, ids, gb_o, df, count)
    down_got = swap_cores(down_other, cores)
    down_own = down_grad(0, ids, gb, after(df, down_other), count)
    sums = []

    def add_sums(own, received):
        for part in range(PARTS):
            sums.append(GroupSum(mesh, len(sums), own[part], received[part]))

    add_sums(down_own, down_got)
    landed, sents, final = [[], []], [[], []], [[], []]

    def exchange(parts, *earlier):
        which = parts[0] % 2
        earlier += tuple(landed[which]) + tuple(sents[1 - which])
        sents[which] = [sums[part].step(*earlier) for part in parts]
        landed[which] = final[which] + [sums[part].terms[-1] for part in parts if sums[part].at < sums[part].steps]
        final[which] = [sums[part].terms[-1] for part in parts if sums[part].at == sums[part].steps]

    def exchange_all(stage, *earlier):
        for parts in EARLY[stage]:
            exchange(parts, *earlier)
        return sents[0] + sents[1]

    sent = exchange_all(0, df)
    up_other, bu_o, dh = ffn_bwd(1, ids, after(df, *sent), hb, gp_o, w_down_o, w_up_o, (dr2,), count)
    up_got = swap_cores(up_other, cores)
    sent = exchange_all(1, dh)
    up_own, bu, dr1, da, vec_a = ffn_bwd(
        0, ids, after(df, *sent), hb, gp, w_down, w_up, (dh, n1, rstd, gain_attn), count
    )
    add_sums(up_own, up_got)
    sent = exchange_all(2, da)
    bwd_scal = (ids, bucket_len, seq_lengths, keep_mask)
    qkv_other, ig_part = attn_bwd(
        1, bwd_scal, qa_o, k_o, v_o, o_o, after(da, *sent), w_out_o, w_qkv_o, tokens,
        (bu_o, vec_a, vec_f), (dr1, out_grad), count,
    )
    qkv_got = swap_cores(qkv_other, cores)
    sent = exchange_all(3, ig_part, mixed_o)
    qkv_own, ig = attn_bwd(
        0, bwd_scal, qa, k, v, o, after(da, *sent), w_out, w_qkv, tokens, (bu, vec_a, vec_f), (ig_part,), count
    )
    ig_o = swap_cores(ig, cores)
    add_sums(qkv_own, qkv_got)

    def rows_at(each, size, shift=0, cols=slice(None)):
        def target(out, a):
            start = pl.multiple_of(a * each, each)
            return out.at[pl.ds(start + shift, size), cols]

        return target

    every = (slice(None), slice(None))
    size, out_size, wide = width // count, local // count, width // local
    half_rows = hidden // (count * PARTS)
    plans = []
    for part in range(PARTS):
        target = rows_at(PARTS * half_rows, half_rows, part * half_rows)
        plans.append([((hidden, width), (half_rows, width), [(every, 0, half_rows)], target)])
    for part in range(hidden // width):
        target = rows_at(size, size, 0, slice(part * width, (part + 1) * width))
        plans.append([((width, hidden), (size, width), [(every, 0, size)], target)])

    def planes_at(first, planes):
        return lambda out, a: out.at[first : first + planes, pl.ds(pl.multiple_of(a * size, size), size), :]

    shape = (3, width, local)
    plans.append([(shape, (2, size, local), [((n,) + every, n * size, size) for n in range(2)], planes_at(0, 2))])
    pieces = [((slice(None), slice(n * local, (n + 1) * local)), size + n * out_size, out_size) for n in range(wide)]
    plans.append(
        [
            (shape, (1, size, local), [((0,) + every, 0, size)], planes_at(2, 1)),
            ((local, width), (out_size, width), pieces, rows_at(out_size, out_size)),
        ]
    )
    per_up, per_norm = hidden // local, width // local
    small_plan = [[(n, 0, n) for n in range(2)], [(None, c * local, 2 + c) for c in range(per_up)]]
    for n in range(6):
        small_plan.append([(None, c * local, 2 + per_up + n * per_norm + c) for c in range(per_norm)])
    small_outs = [shaped((2, local), F32), shaped((hidden,), F32)] + [shaped((width,), F32)] * 6
    held = {0: [], 1: [], 2: []}
    small = []

    def put(part, late, *earlier):
        each = sums[part]
        pieces = [after(each.terms[1] if late else each.terms[0], *earlier)] if earlier else [each.terms[1 if late else 0]]
        first = count // 2 if late else 0
        batch = part // PARTS
        extra = held[batch][: len(plans[part])]
        if late and part == len(plans) - 1:
            placed = place(part, first, ids, pieces + [each.terms[0]], plans[part], extra, small_outs, small_plan)
            small.extend(placed[len(plans[part]) :])
            placed = placed[: len(plans[part])]
        else:
            placed = place(part, first, ids, pieces, plans[part], extra)
        held[batch] = list(placed) + held[batch][len(placed) :]
        return placed[0]

    put_early, put_late = set(), set()
    fillers = [ig]
    for turn, parts in enumerate(TURNS):
        active = [part for part in parts if sums[part].at < sums[part].steps]
        earlier, later = fillers, []
        if turn == JOIN_AT:
            out_mixed, out_ig = join(ids, cores, (mixed, after(ig, *sents[0])), (mixed_o, ig_o))
            later.append(out_ig)
        for part in parts:
            if sums[part].at == sums[part].steps and part not in put_late and part < 4:
                later.append(put(part, True, *landed[part % 2]))
                put_late.add(part)
        if active:
            exchange(active, *earlier)
        for part in parts:
            if sums[part].at == sums[part].steps and part not in put_early:
                put(part, False)
                put_early.add(part)
        fillers = later
    for part in range(len(plans)):
        if part not in put_late:
            put(part, True)
    grad_w_down, grad_w_up = held[0][0], held[1][0]
    grad_w_qkv, grad_w_out = held[2]
    grad_bias_qv, grad_bias_up, *norms = small
    return (
        out_mixed,
        out_ig,
        grad_w_qkv,
        grad_bias_qv,
        grad_w_out,
        norms[2],
        norms[0],
        norms[1],
        grad_w_up,
        grad_bias_up,
        grad_w_down,
        norms[5],
        norms[3],
        norms[4],
    )


def solution(mesh):
    in_specs = (
        P("dp", None),
        P(None, None, "tensor"),
        P(None, "tensor"),
        P("tensor", None),
        P(),
        P(),
        P(),
        P(None, "tensor"),
        P("tensor"),
        P("tensor", None),
        P(),
        P(),
        P(),
        P("dp", None),
        P("dp"),
        P("dp", None),
        P("dp", None),
    )
    out_specs = (
        P("dp", None),
        P("dp", None),
        P(None, None, "tensor"),
        P(None, "tensor"),
        P("tensor", None),
        P(),
        P(),
        P(),
        P(None, "tensor"),
        P("tensor"),
        P("tensor", None),
        P(),
        P(),
        P(),
    )
    return jax.shard_map(
        functools.partial(per_device, mesh),
        mesh=mesh,
        in_specs=in_specs,
        out_specs=out_specs,
        check_vma=False,
    )
```

```python
import functools

import jax
import jax.numpy as jnp
from jax import lax
from jax.experimental import pallas as pl
from jax.experimental.pallas import tpu as pltpu
from jax.sharding import PartitionSpec as P

HD = 64
BUCKET_LONG = 512
LANES = 128
EPS = 1e-05
F32 = jnp.float32
BF16 = jnp.bfloat16
NEG = -1e30
MIB = 1 << 20
VMEM_MIB = 16
COVER = 20

STEP_BITS = ((((1, 0, 2), (2, 1, 0)), ((0, 1, 2), (2, 0, 1))), (((1, 2, 0), (2, 1, 0)), ((0, 2, 1), (2, 0, 1))), (((0, 1, 2), (2, 0, 1)), ((1, 0, 2), (1, 0, 2))), (((0, 1, 2), (0, 2, 1)), ((1, 0, 2), (2, 1, 0))), (((0, 1, 2), (2, 0, 1)), ((1, 0, 2), (0, 1, 2))), (((0, 1, 2), (0, 1, 2)), ((1, 0, 2), (1, 2, 0))))
PARTS = 2
EARLY = (((0,), (1,)), ((0,),), ((0, 2), (1, 3)), ((0, 2), (1, 3)))
TURNS = ((4, 2, 0), (5, 3, 1)) * 7
JOIN_AT = 2


def dot_nn(left, right):
    return lax.dot_general(left, right, (((1,), (0,)), ((), ())), preferred_element_type=F32)


def dot_nt(left, right):
    return lax.dot_general(left, right, (((1,), (1,)), ((), ())), preferred_element_type=F32)


def dot_tn(left, right):
    return lax.dot_general(left, right, (((0,), (0,)), ((), ())), preferred_element_type=F32)


def resident():
    return pl.BlockSpec(memory_space=pltpu.VMEM)


def anywhere():
    return pl.BlockSpec(memory_space=pl.ANY)


def shaped(shape, dtype):
    return jax.ShapeDtypeStruct(shape, dtype)


def call(body, outs, scalars, operands, scratch=(), vmem=VMEM_MIB, flops=0, moved=0, trans=0, **kwargs):
    specs = kwargs.pop("in_specs", None) or [resident()] * len(operands)
    return pl.pallas_call(
        body,
        out_shape=outs,
        grid_spec=pltpu.PrefetchScalarGridSpec(
            num_scalar_prefetch=len(scalars),
            grid=(1,),
            in_specs=specs,
            out_specs=kwargs.pop("out_specs", None) or [resident()] * len(outs),
            scratch_shapes=list(scratch),
        ),
        compiler_params=pltpu.CompilerParams(dimension_semantics=("arbitrary",), vmem_limit_bytes=vmem * MIB),
        cost_estimate=pl.CostEstimate(flops=COVER * flops, bytes_accessed=moved, transcendentals=trans),
        **kwargs,
    )(*scalars, *operands)


def chunk_of(index, size):
    return pl.ds(pl.multiple_of(index * size, size), size)


def after(value, *earlier):
    return lax.optimization_barrier((value,) + earlier)[0]


def move_bits(number, pairs):
    out = 0
    for take, put in pairs:
        out = out | lax.shift_left(lax.shift_right_logical(number, take) & 1, put)
    return out


def step_bits(batch, core, gathering, steps):
    return [bit for bit in STEP_BITS[batch][core % 2][gathering] if bit < steps]


def spot_of(ids, batch, kind, number, count):
    steps = count.bit_length() - 1
    me = ids[1] & (count - 1)
    number = jnp.int32(number) if isinstance(number, int) else number
    spots = []
    for core in range(2):
        bits = step_bits(batch, 1 - core if kind == 1 else core, kind > 1, steps)
        places = range(steps) if kind > 1 else range(steps - 1, -1, -1)
        if kind == 2:
            spots.append(move_bits(number, zip(places, bits, strict=True)) ^ me)
        else:
            spots.append(move_bits(number ^ me, zip(bits, places, strict=True)))
    return jnp.where((ids[0] & 1) == 0, spots[0], spots[1])


def bucket_shift(bucket_ref):
    return jnp.where(bucket_ref[0] >= BUCKET_LONG, 9, 7)


def mask_columns(ids_ref, bucket_ref, lens_ref, rows):
    shift = bucket_shift(bucket_ref)
    first = ids_ref[0] * lax.shift_right_logical(BUCKET_LONG, shift)
    place = lax.broadcasted_iota(jnp.int32, (rows, LANES), 0)
    lane = lax.broadcasted_iota(jnp.int32, (rows, LANES), 1) & (HD - 1)
    seq = lax.shift_right_logical(place, jnp.full((rows, LANES), shift, jnp.int32))
    pos = place - lax.shift_left(seq, jnp.full((rows, LANES), shift, jnp.int32))
    length = jnp.full((rows, LANES), lens_ref[0, first], jnp.int32)
    for slot in range(1, 4):
        length = jnp.where(seq == slot, lens_ref[0, first + slot], length)
    hit = seq == lane
    query_cols = jnp.where(hit, 1.0, 0.0)
    key_cols = jnp.where(hit & (pos < length), 0.0, NEG)
    key_cols = jnp.where(lane < 4, key_cols, jnp.where(lane < 7, 1.0, 0.0))
    return query_cols.astype(BF16), key_cols.astype(BF16)


def low_half(rows):
    return lax.broadcasted_iota(jnp.int32, (rows, LANES), 1) < HD


def row_of(vec_ref):
    return vec_ref[...].reshape(1, -1)


def attn_fwd_body(last, ids, bucket, lens, x_ref, w_ref, b_ref, *rest):
    if last:
        (other_o, wo_own, wo_other, bias_out, gain, shift_vec) = rest[:6]
        qa_ref, k_ref, v_ref, o_ref, n_ref, rstd_ref, hb_ref = rest[6:13]
        am_s, bm_s = rest[13:]
    else:
        qa_ref, k_ref, v_ref, o_ref, am_s, bm_s, x_s, w_s, b_s, sems = rest
    pairs, rows, _ = k_ref.shape
    if not last:
        copies = [pltpu.make_async_copy(x_ref.at[chunk_of(ids[0], rows), :], x_s, sems.at[0])]
        copies.append(pltpu.make_async_copy(b_ref, b_s, sems.at[1]))
        for p in range(pairs):
            cols = slice(p * LANES, (p + 1) * LANES)
            copies.append(pltpu.make_async_copy(w_ref.at[:, :, cols], w_s.at[p], sems.at[2 + p]))
        for copy in copies:
            copy.start()
        b_ref = b_s
    am_s[...], bm_s[...] = mask_columns(ids, bucket, lens, rows)
    tile = rows // 2
    if not last:
        copies[0].wait()
        copies[1].wait()

    def pair(p, carry):
        cols = chunk_of(p, LANES)
        if last:
            weights = jnp.concatenate([w_ref[n, :, cols] for n in range(3)], axis=1)
            qkv = dot_nn(x_ref[chunk_of(ids[0], rows), :], weights)
        else:
            pltpu.make_async_copy(w_ref.at[:, :, slice(0, LANES)], w_s.at[p], sems.at[2 + p]).wait()
            qkv = dot_nn(x_s[...], jnp.concatenate([w_s[p, n] for n in range(3)], axis=1))
        qp = ((qkv[:, :LANES] + b_ref[0:1, cols]).astype(BF16).astype(F32) * 0.125).astype(BF16)
        kp = qkv[:, LANES : 2 * LANES].astype(BF16)
        vp = (qkv[:, 2 * LANES :] + b_ref[1:2, cols]).astype(BF16)
        k_ref[p] = kp
        v_ref[p] = vp
        bm = bm_s[...]
        low_r, low_t = low_half(rows), low_half(tile)
        lane = lax.broadcasted_iota(jnp.int32, (tile, LANES), 1) & (HD - 1)
        for rb in range(2):
            r = slice(rb * tile, (rb + 1) * tile)
            am = am_s[r, :]
            qpr = qp[r, :]
            sums = []
            for par in range(2):
                own_t = low_t if par == 0 else jnp.logical_not(low_t)
                own_r = low_r if par == 0 else jnp.logical_not(low_r)
                scores = dot_nt(jnp.where(own_t, qpr, am), jnp.where(own_r, kp, bm))
                top = jnp.max(scores, axis=1, keepdims=True)
                expo = jnp.exp(scores - top).astype(BF16)
                total = dot_nn(expo, jnp.where(own_r, vp, jnp.ones_like(vp)))
                sums.append(total)
                neg_log = -(top + jnp.log(jnp.where(own_t, 1.0, total)))
                hi = neg_log.astype(BF16)
                mid = (neg_log - hi.astype(F32)).astype(BF16)
                lo = (neg_log - hi.astype(F32) - mid.astype(F32)).astype(BF16)
                parts = jnp.where(lane == 4, hi, jnp.where(lane == 5, mid, jnp.where(lane == 6, lo, am)))
                qa_ref[2 * p + par, r, :] = jnp.where(own_t, qpr, parts)
            total = pltpu.roll(jnp.where(low_t, sums[1], sums[0]), HD, 1)
            o_ref[p, r, :] = (jnp.where(low_t, sums[0], sums[1]) / total).astype(BF16)
        return carry

    lax.fori_loop(0, pairs, pair, 0)
    if last:
        block = rows // 4
        gain_row, shift_row, bias_row = row_of(gain), row_of(shift_vec), row_of(bias_out)

        def norm(i, carry):
            r = chunk_of(i, block)
            heads = [o_ref[n, r, :] for n in range(pairs)] + [other_o[n, r, :] for n in range(pairs)]
            weights = jnp.concatenate([wo_own[...], wo_other[...]], axis=0)
            acc = dot_nn(jnp.concatenate(heads, axis=1), weights)
            acc += x_ref[pl.ds(pl.multiple_of(ids[0] * rows + i * block, block), block), :].astype(F32) + bias_row
            centre = acc - jnp.mean(acc, axis=1, keepdims=True)
            rstd = lax.rsqrt(jnp.mean(centre * centre, axis=1, keepdims=True) + EPS)
            normed = centre * rstd
            n_ref[r, :] = normed
            rstd_ref[r, :] = jnp.broadcast_to(rstd, (block, LANES))
            hb_ref[r, :] = (normed * gain_row + shift_row).astype(BF16)
            return carry

        lax.fori_loop(0, 4, norm, 0, unroll=True)


def attn_fwd(last, scal, tokens, w, b, rows, extra=()):
    width = tokens.shape[1]
    local = w.shape[2]
    pairs = local // LANES
    outs = [shaped((2 * pairs, rows, LANES), BF16)] + [shaped((pairs, rows, LANES), BF16)] * 3
    if last:
        outs += [shaped((rows, width), F32), shaped((rows, LANES), F32), shaped((rows, width), BF16)]
    scratch = [pltpu.VMEM((rows, LANES), BF16)] * 2
    specs = None
    if not last:
        scratch += [pltpu.VMEM((rows, width), BF16), pltpu.VMEM((pairs, 3, width, LANES), BF16)]
        scratch += [pltpu.VMEM(b.shape, F32), pltpu.SemaphoreType.DMA((2 + pairs,))]
        specs = [anywhere()] * 3
        tokens, w, b = (pltpu.with_memory_space_constraint(each, pltpu.HBM) for each in (tokens, w, b))
    return call(
        functools.partial(attn_fwd_body, last),
        outs,
        scal,
        (tokens, w, b, *extra),
        scratch,
        in_specs=specs,
        flops=2 * rows * local * (3 * width + 4 * rows + (2 * width if last else 0)),
        moved=2 * (rows * width + 3 * width * local + 5 * rows * local),
        trans=2 * pairs * rows * rows,
    )


def keep_of(ids, bucket, keep, block):
    shift = bucket_shift(bucket)
    first = ids[0] * lax.shift_right_logical(BUCKET_LONG, shift)
    return keep[0, first + lax.shift_right_logical(block * LANES, shift)] > 0


def fold_rows(array_in):
    rows, cols = array_in.shape
    return jnp.sum(array_in.reshape(rows // 8, 8, cols), axis=0)


def ffn_fwd_body(
    ids, bucket, keep, hb_ref, n_ref, up_own, up_other, bu_own, bu_other, down_own, down_other,
    gain_a, shift_a, bias_down, gain_f, shift_f, x_ref, g_ref,
    gb_own, gb_other, gp_own, gp_other, mixed_ref, dr2_ref, df_ref, vec_ref, acc, fold_s,
):
    rows, width = hb_ref.shape
    acc[...] = n_ref[...] * row_of(gain_a) + (row_of(shift_a) + row_of(bias_down))
    half = rows // 2
    chunk = 256

    def hidden(i, carry):
        cols = chunk_of(i, chunk)
        for r in range(2):
            rs = slice(r * half, (r + 1) * half)
            hb = hb_ref[rs, :]
            total = None
            for up, bu, down, gb, gp in (
                (up_own, bu_own, down_own, gb_own, gp_own),
                (up_other, bu_other, down_other, gb_other, gp_other),
            ):
                u = dot_nn(hb, up[:, cols]) + bu[cols].reshape(1, -1)
                cdf = 0.5 * (1.0 + lax.erf(u * 0.7071067811865476))
                pdf = jnp.exp(-0.5 * u * u) * 0.3989422804014327
                gp[rs, cols] = cdf + u * pdf
                act = (u * cdf).astype(BF16)
                gb[rs, cols] = act
                part = dot_nn(act, down[cols, :])
                total = part if total is None else total + part
            acc[rs, :] += total
        return carry

    lax.fori_loop(0, up_own.shape[1] // chunk, hidden, 0, unroll=2)
    fold_s[...] = jnp.zeros_like(fold_s)
    gain_row, shift_row = row_of(gain_f), row_of(shift_f)

    def norm(blk, carry):
        r = chunk_of(blk, LANES)
        far = pl.ds(pl.multiple_of(ids[0] * rows + blk * LANES, LANES), LANES)
        kept = keep_of(ids, bucket, keep, blk)
        res = acc[r, :]
        centre = res - jnp.mean(res, axis=1, keepdims=True)
        rstd = lax.rsqrt(jnp.mean(centre * centre, axis=1, keepdims=True) + EPS)
        normed = centre * rstd
        final = normed * gain_row + shift_row
        mixed_ref[r, :] = jnp.where(kept, final, x_ref[far, :].astype(F32)).astype(BF16)
        grad = jnp.where(kept, g_ref[far, :].astype(F32), 0.0)
        fold_s[0] += fold_rows(grad * normed)
        fold_s[1] += fold_rows(grad)
        scaled = grad * gain_row
        mean_a = jnp.mean(scaled, axis=1, keepdims=True)
        mean_b = jnp.mean(scaled * normed, axis=1, keepdims=True)
        dr2 = (scaled - mean_a - normed * mean_b) * rstd
        dr2_ref[r, :] = dr2
        df = dr2.astype(BF16)
        df_ref[r, :] = df
        fold_s[2] += fold_rows(df.astype(F32))
        return carry

    lax.fori_loop(0, rows // LANES, norm, 0, unroll=True)
    vec_ref[...] = jnp.sum(fold_s[...], axis=1)


def ffn_fwd(scal, hb, n1, up_own, up_other, bu_own, bu_other, down_own, down_other, vecs, tokens, out_grad):
    rows, width = hb.shape
    hidden = up_own.shape[1]
    outs = [
        shaped((rows, hidden), BF16), shaped((rows, hidden), BF16),
        shaped((rows, hidden), F32), shaped((rows, hidden), F32),
        shaped((rows, width), BF16), shaped((rows, width), F32), shaped((rows, width), BF16),
        shaped((3, width), F32),
    ]
    return call(
        ffn_fwd_body,
        outs,
        scal,
        (hb, n1, up_own, up_other, bu_own, bu_other, down_own, down_other, *vecs, tokens, out_grad),
        [pltpu.VMEM((rows, width), F32), pltpu.VMEM((3, 8, width), F32)],
        flops=8 * rows * width * hidden,
        moved=12 * rows * hidden + 8 * width * hidden + 20 * rows * width,
        trans=4 * rows * hidden,
    )


def down_grad_body(kind, ids, gb_ref, df_ref, out_ref):
    _, count, size, _ = out_ref.shape
    per = 2 if count % 2 == 0 else 1

    def step(i, carry):
        value = dot_tn(gb_ref[:, chunk_of(i, per * PARTS * size)], df_ref[...]).astype(BF16)
        for c in range(per):
            for part in range(PARTS):
                first = (c * PARTS + part) * size
                out_ref[part, spot_of(ids, part, kind, i * per + c, count)] = value[first : first + size, :]
        return carry

    lax.fori_loop(0, count // per, step, 0, unroll=2)


def down_grad(kind, ids, gb, df, count):
    rows, width = df.shape
    hidden = gb.shape[1]
    return call(
        functools.partial(down_grad_body, kind),
        [shaped((PARTS, count, hidden // (count * PARTS), width), BF16)],
        (ids,),
        (gb, df),
        flops=2 * rows * width * hidden,
        moved=2 * rows * hidden + 2 * width * hidden + 2 * rows * width,
    )[0]


def ffn_bwd_body(kind, ids, df_ref, hb_ref, gp_ref, down_ref, up_ref, *rest):
    if kind == 1:
        dr2_ref, out_ref, bu_ref, acc = rest
        acc[...] = dr2_ref[...]
    else:
        acc_in, n_ref, rstd_ref, gain_a, out_ref, bu_ref, dr1_ref, da_ref, vec_ref, acc, fold_s = rest
        acc[...] = acc_in[...]
    rows, width = df_ref.shape
    _, count, _, _ = out_ref.shape
    hidden = up_ref.shape[1]
    up_rows = width // count
    chunk = 384
    per_line = width // chunk

    def step(i, carry):
        cols = chunk_of(i, chunk)
        du = (dot_nt(df_ref[...], down_ref[cols, :]) * gp_ref[:, cols]).astype(BF16)
        bu_ref[:, cols] = jnp.sum(fold_rows(du.astype(F32)), axis=0, keepdims=True)
        value = dot_tn(hb_ref[...], du).astype(BF16)
        part, col = i // per_line, chunk_of(i % per_line, chunk)
        for a in range(count):
            spots = [spot_of(ids, 2 + n, kind, a, count) for n in range(PARTS)]
            spot = jnp.where(part == 0, spots[0], spots[1])
            out_ref[part, spot, :, col] = value[a * up_rows : (a + 1) * up_rows, :]
        acc[...] += dot_nt(du, up_ref[:, cols])
        return carry

    lax.fori_loop(0, hidden // chunk, step, 0, unroll=4 if kind == 0 else 2)
    if kind == 0:
        fold_s[...] = jnp.zeros_like(fold_s)
        gain_row = row_of(gain_a)

        def norm(blk, carry):
            r = chunk_of(blk, LANES)
            grad = acc[r, :]
            normed = n_ref[r, :]
            fold_s[0] += fold_rows(grad * normed)
            fold_s[1] += fold_rows(grad)
            scaled = grad * gain_row
            mean_a = jnp.mean(scaled, axis=1, keepdims=True)
            mean_b = jnp.mean(scaled * normed, axis=1, keepdims=True)
            dr1 = (scaled - mean_a - normed * mean_b) * rstd_ref[r, 0:1]
            dr1_ref[r, :] = dr1
            da = dr1.astype(BF16)
            da_ref[r, :] = da
            fold_s[2] += fold_rows(da.astype(F32))
            return carry

        lax.fori_loop(0, rows // LANES, norm, 0, unroll=True)
        vec_ref[...] = jnp.sum(fold_s[...], axis=1)


def ffn_bwd(kind, ids, df, hb, gp, down, up, extra, count):
    rows, width = df.shape
    hidden = up.shape[1]
    outs = [shaped((hidden // width, count, width // count, width), BF16), shaped((1, hidden), F32)]
    scratch = []
    if kind == 1:
        outs += [shaped((rows, width), F32)]
    else:
        outs += [shaped((rows, width), F32), shaped((rows, width), BF16), shaped((3, width), F32)]
        scratch = [pltpu.VMEM((rows, width), F32), pltpu.VMEM((3, 8, width), F32)]
    return call(
        functools.partial(ffn_bwd_body, kind),
        outs,
        (ids,),
        (df, hb, gp, down, up, *extra),
        scratch,
        flops=6 * rows * width * hidden,
        moved=4 * rows * hidden + 6 * width * hidden + 10 * rows * width,
    )


def attn_bwd_body(
    kind, ids, bucket, lens, keep, qa_ref, k_ref, v_ref, o_ref, da_ref, wo_ref, w_ref, x_ref, bu_ref, va_ref, vf_ref, *rest
):
    if kind == 1:
        dr1_ref, g_ref, dw_ref, ig_ref, bm_s = rest
    else:
        ig_in, dw_ref, ig_ref, bm_s = rest
    rows, width = da_ref.shape
    pairs = k_ref.shape[0]
    local = pairs * LANES
    count = dw_ref.shape[1]
    size, out_size, wide = width // count, local // count, width // local
    _, bm_s[...] = mask_columns(ids, bucket, lens, rows)
    if kind == 1:
        for blk in range(rows // LANES):
            r = slice(blk * LANES, (blk + 1) * LANES)
            far = pl.ds(pl.multiple_of(ids[0] * rows + blk * LANES, LANES), LANES)
            kept = keep_of(ids, bucket, keep, blk)
            ig_ref[r, :] = dr1_ref[r, :] + jnp.where(kept, 0.0, g_ref[far, :].astype(F32))
    else:
        ig_ref[...] = ig_in[...]
    tile = rows // 2

    def pair(p, carry):
        cols = chunk_of(p, LANES)
        kp = k_ref[p]
        vp = v_ref[p]
        bm = bm_s[...]
        low_t, low_r = low_half(tile), low_half(rows)
        zero_t, zero_r = jnp.zeros((tile, LANES), BF16), jnp.zeros((rows, LANES), BF16)
        wo = wo_ref[cols, :]
        dk_sum = dv_sum = None
        dqs = []
        for rb in range(2):
            r = slice(rb * tile, (rb + 1) * tile)
            dop = dot_nt(da_ref[r, :], wo).astype(BF16)
            dq = None
            for par in range(2):
                own_t = low_t if par == 0 else jnp.logical_not(low_t)
                own_r = low_r if par == 0 else jnp.logical_not(low_r)
                qa = qa_ref[2 * p + par, r, :]
                doa = jnp.where(own_t, dop, zero_t)
                prob = jnp.exp(dot_nt(jnp.where(own_r, kp, bm), qa))
                dprob = dot_nt(vp, doa)
                inner = jnp.sum(prob * dprob, axis=0, keepdims=True)
                dscore = (prob * (dprob - inner)).astype(BF16)
                dv = dot_nn(prob.astype(BF16), doa)
                dk = dot_nn(dscore, jnp.where(own_t, qa, zero_t))
                dqp = dot_tn(dscore, jnp.where(own_r, kp, zero_r))
                dv_sum = dv if dv_sum is None else dv_sum + dv
                dk_sum = dk if dk_sum is None else dk_sum + dk
                dq = dqp if dq is None else dq + dqp
            dqs.append((dq * 0.125).astype(BF16))
        dqp = jnp.concatenate(dqs, axis=0)
        dvp = dv_sum.astype(BF16)
        grads = jnp.concatenate([dqp, dk_sum.astype(BF16), dvp], axis=1)
        weights = jnp.concatenate([w_ref[n, :, cols] for n in range(3)], axis=1)
        ig_ref[...] += dot_nt(grads, weights)
        value = dot_tn(x_ref[chunk_of(ids[0], rows), :], grads).astype(BF16)
        heads = jnp.concatenate([o_ref[n] for n in range(pairs)], axis=1)
        da = [da_ref[:, pl.ds(pl.multiple_of(n * local + p * LANES, LANES), LANES)] for n in range(wide)]
        out_value = dot_tn(heads, jnp.concatenate(da, axis=1)).astype(BF16)
        small = [jnp.sum(fold_rows(g.astype(F32)), axis=0, keepdims=True) for g in (dqp, dvp)]
        for ref in (bu_ref, va_ref, vf_ref):
            for n in range(ref.shape[0]):
                for c in range(0, ref.shape[1], local):
                    small.append(ref[n : n + 1, pl.ds(pl.multiple_of(c + p * LANES, LANES), LANES)])
        line = lax.broadcasted_iota(jnp.int32, (8, LANES), 0)
        for a in range(count):
            spots = [spot_of(ids, 4 + n, kind, a, count) for n in range(PARTS)]
            rows_a = slice(a * size, (a + 1) * size)
            dw_ref[0, spots[0], 0:size, cols] = value[rows_a, 0:LANES]
            dw_ref[0, spots[0], size : 2 * size, cols] = value[rows_a, LANES : 2 * LANES]
            dw_ref[1, spots[1], 0:size, cols] = value[rows_a, 2 * LANES :]
            for n in range(wide):
                part = out_value[a * out_size : (a + 1) * out_size, n * LANES : (n + 1) * LANES]
                at = size + n * out_size
                dw_ref[1, spots[1], at : at + out_size, cols] = part
            tile_s = jnp.zeros((8, LANES), F32)
            dw_ref[0, spots[0], 2 * size : 2 * size + 8, cols] = tile_s.astype(BF16)
            for n, row in enumerate(small[a::count]):
                tile_s = jnp.where(line == n, row, tile_s)
            dw_ref[1, spots[1], 2 * size : 2 * size + 8, cols] = tile_s.astype(BF16)
        return carry

    lax.fori_loop(0, pairs, pair, 0)


def attn_bwd(kind, scal, qa, k, v, o, da, wo, w, tokens, smalls, extra, count):
    rows, width = da.shape
    pairs = k.shape[0]
    local = pairs * LANES
    lines = 2 * width // count + 8
    return call(
        functools.partial(attn_bwd_body, kind),
        [shaped((PARTS, count, lines, local), BF16), shaped((rows, width), F32)],
        scal,
        (qa, k, v, o, da, wo, w, tokens, *smalls, *extra),
        [pltpu.VMEM((rows, LANES), BF16)],
        flops=2 * rows * local * (8 * width + 10 * rows),
        moved=2 * (rows * local * 4 + width * local * 7 + rows * width * 2) + 8 * rows * width,
        trans=2 * pairs * rows * rows,
    )


def place_body(part, first, count, plan, n_held, small_plan, ids, *refs):
    pieces = refs[: 1 if small_plan is None else 2]
    refs = refs[len(pieces) + n_held :]
    outs, refs = refs[: len(plan)], refs[len(plan) :]
    n_small = 0 if small_plan is None else len(small_plan)
    small_outs, refs = refs[:n_small], refs[n_small:]
    stages, sems = refs[:-1], refs[-1]
    half, lines, _ = pieces[0].shape
    copies = []
    for q in range(half):
        a = spot_of(ids, part, 2, first + q, count)
        for n, (parts, target) in enumerate(plan):
            for at, start, size in parts:
                stages[n][(q,) + at] = pieces[0][q, start : start + size, :].astype(F32)
            copy = pltpu.make_async_copy(stages[n].at[q], target(outs[n], a), sems.at[n, q])
            copy.start()
            copies.append(copy)
    for n in range(n_small):
        for line, c0, row in small_plan[n]:
            p = spot_of(ids, part, 3, row % count, count)
            high = pieces[0][p & (half - 1), lines - 8 :, :].astype(F32)
            low = pieces[1][p & (half - 1), lines - 8 :, :].astype(F32)
            tile = jnp.where(p < half, low, high)
            width = tile.shape[1]
            value = tile[row // count : row // count + 1, :]
            if line is None:
                small_outs[n][c0 : c0 + width] = value.reshape(width)
            else:
                small_outs[n][line : line + 1, c0 : c0 + width] = value
    for copy in copies:
        copy.wait()


def place(part, first, ids, pieces, plan, held=(), small_outs=(), small_plan=None):
    half = pieces[0].shape[0]
    outs = [shaped(entry[0], F32) for entry in plan]
    return call(
        functools.partial(place_body, part, first, 2 * half, [entry[2:] for entry in plan], len(held), small_plan),
        outs + list(small_outs),
        (ids,),
        (*pieces, *held),
        [pltpu.VMEM((half,) + entry[1], F32) for entry in plan] + [pltpu.SemaphoreType.DMA((len(outs), half))],
        moved=6 * half * pieces[0].shape[1] * pieces[0].shape[2],
        in_specs=[resident()] * len(pieces) + [anywhere()] * len(held),
        out_specs=[anywhere()] * len(outs) + [resident()] * len(small_outs),
        input_output_aliases={1 + len(pieces) + n: n for n in range(len(held))},
    )


def join_body(cores, ids, *refs):
    n = (len(refs) - 1) // 3
    owns, others, outs, sems = refs[:n], refs[n : 2 * n], refs[2 * n : 3 * n], refs[-1]
    copies = []
    for k in range(n):
        rows = owns[k].shape[0]
        for part, where in ((owns[k], ids[0]), (others[k], cores - 1 - ids[0])):
            target = outs[k].at[pl.ds(pl.multiple_of(where * rows, rows), rows), :]
            copies.append(pltpu.make_async_copy(part, target, sems.at[len(copies)]))
            copies[-1].start()
    for copy in copies:
        copy.wait()


def join(ids, cores, owns, others):
    return call(
        functools.partial(join_body, cores),
        [shaped((cores * o.shape[0], o.shape[1]), o.dtype) for o in owns],
        (ids,),
        (*owns, *others),
        [pltpu.SemaphoreType.DMA((2 * len(owns),))],
        moved=sum(4 * o.size * o.dtype.itemsize for o in owns),
        out_specs=[anywhere()] * len(owns),
    )


def swap_cores(array_in, cores):
    return lax.ppermute(array_in, "tensor", [(c, cores - 1 - c) for c in range(cores)])


class GroupSum:
    def __init__(self, mesh, batch, own, other_received):
        self.mesh, self.batch = mesh, batch
        self.halvings = own.shape[0].bit_length() - 1
        self.steps = 2 * self.halvings + 1
        self.terms = [own, other_received]
        self.at = 0
        self.sent = None

    def exchange(self, array_in, bit_of):
        groups, cores = self.mesh.shape["dp"], self.mesh.shape["tensor"]
        pairs = [(i * cores + c, (i ^ (1 << bit_of(c))) * cores + c) for i in range(groups) for c in range(cores)]
        return lax.ppermute(array_in, ("dp", "tensor"), pairs)

    def total(self, terms):
        acc = terms[0].astype(F32)
        for term in terms[1:]:
            acc = acc + term.astype(F32)
        return acc.astype(BF16)

    def step(self, *earlier):
        terms = self.terms
        if earlier:
            terms = terms[:-1] + [after(terms[-1], *earlier)]
        n = self.at
        if n < self.halvings:
            half = terms[0].shape[0] // 2
            self.sent = self.total([term[half:] for term in terms])
            received = self.exchange(self.sent, lambda c: step_bits(self.batch, c, 0, self.halvings)[n])
            self.terms = [term[:half] for term in terms] + [received]
        elif n == self.halvings:
            doublings = (self.mesh.shape["dp"] >> self.halvings).bit_length() - 1
            for k in range(doublings):
                self.sent = self.total(terms)
                terms = [self.sent, self.exchange(self.sent, lambda c, k=k: self.halvings + k)]
            self.terms = terms
        else:
            n -= self.halvings + 1
            self.sent = self.total(terms) if n == 0 else jnp.concatenate(terms, axis=0)
            received = self.exchange(self.sent, lambda c: step_bits(self.batch, c, 1, self.halvings)[n])
            self.terms = [self.sent, received]
        self.at += 1
        return self.sent


def per_device(
    mesh,
    tokens,
    w_qkv,
    bias_qv,
    w_out,
    bias_out,
    gain_attn,
    shift_attn,
    w_up,
    bias_up,
    w_down,
    bias_down,
    gain_ffn,
    shift_ffn,
    out_grad,
    bucket_len,
    seq_lengths,
    keep_mask,
):
    cores = mesh.shape["tensor"]
    count = min(8, mesh.shape["dp"])
    width = tokens.shape[1]
    rows = tokens.shape[0] // cores
    hidden = w_up.shape[1]
    local = w_qkv.shape[2]
    ids = jnp.where(jnp.arange(2) == 0, lax.axis_index("tensor"), lax.axis_index("dp")).astype(jnp.int32)

    w_qkv_o = swap_cores(w_qkv, cores)
    bias_qv_o = swap_cores(bias_qv, cores)
    w_out_o = swap_cores(w_out, cores)
    bias_up_o = swap_cores(bias_up, cores)
    w_up_o = swap_cores(w_up, cores)
    w_down_o = swap_cores(w_down, cores)

    attn_scal = (ids, bucket_len, seq_lengths)
    qa, k, v, o = attn_fwd(False, attn_scal, tokens, w_qkv, bias_qv, rows)
    qa_o, k_o, v_o, o_o, n1, rstd, hb = attn_fwd(
        True,
        attn_scal,
        tokens,
        w_qkv_o,
        bias_qv_o,
        rows,
        (o, w_out_o, w_out, bias_out, gain_attn, shift_attn),
    )
    keep_scal = (ids, bucket_len, keep_mask)
    vecs = (gain_attn, shift_attn, bias_down, gain_ffn, shift_ffn)
    gb, gb_o, gp, gp_o, mixed, dr2, df, vec_f = ffn_fwd(
        keep_scal, hb, n1, w_up, w_up_o, bias_up, bias_up_o, w_down, w_down_o, vecs, tokens, out_grad
    )
    mixed_o = swap_cores(mixed, cores)
    down_other = down_grad(1, ids, gb_o, df, count)
    down_got = swap_cores(down_other, cores)
    down_own = down_grad(0, ids, gb, after(df, down_other), count)
    sums = []

    def add_sums(own, received):
        for part in range(PARTS):
            sums.append(GroupSum(mesh, len(sums), own[part], received[part]))

    add_sums(down_own, down_got)
    landed, sents, final = [[], []], [[], []], [[], []]

    def exchange(parts, *earlier):
        which = parts[0] % 2
        earlier += tuple(landed[which]) + tuple(sents[1 - which])
        sents[which] = [sums[part].step(*earlier) for part in parts]
        landed[which] = final[which] + [sums[part].terms[-1] for part in parts if sums[part].at < sums[part].steps]
        final[which] = [sums[part].terms[-1] for part in parts if sums[part].at == sums[part].steps]

    def exchange_all(stage, *earlier):
        for parts in EARLY[stage]:
            exchange(parts, *earlier)
        return sents[0] + sents[1]

    sent = exchange_all(0, df)
    up_other, bu_o, dh = ffn_bwd(1, ids, after(df, *sent), hb, gp_o, w_down_o, w_up_o, (dr2,), count)
    up_got = swap_cores(up_other, cores)
    sent = exchange_all(1, dh)
    up_own, bu, dr1, da, vec_a = ffn_bwd(
        0, ids, after(df, *sent), hb, gp, w_down, w_up, (dh, n1, rstd, gain_attn), count
    )
    add_sums(up_own, up_got)
    sent = exchange_all(2, da)
    bwd_scal = (ids, bucket_len, seq_lengths, keep_mask)
    qkv_other, ig_part = attn_bwd(
        1, bwd_scal, qa_o, k_o, v_o, o_o, after(da, *sent), w_out_o, w_qkv_o, tokens,
        (bu_o, vec_a, vec_f), (dr1, out_grad), count,
    )
    qkv_got = swap_cores(qkv_other, cores)
    sent = exchange_all(3, ig_part, mixed_o)
    qkv_own, ig = attn_bwd(
        0, bwd_scal, qa, k, v, o, after(da, *sent), w_out, w_qkv, tokens, (bu, vec_a, vec_f), (ig_part,), count
    )
    ig_o = swap_cores(ig, cores)
    add_sums(qkv_own, qkv_got)

    def rows_at(each, size, shift=0, cols=slice(None)):
        def target(out, a):
            start = pl.multiple_of(a * each, each)
            return out.at[pl.ds(start + shift, size), cols]

        return target

    every = (slice(None), slice(None))
    size, out_size, wide = width // count, local // count, width // local
    half_rows = hidden // (count * PARTS)
    plans = []
    for part in range(PARTS):
        target = rows_at(PARTS * half_rows, half_rows, part * half_rows)
        plans.append([((hidden, width), (half_rows, width), [(every, 0, half_rows)], target)])
    for part in range(hidden // width):
        target = rows_at(size, size, 0, slice(part * width, (part + 1) * width))
        plans.append([((width, hidden), (size, width), [(every, 0, size)], target)])

    def planes_at(first, planes):
        return lambda out, a: out.at[first : first + planes, pl.ds(pl.multiple_of(a * size, size), size), :]

    shape = (3, width, local)
    plans.append([(shape, (2, size, local), [((n,) + every, n * size, size) for n in range(2)], planes_at(0, 2))])
    pieces = [((slice(None), slice(n * local, (n + 1) * local)), size + n * out_size, out_size) for n in range(wide)]
    plans.append(
        [
            (shape, (1, size, local), [((0,) + every, 0, size)], planes_at(2, 1)),
            ((local, width), (out_size, width), pieces, rows_at(out_size, out_size)),
        ]
    )
    per_up, per_norm = hidden // local, width // local
    small_plan = [[(n, 0, n) for n in range(2)], [(None, c * local, 2 + c) for c in range(per_up)]]
    for n in range(6):
        small_plan.append([(None, c * local, 2 + per_up + n * per_norm + c) for c in range(per_norm)])
    small_outs = [shaped((2, local), F32), shaped((hidden,), F32)] + [shaped((width,), F32)] * 6
    held = {0: [], 1: [], 2: []}
    small = []

    def put(part, late, *earlier):
        each = sums[part]
        pieces = [after(each.terms[1] if late else each.terms[0], *earlier)] if earlier else [each.terms[1 if late else 0]]
        first = count // 2 if late else 0
        batch = part // PARTS
        extra = held[batch][: len(plans[part])]
        if late and part == len(plans) - 1:
            placed = place(part, first, ids, pieces + [each.terms[0]], plans[part], extra, small_outs, small_plan)
            small.extend(placed[len(plans[part]) :])
            placed = placed[: len(plans[part])]
        else:
            placed = place(part, first, ids, pieces, plans[part], extra)
        held[batch] = list(placed) + held[batch][len(placed) :]
        return placed[0]

    put_early, put_late = set(), set()
    fillers = [ig]
    for turn, parts in enumerate(TURNS):
        active = [part for part in parts if sums[part].at < sums[part].steps]
        earlier, later = fillers, []
        if turn == JOIN_AT:
            out_mixed, out_ig = join(ids, cores, (mixed, after(ig, *sents[0])), (mixed_o, ig_o))
            later.append(out_ig)
        for part in parts:
            if sums[part].at == sums[part].steps and part not in put_late and part < 4:
                later.append(put(part, True, *landed[part % 2]))
                put_late.add(part)
        if active:
            exchange(active, *earlier)
        for part in parts:
            if sums[part].at == sums[part].steps and part not in put_early:
                put(part, False)
                put_early.add(part)
        fillers = later
    for part in range(len(plans)):
        if part not in put_late:
            put(part, True)
    grad_w_down, grad_w_up = held[0][0], held[1][0]
    grad_w_qkv, grad_w_out = held[2]
    grad_bias_qv, grad_bias_up, *norms = small
    return (
        out_mixed,
        out_ig,
        grad_w_qkv,
        grad_bias_qv,
        grad_w_out,
        norms[2],
        norms[0],
        norms[1],
        grad_w_up,
        grad_bias_up,
        grad_w_down,
        norms[5],
        norms[3],
        norms[4],
    )


def solution(mesh):
    in_specs = (
        P("dp", None),
        P(None, None, "tensor"),
        P(None, "tensor"),
        P("tensor", None),
        P(),
        P(),
        P(),
        P(None, "tensor"),
        P("tensor"),
        P("tensor", None),
        P(),
        P(),
        P(),
        P("dp", None),
        P("dp"),
        P("dp", None),
        P("dp", None),
    )
    out_specs = (
        P("dp", None),
        P("dp", None),
        P(None, None, "tensor"),
        P(None, "tensor"),
        P("tensor", None),
        P(),
        P(),
        P(),
        P(None, "tensor"),
        P("tensor"),
        P("tensor", None),
        P(),
        P(),
        P(),
    )
    return jax.shard_map(
        functools.partial(per_device, mesh),
        mesh=mesh,
        in_specs=in_specs,
        out_specs=out_specs,
        check_vma=False,
    )
```
